128 devices in a mesh: rows: 32 (over x, y, core), grp: 4 (over z).
Axes of the slice: x: 4, y: 4, z: 4, core: 2. Of those that a mesh axis runs over, the one named last changes fastest.
Arguments:
- embeddings: bfloat16 [262144, 1024], P('rows', 'grp'), may hold values from -6 to 6
- fine_local: int32 [262144], P('rows'), may hold values from 0 to 2047
- send_counts: int32 [32, 32], P('rows'), may hold values from 0 to 512, as said below
- old_fine: bfloat16 [65536, 1024], P('rows', 'grp'), may hold values from -6 to 6
- coarse_ids: int32 [65536], P('rows'), may hold values from 0 to 8191, as said below
- old_coarse: bfloat16 [8192, 1024], P('rows', 'grp'), may hold values from -6 to 6
Outputs:
- new_fine: bfloat16 [65536, 1024], P('rows', 'grp')
- coarse_dirs: bfloat16 [8192, 1024], P('rows')
The draws below stay inside these ranges and needn't reach their ends.
Inputs may be any that keep to these rules, and one draw needn't show every extreme that they name: Row d of send_counts splits the 8192 rows of block d, in order, into segments for owners 0, 1, ...; each row of send_counts sums to 8192; one owner receives exactly 512 rows from every block. `coarse_ids`: within each block of 2048 consecutive level-1 clusters, at most 128 have a level-2 cluster in any one block of 256 consecutive level-2 clusters; one such block reaches that from every block.
All inputs are finite; a program needn't handle non-finite values.
Results may differ from the reference program's by a relative error of at most 0.006.
Values may be sent and summed in bfloat16 or wider, within the bound.
No kernel may reach another device: no remote copies, remote signals or barrier semaphores. Data moves between devices by JAX's collectives and lax.ppermute only.
A program may use at most 64 MiB of HBM per device.

```python
import jax
import jax.numpy as jnp
from jax import lax

D = 1024
R_DEV = 8192
K1_DEV = 2048
K2_DEV = 256
K1 = 65536
K2 = 8192
NROWS = 262144
N_ROWS = 32


def owner_loads(key, devices, total):
    mean_load = total // devices
    order = jax.random.permutation(jax.random.fold_in(key, 1), devices)
    half = devices // 2
    heavy = order[:half]
    light = order[half:]
    shift = jax.random.randint(jax.random.fold_in(key, 2), (devices, half), mean_load // 2, mean_load + 1)
    shift = shift.at[:, 0].set(mean_load)
    loads = jnp.full((devices, devices), mean_load, jnp.int32)
    loads = loads.at[:, heavy].add(shift).at[:, light].add(-shift)
    return loads.astype(jnp.int32)


def draw_send_counts(key, part):
    return owner_loads(jax.random.fold_in(key, 3), N_ROWS, R_DEV)


def draw_coarse_ids(key, part):
    loads = owner_loads(jax.random.fold_in(key, 7), N_ROWS, K1_DEV)
    ends = jnp.cumsum(loads, axis=1)
    position = jnp.arange(K1_DEV, dtype=jnp.int32)
    owners = jnp.sum((ends[:, None, :] <= position[None, :, None]).astype(jnp.int32), axis=2).astype(jnp.int32)
    shuffle_keys = jax.random.split(jax.random.fold_in(key, 8), N_ROWS)
    owners = jax.vmap(lambda k, o: jax.random.permutation(k, o))(shuffle_keys, owners)
    local_id = jax.random.randint(jax.random.fold_in(key, 9), (N_ROWS, K1_DEV), 0, K2_DEV)
    return (owners * K2_DEV + local_id).reshape(-1).astype(jnp.int32)


def place_ends(drawn, stream_key, least, top_value):
    extent = drawn.shape
    spot = [jax.random.randint(jax.random.fold_in(stream_key, axis), (), 0, extent[axis]) for axis in range(len(extent))]
    drawn = drawn.at[tuple(spot)].set(least)
    longest = extent.index(max(extent))
    spot[longest] = (spot[longest] + 1) % extent[longest]
    return drawn.at[tuple(spot)].set(top_value)


def shard_levels(key, shape, shards, least, top_value):
    def one(axis_at, blocks):
        heights = jax.random.uniform(jax.random.fold_in(jax.random.fold_in(key, 6), axis_at), (blocks,), jnp.float32, least / len(shards), top_value / len(shards))
        return jnp.repeat(jnp.exp(heights), shape[axis_at] // blocks).reshape((-1,) + (1,) * (len(shape) - axis_at - 1))

    factor_of = one(*shards[0])
    for cut in shards[1:]:
        factor_of = factor_of * one(*cut)
    return factor_of


def noise(rng, extent, deviation, reach, shards=(), kind=jnp.bfloat16):
    array = deviation * jax.random.normal(rng, extent, jnp.float32)
    if shards:
        array = array * shard_levels(rng, extent, shards, -0.22, 0.18)
    return jnp.clip(array, -reach, reach).astype(kind)


def setup_inputs(seed: int = 0) -> dict:
    seeds = jax.random.split(jax.random.key(seed), 7)
    embeddings = noise(seeds[0], (NROWS, D), 1.0, 6.0, ((0, 32), (1, 4)))
    fine_local = place_ends(jax.random.randint(seeds[1], (NROWS,), 0, K1_DEV), jax.random.fold_in(seeds[1], 1), 0, K1_DEV - 1).astype(jnp.int32)
    send_counts = draw_send_counts(jax.random.fold_in(seeds[6], 71), 0)
    old_fine = noise(seeds[3], (K1, D), 1.0, 6.0, ((0, 32), (1, 4)))
    coarse_ids = draw_coarse_ids(jax.random.fold_in(seeds[6], 71), 0)
    old_coarse = noise(seeds[5], (K2, D), 1.0, 6.0, ((0, 32), (1, 4)))
    return {"embeddings": embeddings, "fine_local": fine_local, "send_counts": send_counts, "old_fine": old_fine, "coarse_ids": coarse_ids, "old_coarse": old_coarse}


def segment_owner(send_counts, per_block):
    ends = jnp.cumsum(send_counts, axis=1)
    position = jnp.arange(per_block, dtype=jnp.int32)
    below = (ends[:, None, :] <= position[None, :, None]).astype(jnp.int32)
    return lax.optimization_barrier(jnp.sum(below, axis=2)).astype(jnp.int32)

def reference(embeddings, fine_local, send_counts, old_fine, coarse_ids, old_coarse):
    block_count = send_counts.shape[0]
    per_block = fine_local.shape[0] // block_count
    owners = segment_owner(send_counts, per_block).reshape(-1)
    fine_ids = (owners * K1_DEV + fine_local).astype(jnp.int32)
    fine_sums = jax.ops.segment_sum(embeddings.astype(jnp.float32), fine_ids, num_segments=K1)
    fine_counts = jax.ops.segment_sum(jnp.ones(fine_ids.shape, jnp.float32), fine_ids, num_segments=K1)
    new_fine = ((fine_sums + old_fine.astype(jnp.float32)) / (fine_counts + 1.0)[:, None]).astype(jnp.bfloat16)
    coarse_sums = jax.ops.segment_sum(new_fine.astype(jnp.float32), coarse_ids, num_segments=K2)
    coarse_counts = jax.ops.segment_sum(jnp.ones(coarse_ids.shape, jnp.float32), coarse_ids, num_segments=K2)
    coarse_means = (coarse_sums + old_coarse.astype(jnp.float32)) / (coarse_counts + 1.0)[:, None]
    scale = lax.rsqrt(lax.optimization_barrier(jnp.mean(coarse_means * coarse_means, axis=1, keepdims=True)) + 1e-06)
    coarse_dirs = (coarse_means * scale).astype(jnp.bfloat16)
    return (new_fine, coarse_dirs)
```

```python
import functools

import jax
import jax.numpy as jnp
from jax import lax
from jax.experimental import pallas as pl
from jax.experimental.pallas import tpu as pltpu
from jax.sharding import PartitionSpec as P

F32 = jnp.float32
BF16 = jnp.bfloat16
LANES = 128
TAIL = 8
FIRST = 384


def iota(shape, axis):
    return lax.broadcasted_iota(jnp.int32, shape, axis)


def pack_body(lo_row, rows, capacity, counts, emb, local, *rest):
    extra = rest[0] if len(rest) == 4 else None
    out, wide, labels = rest[-3:]
    owner = pl.program_id(0)
    per_dev = emb.shape[0]
    label_rows = local.shape[0]

    @pl.when(owner == 0)
    def _():
        for at in range(0, per_dev, 512):
            wide[at : at + 512, :] = emb[at : at + 512, :].astype(F32)
        wide[per_dev:, :] = jnp.zeros((capacity + 8, emb.shape[1]), F32)
        labels[:label_rows, :] = local[...]
        labels[label_rows:, :] = jnp.zeros((16, LANES), jnp.int32)

    start = lax.fori_loop(0, owner, lambda o, s: s + counts[0, o], 0)
    count = counts[0, owner]
    first = start + lo_row
    aligned = first // 8
    turn = first - aligned * 8
    turn_back = lax.rem(8 - turn, 8)
    kept = iota((8, 8, emb.shape[1]), 1) < 8 - turn
    for at in range(0, rows, 64):
        window = wide[pl.ds(pl.multiple_of(aligned * 8 + at, 8), 72), :]
        window = pltpu.roll(window.reshape(9, 8, emb.shape[1]), turn_back, 1)
        moved = jnp.where(kept, window[:8], window[1:])
        out[0, at : at + 64, :] = moved.reshape(64, emb.shape[1]).astype(BF16)
    base = first // LANES
    shift = first - base * LANES
    lines = [labels[pl.ds(base + i, 1), :] for i in range(TAIL + 1)]
    here = jnp.concatenate(lines[:TAIL], axis=0)
    after = jnp.concatenate(lines[1:], axis=0)
    back = lax.rem(LANES - shift, LANES)
    here = pltpu.roll(here, back, 1)
    after = pltpu.roll(after, back, 1)
    lane = iota((TAIL, LANES), 1)
    value = jnp.where(lane < LANES - shift, here, after)
    place = iota((TAIL, LANES), 0) * LANES + lane + lo_row
    live = place < count
    high = jnp.where(live, value // LANES, 64).astype(F32)
    low = jnp.where(live, value % LANES, 0).astype(F32)
    if extra is not None:
        high = jnp.where(iota((TAIL, LANES), 0) == 1, extra[pl.ds(owner, 1), :], high)
    out[0, rows:, :] = jnp.concatenate([high, low], axis=1).astype(BF16)


def pack(send_counts, embeddings, local, extra, lo_row, rows, capacity):
    per_dev, width = embeddings.shape
    owners = send_counts.shape[1]
    operands = [send_counts, embeddings, local] + ([] if extra is None else [extra])
    specs = [pl.BlockSpec(memory_space=pltpu.SMEM)] + [
        pl.BlockSpec(a.shape, lambda o: (0, 0)) for a in operands[1:]
    ]
    return pl.pallas_call(
        functools.partial(pack_body, lo_row, rows, capacity),
        grid=(owners,),
        out_shape=jax.ShapeDtypeStruct((owners, rows + TAIL, width), BF16),
        in_specs=specs,
        out_specs=pl.BlockSpec((1, rows + TAIL, width), lambda o: (o, 0, 0)),
        scratch_shapes=[
            pltpu.VMEM((per_dev + capacity + 8, width), F32),
            pltpu.VMEM((local.shape[0] + 16, LANES), jnp.int32),
        ],
        name="pack_rows",
    )(*operands)


def accumulate(block, group, rows, digits, acc, counts, onehot):
    tail = block[:, rows:, :].astype(F32)
    high, low = [], []
    for g in range(group):
        for at in range(rows // LANES):
            high.append(tail[g, at : at + 1, :LANES])
            low.append(tail[g, at : at + 1, LANES : 2 * LANES])
    high = jnp.concatenate(high, axis=1)
    low = jnp.concatenate(low, axis=1)
    depth = group * rows
    low_hot = jnp.where(iota((LANES, depth), 0).astype(F32) == low, 1.0, 0.0).astype(BF16)
    high_hot = jnp.where(iota((digits, depth), 0).astype(F32) == high, 1.0, 0.0)
    for h in range(digits):
        row = jnp.broadcast_to(high_hot[h : h + 1, :], (16, depth)).astype(BF16)
        for at in range(0, LANES, 16):
            onehot[h * LANES + at : h * LANES + at + 16, :] = low_hot[at : at + 16, :] * row
    data = jnp.concatenate([block[g, :rows, :] for g in range(group)], axis=0)
    acc[...] += jnp.dot(onehot[...], data, preferred_element_type=F32)
    counts[...] += lax.dot_general(
        low_hot, high_hot.astype(BF16), (((1,), (1,)), ((), ())), preferred_element_type=F32
    )


def first_sums_body(group, rows, digits, block, acc, counts, onehot):
    @pl.when(pl.program_id(0) == 0)
    def _():
        acc[...] = jnp.zeros_like(acc)
        counts[...] = jnp.zeros_like(counts)

    accumulate(block, group, rows, digits, acc, counts, onehot)


def first_sums(arrived, rows, group, fine_dev):
    peers, tall, width = arrived.shape
    digits = fine_dev // LANES
    return pl.pallas_call(
        functools.partial(first_sums_body, group, rows, digits),
        grid=(peers // group,),
        out_shape=(
            jax.ShapeDtypeStruct((fine_dev, width), F32),
            jax.ShapeDtypeStruct((LANES, digits), F32),
        ),
        in_specs=[pl.BlockSpec((group, tall, width), lambda i: (i, 0, 0))],
        out_specs=(
            pl.BlockSpec((fine_dev, width), lambda i: (0, 0)),
            pl.BlockSpec((LANES, digits), lambda i: (0, 0)),
        ),
        scratch_shapes=[pltpu.VMEM((fine_dev, group * rows), BF16)],
        cost_estimate=pl.CostEstimate(
            flops=2 * peers * rows * fine_dev * width,
            bytes_accessed=arrived.size * 2 + fine_dev * width * 4,
            transcendentals=0,
        ),
        name="first_sums",
    )(arrived)


def last_sums_body(
    group, rows, digits, block, acc_in, counts_in, old, new, acc, counts, onehot
):
    @pl.when(pl.program_id(0) == 0)
    def _():
        acc[...] = acc_in[...]
        counts[...] = counts_in[...]

    accumulate(block, group, rows, digits, acc, counts, onehot)

    @pl.when(pl.program_id(0) == pl.num_programs(0) - 1)
    def _():
        for h in range(digits):
            at = slice(h * LANES, (h + 1) * LANES)
            total = acc[at, :] + old[at, :].astype(F32)
            new[at, :] = (total / (counts[:, h : h + 1] + 1.0)).astype(BF16)


def last_sums(arrived, acc, counts, old_fine, rows, group):
    peers, tall, width = arrived.shape
    fine_dev = old_fine.shape[0]
    digits = fine_dev // LANES
    whole = lambda a: pl.BlockSpec(a.shape, lambda i: (0, 0))
    return pl.pallas_call(
        functools.partial(last_sums_body, group, rows, digits),
        grid=(peers // group,),
        out_shape=jax.ShapeDtypeStruct((fine_dev, width), BF16),
        in_specs=[
            pl.BlockSpec((group, tall, width), lambda i: (i, 0, 0)),
            whole(acc),
            whole(counts),
            whole(old_fine),
        ],
        out_specs=pl.BlockSpec((fine_dev, width), lambda i: (0, 0)),
        scratch_shapes=[
            pltpu.VMEM((fine_dev, width), F32),
            pltpu.VMEM((LANES, digits), F32),
            pltpu.VMEM((fine_dev, group * rows), BF16),
        ],
        name="last_sums",
    )(arrived, acc, counts, old_fine)


def plan_body(coarse_dev, ids, owner_hot, rank_hot, labels):
    peers, fine_dev = owner_hot.shape
    value = ids[...]
    owner = value // coarse_dev
    local = (value - owner * coarse_dev).astype(F32)
    member = jnp.where(iota((peers, fine_dev), 0) == owner, 1.0, 0.0)
    owner_hot[...] = member
    step = 256
    before = jnp.where(iota((step, step), 0) < iota((step, step), 1), 1.0, 0.0).astype(BF16)
    carry = jnp.zeros((peers, 1), F32)
    for at in range(0, fine_dev, step):
        piece = member[:, at : at + step]
        prefix = jnp.dot(piece.astype(BF16), before, preferred_element_type=F32) + carry
        rank = jnp.sum(prefix * piece, axis=0, keepdims=True)
        carry = carry + jnp.sum(piece, axis=1, keepdims=True)
        hot = jnp.where(iota((rank_hot.shape[0], step), 0).astype(F32) == rank, 1.0, 0.0)
        rank_hot[:, at : at + step] = hot.astype(BF16)
    tagged = (member * (local + 1.0)).astype(BF16)
    labels[...] = lax.dot_general(
        tagged, rank_hot[...], (((1,), (1,)), ((), ())), preferred_element_type=F32
    )


def plan(coarse_ids, peers, capacity, coarse_dev):
    fine_dev = coarse_ids.shape[1]
    return pl.pallas_call(
        functools.partial(plan_body, coarse_dev),
        out_shape=(
            jax.ShapeDtypeStruct((peers, fine_dev), F32),
            jax.ShapeDtypeStruct((capacity, fine_dev), BF16),
            jax.ShapeDtypeStruct((peers, capacity), F32),
        ),
        name="plan_clusters",
    )(coarse_ids)


def place_body(group, owner_hot, rank_hot, new, out, placement):
    capacity, fine_dev = rank_hot.shape
    for g in range(group):
        row = jnp.broadcast_to(owner_hot[g : g + 1, :], (16, fine_dev)).astype(BF16)
        for at in range(0, capacity, 16):
            top = g * capacity + at
            placement[top : top + 16, :] = rank_hot[at : at + 16, :] * row
    sent = jnp.dot(placement[...], new[...], preferred_element_type=F32).astype(BF16)
    for g in range(group):
        out[g, :, :] = sent[g * capacity : (g + 1) * capacity, :]


def place(owner_hot, rank_hot, new_fine, group):
    peers, fine_dev = owner_hot.shape
    capacity = rank_hot.shape[0]
    width = new_fine.shape[1]
    whole = lambda a: pl.BlockSpec(a.shape, lambda i: (0, 0))
    return pl.pallas_call(
        functools.partial(place_body, group),
        grid=(peers // group,),
        out_shape=jax.ShapeDtypeStruct((peers, capacity, width), BF16),
        in_specs=[
            pl.BlockSpec((group, fine_dev), lambda i: (i, 0)),
            whole(rank_hot),
            whole(new_fine),
        ],
        out_specs=pl.BlockSpec((group, capacity, width), lambda i: (i, 0, 0)),
        scratch_shapes=[pltpu.VMEM((group * capacity, fine_dev), BF16)],
        name="place_clusters",
    )(owner_hot, rank_hot, new_fine)


def coarse_body(received, tags, old, means, onehot):
    peers, capacity, width = received.shape
    coarse_dev = old.shape[0]
    total = jnp.zeros((coarse_dev, capacity), F32)
    row = iota((coarse_dev, capacity), 0).astype(F32) + 1.0
    for p in range(peers):
        hot = jnp.where(row == tags[p, 1:2, :capacity].astype(F32), 1.0, 0.0)
        total = total + hot
        onehot[:, p * capacity : (p + 1) * capacity] = hot.astype(BF16)
    data = received[...].reshape(peers * capacity, width)
    sums = jnp.dot(onehot[...], data, preferred_element_type=F32)
    count = jnp.sum(total, axis=1, keepdims=True)
    means[...] = ((sums + old[...].astype(F32)) / (count + 1.0)).astype(BF16)


def coarse(received, arrived_tail, rows, old_coarse):
    peers, capacity, width = received.shape
    return pl.pallas_call(
        coarse_body,
        grid=(1,),
        out_shape=jax.ShapeDtypeStruct(old_coarse.shape, BF16),
        in_specs=[
            pl.BlockSpec(received.shape, lambda i: (0, 0, 0)),
            pl.BlockSpec((peers, TAIL, width), lambda i: (0, rows // TAIL, 0)),
            pl.BlockSpec(old_coarse.shape, lambda i: (0, 0)),
        ],
        out_specs=pl.BlockSpec(old_coarse.shape, lambda i: (0, 0)),
        scratch_shapes=[pltpu.VMEM((old_coarse.shape[0], peers * capacity), BF16)],
        name="coarse_means",
    )(received, arrived_tail, old_coarse)


def finish_body(groups, at, *refs):
    pieces, out, full = refs[:groups], refs[groups], refs[groups + 1]
    width = pieces[0].shape[1]
    for step in range(groups):
        place = lax.rem(at[0] + step, groups) * width
        full[:, pl.ds(pl.multiple_of(place, width), width)] = pieces[step][...].astype(F32)
    whole = full[...]
    scale = lax.rsqrt(jnp.mean(whole * whole, axis=1, keepdims=True) + 1e-06)
    out[...] = (whole * scale).astype(BF16)


def finish(at, pieces):
    groups = len(pieces)
    rows, width = pieces[0].shape
    return pl.pallas_call(
        functools.partial(finish_body, groups),
        out_shape=jax.ShapeDtypeStruct((rows, groups * width), BF16),
        in_specs=[pl.BlockSpec(memory_space=pltpu.SMEM)]
        + [pl.BlockSpec(memory_space=pltpu.VMEM)] * groups,
        scratch_shapes=[pltpu.VMEM((rows, groups * width), F32)],
        name="coarse_dirs",
    )(at, *pieces)


def exchange(slots):
    return lax.all_to_all(slots, "rows", split_axis=0, concat_axis=0, tiled=True)


def on_device(embeddings, fine_local, send_counts, old_fine, coarse_ids, old_coarse):
    peers = lax.axis_size("rows")
    groups = lax.axis_size("grp")
    per_dev = embeddings.shape[0]
    fine_dev = old_fine.shape[0]
    coarse_dev = old_coarse.shape[0]
    capacity = 2 * per_dev // peers
    capacity_two = 2 * fine_dev // peers
    second = capacity - FIRST
    local = fine_local.reshape(-1, LANES)

    slots = pack(send_counts, embeddings, local, None, 0, FIRST, capacity)
    arrived = exchange(slots)
    owner_hot, rank_hot, tags = plan(
        coarse_ids.reshape(1, -1), peers, capacity_two, coarse_dev
    )
    more_slots = pack(send_counts, embeddings, local, tags, FIRST, second, capacity)
    more = exchange(more_slots)

    acc, counts = first_sums(arrived, FIRST, 2, fine_dev)
    new_fine = last_sums(more, acc, counts, old_fine, second, 4)

    received = exchange(place(owner_hot, rank_hot, new_fine, 8))
    means = coarse(received, more, second, old_coarse)
    pieces = [means]
    for step in range(1, groups):
        back = [((g + step) % groups, g) for g in range(groups)]
        pieces.append(lax.ppermute(means, "grp", back))
    at = lax.axis_index("grp").astype(jnp.int32).reshape(1)
    return (new_fine, finish(at, pieces))


def solution(mesh):
    in_specs = (
        P("rows", "grp"),
        P("rows"),
        P("rows", None),
        P("rows", "grp"),
        P("rows"),
        P("rows", "grp"),
    )
    out_specs = (P("rows", "grp"), P("rows", None))
    return jax.shard_map(
        on_device, mesh=mesh, in_specs=in_specs, out_specs=out_specs, check_vma=False
    )
```

```python
import functools

import jax
import jax.numpy as jnp
from jax import lax
from jax.experimental import pallas as pl
from jax.experimental.pallas import tpu as pltpu
from jax.sharding import PartitionSpec as P

F32 = jnp.float32
BF16 = jnp.bfloat16
LANES = 128
TAIL = 8
SIDE = 4


def iota(shape, axis):
    return lax.broadcasted_iota(jnp.int32, shape, axis)


def device(x, y, core):
    return (x % SIDE) * 2 * SIDE + (y % SIDE) * 2 + core


CHIPS = [(x, y) for x in range(SIDE) for y in range(SIDE)]


def line_pairs(step, same_class):
    pairs = []
    for x, y in CHIPS:
        for core in range(2):
            kind = core if same_class else 1 - core
            to = device(x + step, y, 0) if kind == 0 else device(x, y + step, 1)
            pairs.append((device(x, y, core), to))
    return pairs


def cross_pairs(step):
    pairs = []
    for x, y in CHIPS:
        pairs.append((device(x, y, 0), device(x, y + step, 0)))
        pairs.append((device(x, y, 1), device(x + step, y, 1)))
    return pairs


def pack_body(slots, capacity, counts, emb, local, *rest):
    outs, (wide, labels, starts) = rest[: len(slots)], rest[len(slots) :]
    cross = pl.program_id(0)
    per_dev, width = emb.shape
    label_rows = local.shape[0]
    owners = counts.shape[1]

    @pl.when(cross == 0)
    def _():
        def add(o, total):
            starts[o] = total
            return total + counts[0, o]

        lax.fori_loop(0, owners, add, 0)
        labels[:label_rows, :] = local[...]
        labels[label_rows:, :] = jnp.zeros((16, LANES), jnp.int32)
        wide[per_dev:, :] = jnp.zeros((capacity + 8, width), F32)
        for at in range(0, per_dev, 512):
            wide[at : at + 512, :] = emb[at : at + 512, :].astype(F32)

    here = lax.axis_index("rows")
    x, y, core = here // (2 * SIDE), lax.rem(here // 2, SIDE), lax.rem(here, 2)
    line = iota((TAIL, LANES), 0) * LANES + iota((TAIL, LANES), 1)
    lane = iota((TAIL, LANES), 1)
    for (same_class, step), out in zip(slots, outs):
        kind = core if same_class else 1 - core
        along, over = lax.rem(x + jnp.where(kind == 0, step, cross), SIDE), lax.rem(
            y + jnp.where(kind == 0, cross, step), SIDE
        )
        owner = along * 2 * SIDE + over * 2 + kind
        first = starts[owner]
        count = counts[0, owner]
        aligned = first // 8
        turn = first - aligned * 8
        turn_back = lax.rem(8 - turn, 8)
        kept = iota((8, 8, width), 1) < 8 - turn
        for at in range(0, capacity, 64):
            window = wide[pl.ds(pl.multiple_of(aligned * 8 + at, 8), 72), :]
            window = pltpu.roll(window.reshape(9, 8, width), turn_back, 1)
            moved = jnp.where(kept, window[:8], window[1:])
            out[0, at : at + 64, :] = moved.reshape(64, width).astype(BF16)
        base = first // LANES
        shift = first - base * LANES
        rows = [labels[pl.ds(base + i, 1), :] for i in range(TAIL + 1)]
        low_part = jnp.concatenate(rows[:TAIL], axis=0)
        high_part = jnp.concatenate(rows[1:], axis=0)
        back = lax.rem(LANES - shift, LANES)
        low_part = pltpu.roll(low_part, back, 1)
        high_part = pltpu.roll(high_part, back, 1)
        value = jnp.where(lane < LANES - shift, low_part, high_part)
        live = line < count
        high = jnp.where(live, lax.shift_right_logical(value, 7), 64).astype(F32)
        low = jnp.where(live, value & 127, 0).astype(F32)
        out[0, capacity:, :] = jnp.concatenate([high, low], axis=1).astype(BF16)


def pack(slots, send_counts, embeddings, local, capacity):
    per_dev, width = embeddings.shape
    tall = capacity + TAIL
    whole = lambda a: pl.BlockSpec(a.shape, lambda q: (0, 0))
    return pl.pallas_call(
        functools.partial(pack_body, slots, capacity),
        grid=(SIDE,),
        out_shape=[jax.ShapeDtypeStruct((SIDE, tall, width), BF16)] * len(slots),
        in_specs=[pl.BlockSpec(memory_space=pltpu.SMEM), whole(embeddings), whole(local)],
        out_specs=[pl.BlockSpec((1, tall, width), lambda q: (q, 0, 0))] * len(slots),
        scratch_shapes=[
            pltpu.VMEM((per_dev + capacity + 8, width), F32),
            pltpu.VMEM((local.shape[0] + 16, LANES), jnp.int32),
            pltpu.SMEM((send_counts.shape[1],), jnp.int32),
        ],
        cost_estimate=pl.CostEstimate(
            flops=0,
            bytes_accessed=per_dev * width * 2 + len(slots) * SIDE * tall * width * 2,
            transcendentals=0,
        ),
        name="pack_rows",
    )(send_counts, embeddings, local)


def sums_body(sources, capacity, blocks, sent, *refs):
    arrived, refs = refs[:sources], refs[sources:]
    had_acc, had_counts = None, None
    if sent is not None:
        had_acc, had_counts, refs = refs[0], refs[1], refs[2:]
    if sent:
        out, low_hot, high_hot, onehot, data = refs
        out_counts = None
    else:
        out, out_counts, low_hot, high_hot, onehot, data = refs
    digits = high_hot.shape[0]
    depth = sources * capacity
    part = pl.program_id(1)
    size = onehot.shape[0]

    @pl.when(part == 0)
    def _():
        for s in range(sources):
            tail = arrived[s][0, capacity:, :].astype(F32)
            data[s * capacity : (s + 1) * capacity, :] = arrived[s][0, :capacity, :]
            for i in range(capacity // LANES):
                at = s * capacity + i * LANES
                high = tail[i : i + 1, :LANES]
                low = tail[i : i + 1, LANES : 2 * LANES]
                low_hot[:, at : at + LANES] = jnp.where(
                    iota((LANES, LANES), 0).astype(F32) == low, 1.0, 0.0
                ).astype(BF16)
                high_hot[:, at : at + LANES] = jnp.where(
                    iota((digits, LANES), 0).astype(F32) == high, 1.0, 0.0
                )
        counts = lax.dot_general(
            high_hot[...].astype(BF16),
            low_hot[...],
            (((1,), (1,)), ((), ())),
            preferred_element_type=F32,
        )
        if had_counts is not None:
            counts = counts + had_counts[0]
        if sent:
            tens = jnp.floor(counts / 64.0)
            out[blocks * size :, :] = jnp.concatenate(
                [tens, counts - 64.0 * tens], axis=1
            ).astype(BF16)
        else:
            out_counts[0] = counts

    group = size // LANES
    for h in range(group):
        row = high_hot[pl.ds(pl.multiple_of(part * group, group), group), :][h : h + 1, :]
        row = jnp.broadcast_to(row, (16, depth)).astype(BF16)
        for at in range(0, LANES, 16):
            onehot[h * LANES + at : h * LANES + at + 16, :] = low_hot[at : at + 16, :] * row
    total = jnp.dot(onehot[...], data[...], preferred_element_type=F32)
    if had_acc is not None:
        total = total + had_acc[0]
    if sent:
        out[pl.ds(pl.multiple_of(part * size, size), size), :] = total.astype(BF16)
    else:
        out[0] = total


def line_sums(arrived, capacity, fine_dev, cross=None, had=None):
    width = arrived[0].shape[2]
    tall = capacity + TAIL
    sources = len(arrived)
    digits = fine_dev // LANES
    size = fine_dev // 2
    blocks = fine_dev // size
    base = 0 if cross is None else cross
    many = SIDE if cross is None else 1
    sent = None if cross is None else cross != 0
    operands = list(arrived)
    in_specs = [pl.BlockSpec((1, tall, width), lambda q, m: (base + q, 0, 0))] * sources
    if had is not None:
        operands += list(had)
        in_specs += [
            pl.BlockSpec((1, size, width), lambda q, m: (base + q, m, 0)),
            pl.BlockSpec((1, digits, LANES), lambda q, m: (base + q, 0, 0)),
        ]
    if sent:
        out_shape = jax.ShapeDtypeStruct((fine_dev + 16, width), BF16)
        out_specs = pl.BlockSpec((fine_dev + 16, width), lambda q, m: (0, 0))
    else:
        out_shape = (
            jax.ShapeDtypeStruct((many, fine_dev, width), F32),
            jax.ShapeDtypeStruct((many, digits, LANES), F32),
        )
        out_specs = (
            pl.BlockSpec((1, size, width), lambda q, m: (q, m, 0)),
            pl.BlockSpec((1, digits, LANES), lambda q, m: (q, 0, 0)),
        )
    return pl.pallas_call(
        functools.partial(sums_body, sources, capacity, blocks, sent),
        grid=(many, blocks),
        out_shape=out_shape,
        in_specs=in_specs,
        out_specs=out_specs,
        scratch_shapes=[
            pltpu.VMEM((LANES, sources * capacity), BF16),
            pltpu.VMEM((digits, sources * capacity), F32),
            pltpu.VMEM((size, sources * capacity), BF16),
            pltpu.VMEM((sources * capacity, width), BF16),
        ],
        cost_estimate=pl.CostEstimate(
            flops=2 * many * sources * capacity * fine_dev * width,
            bytes_accessed=many * (sources * tall * width * 2 + fine_dev * width * 8),
            transcendentals=0,
        ),
        name="line_sums",
    )(*operands)


def update_body(acc, counts, old, *refs):
    steps = SIDE - 1
    got, tails, new, column = refs[:steps], refs[steps : 2 * steps], refs[-2], refs[-1]
    digits = counts.shape[1]
    part = pl.program_id(0)
    group = old.shape[0] // LANES

    @pl.when(part == 0)
    def _():
        count = counts[0]
        for tail in tails:
            value = tail[...].astype(F32)
            count = count + value[:, :LANES] * 64.0 + value[:, LANES : 2 * LANES]
        tens = jnp.floor(count / 64.0)
        eye = jnp.where(iota((LANES, LANES), 0) == iota((LANES, LANES), 1), 1.0, 0.0)
        turn = lambda a: lax.dot_general(
            eye.astype(BF16), a.astype(BF16), (((1,), (1,)), ((), ())), preferred_element_type=F32
        )
        column[...] = turn(tens) * 64.0 + turn(count - 64.0 * tens)

    for p in range(digits // group):

        @pl.when(part == p)
        def _():
            for h in range(group):
                at = slice(h * LANES, (h + 1) * LANES)
                total = acc[0, at, :] + old[at, :].astype(F32)
                for g in got:
                    total = total + g[at, :].astype(F32)
                count = column[:, p * group + h : p * group + h + 1]
                new[at, :] = (total / (count + 1.0)).astype(BF16)


def update(acc, counts, old_fine, got):
    fine_dev, width = old_fine.shape
    digits = fine_dev // LANES
    size = fine_dev // 4
    return pl.pallas_call(
        update_body,
        grid=(fine_dev // size,),
        out_shape=jax.ShapeDtypeStruct((fine_dev, width), BF16),
        in_specs=[
            pl.BlockSpec((1, size, width), lambda m: (0, m, 0)),
            pl.BlockSpec((1, digits, LANES), lambda m: (0, 0, 0)),
            pl.BlockSpec((size, width), lambda m: (m, 0)),
        ]
        + [pl.BlockSpec((size, width), lambda m: (m, 0))] * len(got)
        + [pl.BlockSpec((16, width), lambda m: (fine_dev // 16, 0))] * len(got),
        out_specs=pl.BlockSpec((size, width), lambda m: (m, 0)),
        scratch_shapes=[pltpu.VMEM((LANES, digits), F32)],
        name="new_fine",
    )(acc, counts, old_fine, *got, *got)


def plan_body(coarse_dev, ids, owner_hot, rank_hot, labels):
    peers, fine_dev = owner_hot.shape
    value = ids[...]
    owner = value // coarse_dev
    local = (value - owner * coarse_dev).astype(F32)
    member = jnp.where(iota((peers, fine_dev), 0) == owner, 1.0, 0.0)
    owner_hot[...] = member
    step = 256
    before = jnp.where(iota((step, step), 0) < iota((step, step), 1), 1.0, 0.0).astype(BF16)
    carry = jnp.zeros((peers, 1), F32)
    for at in range(0, fine_dev, step):
        piece = member[:, at : at + step]
        prefix = jnp.dot(piece.astype(BF16), before, preferred_element_type=F32) + carry
        rank = jnp.sum(prefix * piece, axis=0, keepdims=True)
        carry = carry + jnp.sum(piece, axis=1, keepdims=True)
        hot = jnp.where(iota((rank_hot.shape[0], step), 0).astype(F32) == rank, 1.0, 0.0)
        rank_hot[:, at : at + step] = hot.astype(BF16)
    tagged = (member * (local + 1.0)).astype(BF16)
    labels[...] = lax.dot_general(
        tagged, rank_hot[...], (((1,), (1,)), ((), ())), preferred_element_type=F32
    )


def plan(coarse_ids, peers, capacity, coarse_dev):
    fine_dev = coarse_ids.shape[1]
    return pl.pallas_call(
        functools.partial(plan_body, coarse_dev),
        out_shape=(
            jax.ShapeDtypeStruct((peers, fine_dev), F32),
            jax.ShapeDtypeStruct((capacity, fine_dev), BF16),
            jax.ShapeDtypeStruct((peers, capacity), F32),
        ),
        name="plan_clusters",
    )(coarse_ids)


def place_body(group, owner_hot, rank_hot, tags, new, out, placement):
    capacity, fine_dev = rank_hot.shape
    for g in range(group):
        row = jnp.broadcast_to(owner_hot[g : g + 1, :], (16, fine_dev)).astype(BF16)
        for at in range(0, capacity, 16):
            top = g * capacity + at
            placement[top : top + 16, :] = rank_hot[at : at + 16, :] * row
    sent = jnp.dot(placement[...], new[...], preferred_element_type=F32).astype(BF16)
    for g in range(group):
        out[g, :capacity, :] = sent[g * capacity : (g + 1) * capacity, :]
        tag = jnp.broadcast_to(tags[g : g + 1, :], (TAIL, capacity))
        out[g, capacity:, :] = jnp.concatenate([tag, tag], axis=1).astype(BF16)


def place(owner_hot, rank_hot, tags, new_fine, group):
    peers, fine_dev = owner_hot.shape
    capacity = rank_hot.shape[0]
    width = new_fine.shape[1]
    whole = lambda a: pl.BlockSpec(a.shape, lambda i: (0, 0))
    return pl.pallas_call(
        functools.partial(place_body, group),
        grid=(peers // group,),
        out_shape=jax.ShapeDtypeStruct((peers, capacity + TAIL, width), BF16),
        in_specs=[
            pl.BlockSpec((group, fine_dev), lambda i: (i, 0)),
            whole(rank_hot),
            pl.BlockSpec((group, capacity), lambda i: (i, 0)),
            whole(new_fine),
        ],
        out_specs=pl.BlockSpec((group, capacity + TAIL, width), lambda i: (i, 0, 0)),
        scratch_shapes=[pltpu.VMEM((group * capacity, fine_dev), BF16)],
        name="place_clusters",
    )(owner_hot, rank_hot, tags, new_fine)


def coarse_body(received, old, means, onehot, data):
    peers, tall, width = received.shape
    capacity = tall - TAIL
    coarse_dev = old.shape[0]
    total = jnp.zeros((coarse_dev, capacity), F32)
    row = iota((coarse_dev, capacity), 0).astype(F32) + 1.0
    for p in range(peers):
        tag = received[p, capacity:, :].astype(F32)[:1, :capacity]
        hot = jnp.where(row == tag, 1.0, 0.0)
        total = total + hot
        onehot[:, p * capacity : (p + 1) * capacity] = hot.astype(BF16)
        data[p * capacity : (p + 1) * capacity, :] = received[p, :capacity, :]
    sums = jnp.dot(onehot[...], data[...], preferred_element_type=F32)
    count = jnp.sum(total, axis=1, keepdims=True)
    means[...] = ((sums + old[...].astype(F32)) / (count + 1.0)).astype(BF16)


def coarse(received, old_coarse):
    peers, tall, width = received.shape
    deep = peers * (tall - TAIL)
    return pl.pallas_call(
        coarse_body,
        out_shape=jax.ShapeDtypeStruct(old_coarse.shape, BF16),
        scratch_shapes=[
            pltpu.VMEM((old_coarse.shape[0], deep), BF16),
            pltpu.VMEM((deep, width), BF16),
        ],
        name="coarse_means",
    )(received, old_coarse)


def finish_body(groups, at, *refs):
    pieces, out, full = refs[:groups], refs[groups], refs[groups + 1]
    width = pieces[0].shape[1]
    for step in range(groups):
        place = lax.rem(at[0] + step, groups) * width
        full[:, pl.ds(pl.multiple_of(place, width), width)] = pieces[step][...].astype(F32)
    whole = full[...]
    scale = lax.rsqrt(jnp.mean(whole * whole, axis=1, keepdims=True) + 1e-06)
    out[...] = (whole * scale).astype(BF16)


def finish(at, pieces):
    groups = len(pieces)
    rows, width = pieces[0].shape
    return pl.pallas_call(
        functools.partial(finish_body, groups),
        out_shape=jax.ShapeDtypeStruct((rows, groups * width), BF16),
        in_specs=[pl.BlockSpec(memory_space=pltpu.SMEM)]
        + [pl.BlockSpec(memory_space=pltpu.VMEM)] * groups,
        scratch_shapes=[pltpu.VMEM((rows, groups * width), F32)],
        name="coarse_dirs",
    )(at, *pieces)


def exchange(slots):
    return lax.all_to_all(slots, "rows", split_axis=0, concat_axis=0, tiled=True)


def on_device(embeddings, fine_local, send_counts, old_fine, coarse_ids, old_coarse):
    peers = lax.axis_size("rows")
    groups = lax.axis_size("grp")
    per_dev = embeddings.shape[0]
    fine_dev = old_fine.shape[0]
    coarse_dev = old_coarse.shape[0]
    capacity = 2 * per_dev // peers
    capacity_two = 2 * fine_dev // peers
    local = fine_local.reshape(-1, LANES)
    steps = range(1, SIDE)

    def along(slots, step, same_class):
        return lax.ppermute(slots, "rows", line_pairs(step, same_class))

    keep = pack([(True, s) for s in steps], send_counts, embeddings, local, capacity)
    kept = [along(keep[s - 1], s, True) for s in steps]
    give = pack(
        [(False, s) for s in (1, 2, 3, 0)] + [(True, 0)], send_counts, embeddings, local, capacity
    )
    given = [along(give[s - 1], s, False) for s in steps]
    swapped = along(give[3], 0, False)
    owner_hot, rank_hot, tags = plan(
        coarse_ids.reshape(1, -1), peers, capacity_two, coarse_dev
    )
    had = line_sums([give[4], swapped, kept[0], kept[2]], capacity, fine_dev)
    rest = [kept[1], given[0], given[2], given[1]]
    got = {}
    for cross in (2, 1, 3):
        part = line_sums(rest, capacity, fine_dev, cross, had)
        got[cross] = lax.ppermute(part, "rows", cross_pairs(cross))
    acc, counts = line_sums(rest, capacity, fine_dev, 0, had)
    new_fine = update(acc, counts, old_fine, [got[c] for c in steps])

    received = exchange(place(owner_hot, rank_hot, tags, new_fine, 8))
    means = coarse(received, old_coarse)
    pieces = [means]
    for step in range(1, groups):
        back = [((g + step) % groups, g) for g in range(groups)]
        pieces.append(lax.ppermute(means, "grp", back))
    at = lax.axis_index("grp").astype(jnp.int32).reshape(1)
    return (new_fine, finish(at, pieces))


def solution(mesh):
    in_specs = (
        P("rows", "grp"),
        P("rows"),
        P("rows", None),
        P("rows", "grp"),
        P("rows"),
        P("rows", "grp"),
    )
    out_specs = (P("rows", "grp"), P("rows", None))
    return jax.shard_map(
        on_device, mesh=mesh, in_specs=in_specs, out_specs=out_specs, check_vma=False
    )
```

```python
import functools

import jax
import jax.numpy as jnp
from jax import lax
from jax.experimental import pallas as pl
from jax.experimental.pallas import tpu as pltpu
from jax.sharding import PartitionSpec as P


F32 = jnp.float32
BF16 = jnp.bfloat16
LANES = 128
TAIL = 8
SIDE = 4


def iota(shape, axis):
    return lax.broadcasted_iota(jnp.int32, shape, axis)


def device(x, y, core):
    return (x % SIDE) * 2 * SIDE + (y % SIDE) * 2 + core


CHIPS = [(x, y) for x in range(SIDE) for y in range(SIDE)]


def line_pairs(step, same_class):
    pairs = []
    for x, y in CHIPS:
        for core in range(2):
            kind = core if same_class else 1 - core
            to = device(x + step, y, 0) if kind == 0 else device(x, y + step, 1)
            pairs.append((device(x, y, core), to))
    return pairs


def cross_pairs(step):
    pairs = []
    for x, y in CHIPS:
        pairs.append((device(x, y, 0), device(x, y + step, 0)))
        pairs.append((device(x, y, 1), device(x + step, y, 1)))
    return pairs


def pack_body(slots, capacity, counts, emb, local, *rest):
    outs, (rows, labels, starts, done) = rest[: len(slots)], rest[len(slots) :]
    per_dev, width = emb.shape
    label_rows = local.shape[0]
    owners = counts.shape[1]
    at_step = pl.program_id(0)

    @pl.when(at_step == 0)
    def _():
        fetch = pltpu.make_async_copy(emb, rows.at[:per_dev, :], done)
        fetch.start()

        def add(o, total):
            starts[o] = total
            return total + counts[0, o]

        lax.fori_loop(0, owners, add, 0)
        labels[:label_rows, :] = local[...]
        labels[label_rows:, :] = jnp.zeros((16, LANES), jnp.int32)
        rows[per_dev:, :] = jnp.zeros((capacity + 16, width), BF16)
        fetch.wait()

    here = lax.axis_index("rows")
    x, y, core = here // (2 * SIDE), lax.rem(here // 2, SIDE), lax.rem(here, 2)
    line = iota((TAIL, LANES), 0) * LANES + iota((TAIL, LANES), 1)
    lane = iota((TAIL, LANES), 1)
    for (same_class, step, crosses), out in zip(slots, outs):

        @pl.when(at_step < len(crosses))
        def _():
            cross = at_step + crosses[0]
            kind = core if same_class else 1 - core
            along = lax.rem(x + jnp.where(kind == 0, step, cross), SIDE)
            over = lax.rem(y + jnp.where(kind == 0, cross, step), SIDE)
            owner = along * 2 * SIDE + over * 2 + kind
            first = starts[owner]
            count = counts[0, owner]
            aligned = first // 16
            turn = first - aligned * 16
            far = turn >= 8
            small = jnp.where(far, turn - 8, turn)
            turn_back = lax.rem(8 - small, 8)
            kept = iota((9, 8, width), 1) < 8 - small
            for at in range(0, capacity, 64):
                window = rows[pl.ds(pl.multiple_of(aligned * 16 + at, 16), 80), :]
                window = window.astype(F32).reshape(10, 8, width)
                window = pltpu.roll(window, turn_back, 1)
                moved = jnp.where(kept, window[:9], window[1:])
                moved = jnp.where(far, moved[1:], moved[:8])
                out[0, at : at + 64, :] = moved.reshape(64, width).astype(BF16)
            base = first // LANES
            shift = first - base * LANES
            got = [labels[pl.ds(base + i, 1), :] for i in range(TAIL + 1)]
            low_part = jnp.concatenate(got[:TAIL], axis=0)
            high_part = jnp.concatenate(got[1:], axis=0)
            back = lax.rem(LANES - shift, LANES)
            low_part = pltpu.roll(low_part, back, 1)
            high_part = pltpu.roll(high_part, back, 1)
            value = jnp.where(lane < LANES - shift, low_part, high_part)
            live = line < count
            high = jnp.where(live, lax.shift_right_logical(value, 7), 64).astype(F32)
            low = jnp.where(live, value & 127, 0).astype(F32)
            out[0, capacity:, :] = jnp.concatenate([high, low], axis=1).astype(BF16)


def pack(slots, send_counts, embeddings, local, capacity):
    per_dev, width = embeddings.shape
    tall = capacity + TAIL
    longest = max(len(c) for _, _, c in slots)

    def spec(length):
        return pl.BlockSpec((1, tall, width), lambda q: (jnp.minimum(q, length - 1), 0, 0))

    many = sum(len(c) for _, _, c in slots)
    return pl.pallas_call(
        functools.partial(pack_body, slots, capacity),
        grid=(longest,),
        out_shape=[jax.ShapeDtypeStruct((len(c), tall, width), BF16) for _, _, c in slots],
        in_specs=[
            pl.BlockSpec(memory_space=pltpu.SMEM),
            pl.BlockSpec(memory_space=pl.ANY),
            pl.BlockSpec(local.shape, lambda q: (0, 0)),
        ],
        out_specs=[spec(len(c)) for _, _, c in slots],
        scratch_shapes=[
            pltpu.VMEM((per_dev + capacity + 16, width), BF16),
            pltpu.VMEM((local.shape[0] + 16, LANES), jnp.int32),
            pltpu.SMEM((send_counts.shape[1],), jnp.int32),
            pltpu.SemaphoreType.DMA,
        ],
        cost_estimate=pl.CostEstimate(
            flops=0,
            bytes_accessed=per_dev * width * 2 + many * tall * width * 2,
            transcendentals=0,
        ),
        name="pack_rows",
    )(send_counts, embeddings, local)


def sums_body(sources, capacity, blocks, had, sent, *refs):
    arrived, refs = refs[:sources], refs[sources:]
    had_acc, had_counts = None, None
    if had:
        had_acc, had_counts, refs = refs[0], refs[1], refs[2:]
    if sent:
        out, low_hot, high_hot, onehot, data = refs
        out_counts = None
    else:
        out, out_counts, low_hot, high_hot, onehot, data = refs
    digits = high_hot.shape[0]
    depth = sources * capacity
    part = pl.program_id(1)
    size = onehot.shape[0]

    @pl.when(part == 0)
    def _():
        for s in range(sources):
            tail = arrived[s][0, capacity:, :].astype(F32)
            data[s * capacity : (s + 1) * capacity, :] = arrived[s][0, :capacity, :]
            for i in range(capacity // LANES):
                at = s * capacity + i * LANES
                high = tail[i : i + 1, :LANES]
                low = tail[i : i + 1, LANES : 2 * LANES]
                low_hot[:, at : at + LANES] = jnp.where(
                    iota((LANES, LANES), 0).astype(F32) == low, 1.0, 0.0
                ).astype(BF16)
                high_hot[:, at : at + LANES] = jnp.where(
                    iota((digits, LANES), 0).astype(F32) == high, 1.0, 0.0
                )
        counts = lax.dot_general(
            high_hot[...].astype(BF16),
            low_hot[...],
            (((1,), (1,)), ((), ())),
            preferred_element_type=F32,
        )
        if had_counts is not None:
            counts = counts + had_counts[0]
        if sent:
            tens = jnp.floor(counts / 64.0)
            out[blocks * size :, :] = jnp.concatenate(
                [tens, counts - 64.0 * tens], axis=1
            ).astype(BF16)
        else:
            out_counts[0] = counts

    group = size // LANES
    for h in range(group):
        row = high_hot[pl.ds(pl.multiple_of(part * group, group), group), :][h : h + 1, :]
        row = jnp.broadcast_to(row, (16, depth)).astype(BF16)
        for at in range(0, LANES, 16):
            onehot[h * LANES + at : h * LANES + at + 16, :] = low_hot[at : at + 16, :] * row
    total = jnp.dot(onehot[...], data[...], preferred_element_type=F32)
    if had_acc is not None:
        total = total + had_acc[0]
    if sent:
        out[pl.ds(pl.multiple_of(part * size, size), size), :] = total.astype(BF16)
    else:
        out[0] = total


def line_sums(arrived, capacity, fine_dev, crosses, had=None, send=False):
    width = arrived[0][0].shape[2]
    tall = capacity + TAIL
    sources = len(arrived)
    digits = fine_dev // LANES
    size = fine_dev // 2
    blocks = fine_dev // size
    many = len(crosses)

    def source(lowest):
        at = crosses[0] - lowest
        return pl.BlockSpec((1, tall, width), lambda q, m: (at + q, 0, 0))

    operands = [a for a, _ in arrived]
    in_specs = [source(lowest) for _, lowest in arrived]
    if had is not None:
        acc, counts, lowest = had
        at = crosses[0] - lowest
        operands += [acc, counts]
        in_specs += [
            pl.BlockSpec((1, size, width), lambda q, m: (at + q, m, 0)),
            pl.BlockSpec((1, digits, LANES), lambda q, m: (at + q, 0, 0)),
        ]
    if send:
        out_shape = jax.ShapeDtypeStruct((fine_dev + 16, width), BF16)
        out_specs = pl.BlockSpec((fine_dev + 16, width), lambda q, m: (0, 0))
    else:
        out_shape = (
            jax.ShapeDtypeStruct((many, fine_dev, width), F32),
            jax.ShapeDtypeStruct((many, digits, LANES), F32),
        )
        out_specs = (
            pl.BlockSpec((1, size, width), lambda q, m: (q, m, 0)),
            pl.BlockSpec((1, digits, LANES), lambda q, m: (q, 0, 0)),
        )
    return pl.pallas_call(
        functools.partial(sums_body, sources, capacity, blocks, had is not None, send),
        grid=(many, blocks),
        out_shape=out_shape,
        in_specs=in_specs,
        out_specs=out_specs,
        scratch_shapes=[
            pltpu.VMEM((LANES, sources * capacity), BF16),
            pltpu.VMEM((digits, sources * capacity), F32),
            pltpu.VMEM((size, sources * capacity), BF16),
            pltpu.VMEM((sources * capacity, width), BF16),
        ],
        cost_estimate=pl.CostEstimate(
            flops=2 * many * sources * capacity * fine_dev * width,
            bytes_accessed=many * (sources * tall * width * 2 + fine_dev * width * 8),
            transcendentals=0,
        ),
        name="line_sums",
    )(*operands)


def update_body(acc, counts, old, *refs):
    steps = SIDE - 1
    got, tails, new, column = refs[:steps], refs[steps : 2 * steps], refs[-2], refs[-1]
    digits = counts.shape[1]
    part = pl.program_id(0)
    group = old.shape[0] // LANES

    @pl.when(part == 0)
    def _():
        count = counts[0]
        for tail in tails:
            value = tail[...].astype(F32)
            count = count + value[:, :LANES] * 64.0 + value[:, LANES : 2 * LANES]
        tens = jnp.floor(count / 64.0)
        eye = jnp.where(iota((LANES, LANES), 0) == iota((LANES, LANES), 1), 1.0, 0.0)
        turn = lambda a: lax.dot_general(
            eye.astype(BF16), a.astype(BF16), (((1,), (1,)), ((), ())), preferred_element_type=F32
        )
        column[...] = turn(tens) * 64.0 + turn(count - 64.0 * tens)

    for p in range(digits // group):

        @pl.when(part == p)
        def _():
            for h in range(group):
                at = slice(h * LANES, (h + 1) * LANES)
                total = acc[0, at, :] + old[at, :].astype(F32)
                for g in got:
                    total = total + g[at, :].astype(F32)
                count = column[:, p * group + h : p * group + h + 1]
                new[at, :] = (total / (count + 1.0)).astype(BF16)


def update(acc, counts, old_fine, got):
    fine_dev, width = old_fine.shape
    digits = fine_dev // LANES
    size = fine_dev // 4
    return pl.pallas_call(
        update_body,
        grid=(fine_dev // size,),
        out_shape=jax.ShapeDtypeStruct((fine_dev, width), BF16),
        in_specs=[
            pl.BlockSpec((1, size, width), lambda m: (0, m, 0)),
            pl.BlockSpec((1, digits, LANES), lambda m: (0, 0, 0)),
            pl.BlockSpec((size, width), lambda m: (m, 0)),
        ]
        + [pl.BlockSpec((size, width), lambda m: (m, 0))] * len(got)
        + [pl.BlockSpec((16, width), lambda m: (fine_dev // 16, 0))] * len(got),
        out_specs=pl.BlockSpec((size, width), lambda m: (m, 0)),
        scratch_shapes=[pltpu.VMEM((LANES, digits), F32)],
        name="new_fine",
    )(acc, counts, old_fine, *got, *got)


def plan_body(coarse_dev, ids, owner_hot, rank_hot, labels):
    peers, fine_dev = owner_hot.shape
    value = ids[...]
    owner = value // coarse_dev
    local = (value - owner * coarse_dev).astype(F32)
    member = jnp.where(iota((peers, fine_dev), 0) == owner, 1.0, 0.0)
    owner_hot[...] = member
    step = 256
    before = jnp.where(iota((step, step), 0) < iota((step, step), 1), 1.0, 0.0).astype(BF16)
    carry = jnp.zeros((peers, 1), F32)
    for at in range(0, fine_dev, step):
        piece = member[:, at : at + step]
        prefix = jnp.dot(piece.astype(BF16), before, preferred_element_type=F32) + carry
        rank = jnp.sum(prefix * piece, axis=0, keepdims=True)
        carry = carry + jnp.sum(piece, axis=1, keepdims=True)
        hot = jnp.where(iota((rank_hot.shape[0], step), 0).astype(F32) == rank, 1.0, 0.0)
        rank_hot[:, at : at + step] = hot.astype(BF16)
    tagged = (member * (local + 1.0)).astype(BF16)
    labels[...] = lax.dot_general(
        tagged, rank_hot[...], (((1,), (1,)), ((), ())), preferred_element_type=F32
    )


def plan(coarse_ids, peers, capacity, coarse_dev):
    fine_dev = coarse_ids.shape[1]
    return pl.pallas_call(
        functools.partial(plan_body, coarse_dev),
        out_shape=(
            jax.ShapeDtypeStruct((peers, fine_dev), F32),
            jax.ShapeDtypeStruct((capacity, fine_dev), BF16),
            jax.ShapeDtypeStruct((peers, capacity), F32),
        ),
        name="plan_clusters",
    )(coarse_ids)


def place_body(group, owner_hot, rank_hot, tags, new, out, placement):
    capacity, fine_dev = rank_hot.shape
    for g in range(group):
        row = jnp.broadcast_to(owner_hot[g : g + 1, :], (16, fine_dev)).astype(BF16)
        for at in range(0, capacity, 16):
            top = g * capacity + at
            placement[top : top + 16, :] = rank_hot[at : at + 16, :] * row
    sent = jnp.dot(placement[...], new[...], preferred_element_type=F32).astype(BF16)
    for g in range(group):
        out[g, :capacity, :] = sent[g * capacity : (g + 1) * capacity, :]
        tag = jnp.broadcast_to(tags[g : g + 1, :], (TAIL, capacity))
        out[g, capacity:, :] = jnp.concatenate([tag, tag], axis=1).astype(BF16)


def place(owner_hot, rank_hot, tags, new_fine, group):
    peers, fine_dev = owner_hot.shape
    capacity = rank_hot.shape[0]
    width = new_fine.shape[1]
    whole = lambda a: pl.BlockSpec(a.shape, lambda i: (0, 0))
    return pl.pallas_call(
        functools.partial(place_body, group),
        grid=(peers // group,),
        out_shape=jax.ShapeDtypeStruct((peers, capacity + TAIL, width), BF16),
        in_specs=[
            pl.BlockSpec((group, fine_dev), lambda i: (i, 0)),
            whole(rank_hot),
            pl.BlockSpec((group, capacity), lambda i: (i, 0)),
            whole(new_fine),
        ],
        out_specs=pl.BlockSpec((group, capacity + TAIL, width), lambda i: (i, 0, 0)),
        scratch_shapes=[pltpu.VMEM((group * capacity, fine_dev), BF16)],
        name="place_clusters",
    )(owner_hot, rank_hot, tags, new_fine)


def coarse_body(received, old, means, onehot, data):
    peers, tall, _ = received.shape
    capacity = tall - TAIL
    coarse_dev = old.shape[0]
    total = jnp.zeros((coarse_dev, capacity), F32)
    row = iota((coarse_dev, capacity), 0).astype(F32) + 1.0
    for p in range(peers):
        tag = received[p, capacity:, :].astype(F32)[:1, :capacity]
        hot = jnp.where(row == tag, 1.0, 0.0)
        total = total + hot
        onehot[:, p * capacity : (p + 1) * capacity] = hot.astype(BF16)
        data[p * capacity : (p + 1) * capacity, :] = received[p, :capacity, :]
    sums = jnp.dot(onehot[...], data[...], preferred_element_type=F32)
    count = jnp.sum(total, axis=1, keepdims=True)
    means[...] = ((sums + old[...].astype(F32)) / (count + 1.0)).astype(BF16)


def coarse(received, old_coarse):
    peers, tall, width = received.shape
    deep = peers * (tall - TAIL)
    return pl.pallas_call(
        coarse_body,
        out_shape=jax.ShapeDtypeStruct(old_coarse.shape, BF16),
        scratch_shapes=[
            pltpu.VMEM((old_coarse.shape[0], deep), BF16),
            pltpu.VMEM((deep, width), BF16),
        ],
        name="coarse_means",
    )(received, old_coarse)


def finish_body(groups, at, *refs):
    pieces, out, full = refs[:groups], refs[groups], refs[groups + 1]
    width = pieces[0].shape[1]
    for step in range(groups):
        place = lax.rem(at[0] + step, groups) * width
        full[:, pl.ds(pl.multiple_of(place, width), width)] = pieces[step][...].astype(F32)
    whole = full[...]
    scale = lax.rsqrt(jnp.mean(whole * whole, axis=1, keepdims=True) + 1e-06)
    out[...] = (whole * scale).astype(BF16)


def finish(at, pieces):
    groups = len(pieces)
    rows, width = pieces[0].shape
    return pl.pallas_call(
        functools.partial(finish_body, groups),
        out_shape=jax.ShapeDtypeStruct((rows, groups * width), BF16),
        in_specs=[pl.BlockSpec(memory_space=pltpu.SMEM)]
        + [pl.BlockSpec(memory_space=pltpu.VMEM)] * groups,
        scratch_shapes=[pltpu.VMEM((rows, groups * width), F32)],
        name="coarse_dirs",
    )(at, *pieces)


def exchange(slots):
    return lax.all_to_all(slots, "rows", split_axis=0, concat_axis=0, tiled=True)


def level_step(embeddings, fine_local, send_counts, old_fine, coarse_ids, old_coarse):
    peers = lax.axis_size("rows")
    groups = lax.axis_size("grp")
    per_dev = embeddings.shape[0]
    fine_dev = old_fine.shape[0]
    coarse_dev = old_coarse.shape[0]
    capacity = 2 * per_dev // peers
    capacity_two = 2 * fine_dev // peers
    local = fine_local.reshape(-1, LANES)
    steps = range(1, SIDE)

    def along(slots, step, same_class):
        return lax.ppermute(slots, "rows", line_pairs(step, same_class))

    rows = (send_counts, embeddings, local, capacity)
    sent, own = tuple(steps), (0,)
    order = (2, 1, 3)

    keep = pack([(True, s, sent) for s in order], *rows)
    kept = [along(a, s, True) for s, a in zip(order, keep)]
    more = pack(
        [(False, s, sent) for s in order]
        + [(False, 0, own + sent), (True, 0, own + sent)]
        + [(k, s, own) for k in (True, False) for s in order],
        *rows,
    )
    swapped = along(more[3], 0, False)
    given = [along(a, s, False) for s, a in zip(order, more[:3])]
    kept_own = [along(a, s, True) for s, a in zip(order, more[5:8])]
    given_own = [along(a, s, False) for s, a in zip(order, more[8:])]
    owner_hot, rank_hot, tags = plan(
        coarse_ids.reshape(1, -1), peers, capacity_two, coarse_dev
    )
    near = [(more[4], 0), (swapped, 0)]
    had = line_sums(near + [(a, 1) for a in kept], capacity, fine_dev, sent)
    got = {}
    for cross in order:
        part = line_sums(
            [(a, 1) for a in given], capacity, fine_dev, (cross,), (*had, 1), send=True
        )
        got[cross] = lax.ppermute(part, "rows", cross_pairs(cross))
    acc, counts = line_sums(
        near + [(a, 0) for a in kept_own + given_own], capacity, fine_dev, own
    )
    new_fine = update(acc, counts, old_fine, [got[c] for c in steps])

    received = exchange(place(owner_hot, rank_hot, tags, new_fine, 8))
    means = coarse(received, old_coarse)
    pieces = [means]
    for step in range(1, groups):
        back = [((g + step) % groups, g) for g in range(groups)]
        pieces.append(lax.ppermute(means, "grp", back))
    at = lax.axis_index("grp").astype(jnp.int32).reshape(1)
    return (new_fine, finish(at, pieces))


def solution(mesh):
    in_specs = (
        P("rows", "grp"),
        P("rows"),
        P("rows", None),
        P("rows", "grp"),
        P("rows"),
        P("rows", "grp"),
    )
    out_specs = (P("rows", "grp"), P("rows", None))
    return jax.shard_map(
        level_step, mesh=mesh, in_specs=in_specs, out_specs=out_specs, check_vma=False
    )
```

```python
import functools

import jax
import jax.numpy as jnp
from jax import lax
from jax.experimental import pallas as pl
from jax.experimental.pallas import tpu as pltpu
from jax.sharding import PartitionSpec as P


F32 = jnp.float32
BF16 = jnp.bfloat16
LANES = 128
MIB = 1024 * 1024
TAIL = 8
SIDE = 4


def iota(shape, axis):
    return lax.broadcasted_iota(jnp.int32, shape, axis)


def device(x, y, core):
    return (x % SIDE) * 2 * SIDE + (y % SIDE) * 2 + core


CHIPS = [(x, y) for x in range(SIDE) for y in range(SIDE)]


def line_pairs(step, same_class):
    pairs = []
    for x, y in CHIPS:
        for core in range(2):
            kind = core if same_class else 1 - core
            to = device(x + step, y, 0) if kind == 0 else device(x, y + step, 1)
            pairs.append((device(x, y, core), to))
    return pairs


def cross_pairs(step):
    pairs = []
    for x, y in CHIPS:
        pairs.append((device(x, y, 0), device(x, y + step, 0)))
        pairs.append((device(x, y, 1), device(x + step, y, 1)))
    return pairs


def pack_body(slots, capacity, counts, emb, local, *rest):
    outs, (rows, labels, starts, done) = rest[: len(slots)], rest[len(slots) :]
    per_dev, width = emb.shape
    label_rows = local.shape[0]
    owners = counts.shape[1]
    at_step = pl.program_id(0)

    @pl.when(at_step == 0)
    def _():
        fetch = pltpu.make_async_copy(emb, rows.at[:per_dev, :], done)
        fetch.start()

        def add(o, total):
            starts[o] = total
            return total + counts[0, o]

        lax.fori_loop(0, owners, add, 0)
        labels[:label_rows, :] = local[...]
        labels[label_rows:, :] = jnp.zeros((16, LANES), jnp.int32)
        rows[per_dev:, :] = jnp.zeros((capacity + 16, width), BF16)
        fetch.wait()

    here = lax.axis_index("rows")
    x, y, core = here // (2 * SIDE), lax.rem(here // 2, SIDE), lax.rem(here, 2)
    line = iota((TAIL, LANES), 0) * LANES + iota((TAIL, LANES), 1)
    lane = iota((TAIL, LANES), 1)
    for (same_class, step, crosses), out in zip(slots, outs):

        @pl.when(at_step < len(crosses))
        def _():
            cross = at_step + crosses[0]
            kind = core if same_class else 1 - core
            along = lax.rem(x + jnp.where(kind == 0, step, cross), SIDE)
            over = lax.rem(y + jnp.where(kind == 0, cross, step), SIDE)
            owner = along * 2 * SIDE + over * 2 + kind
            first = starts[owner]
            count = counts[0, owner]
            aligned = first // 16
            turn = first - aligned * 16
            far = turn >= 8
            small = jnp.where(far, turn - 8, turn)
            turn_back = lax.rem(8 - small, 8)
            kept = iota((9, 8, width), 1) < 8 - small
            for at in range(0, capacity, 64):
                window = rows[pl.ds(pl.multiple_of(aligned * 16 + at, 16), 80), :]
                window = window.astype(F32).reshape(10, 8, width)
                window = pltpu.roll(window, turn_back, 1)
                moved = jnp.where(kept, window[:9], window[1:])
                moved = jnp.where(far, moved[1:], moved[:8])
                out[0, at : at + 64, :] = moved.reshape(64, width).astype(BF16)
            base = first // LANES
            shift = first - base * LANES
            got = [labels[pl.ds(base + i, 1), :] for i in range(TAIL + 1)]
            low_part = jnp.concatenate(got[:TAIL], axis=0)
            high_part = jnp.concatenate(got[1:], axis=0)
            back = lax.rem(LANES - shift, LANES)
            low_part = pltpu.roll(low_part, back, 1)
            high_part = pltpu.roll(high_part, back, 1)
            value = jnp.where(lane < LANES - shift, low_part, high_part)
            live = line < count
            high = jnp.where(live, lax.shift_right_logical(value, 7), 64).astype(F32)
            low = jnp.where(live, value & 127, 0).astype(F32)
            out[0, capacity:, :] = jnp.concatenate([high, low], axis=1).astype(BF16)


def pack(slots, send_counts, embeddings, local, capacity):
    per_dev, width = embeddings.shape
    tall = capacity + TAIL
    longest = max(len(c) for _, _, c in slots)

    def spec(length):
        return pl.BlockSpec((1, tall, width), lambda q: (jnp.minimum(q, length - 1), 0, 0))

    many = sum(len(c) for _, _, c in slots)
    return pl.pallas_call(
        functools.partial(pack_body, slots, capacity),
        grid=(longest,),
        out_shape=[jax.ShapeDtypeStruct((len(c), tall, width), BF16) for _, _, c in slots],
        in_specs=[
            pl.BlockSpec(memory_space=pltpu.SMEM),
            pl.BlockSpec(memory_space=pl.ANY),
            pl.BlockSpec(local.shape, lambda q: (0, 0)),
        ],
        out_specs=[spec(len(c)) for _, _, c in slots],
        scratch_shapes=[
            pltpu.VMEM((per_dev + capacity + 16, width), BF16),
            pltpu.VMEM((local.shape[0] + 16, LANES), jnp.int32),
            pltpu.SMEM((send_counts.shape[1],), jnp.int32),
            pltpu.SemaphoreType.DMA,
        ],
        cost_estimate=pl.CostEstimate(
            flops=0,
            bytes_accessed=per_dev * width * 2 + many * tall * width * 2,
            transcendentals=0,
        ),
        compiler_params=pltpu.CompilerParams(vmem_limit_bytes=60 * MIB),
        name="pack_rows",
    )(send_counts, embeddings, local)


def sums_body(sources, capacity, blocks, had, sent, *refs):
    arrived, refs = refs[:sources], refs[sources:]
    had_acc, had_counts = None, None
    if had:
        had_acc, had_counts, refs = refs[0], refs[1], refs[2:]
    if sent:
        out, low_hot, high_hot, onehot, data = refs
        out_counts = None
    else:
        out, out_counts, low_hot, high_hot, onehot, data = refs
    digits = high_hot.shape[0]
    depth = sources * capacity
    part = pl.program_id(1)
    size = onehot.shape[0]

    @pl.when(part == 0)
    def _():
        for s in range(sources):
            tail = arrived[s][0, capacity:, :].astype(F32)
            data[s * capacity : (s + 1) * capacity, :] = arrived[s][0, :capacity, :]
            for i in range(capacity // LANES):
                at = s * capacity + i * LANES
                high = tail[i : i + 1, :LANES]
                low = tail[i : i + 1, LANES : 2 * LANES]
                low_hot[:, at : at + LANES] = jnp.where(
                    iota((LANES, LANES), 0).astype(F32) == low, 1.0, 0.0
                ).astype(BF16)
                high_hot[:, at : at + LANES] = jnp.where(
                    iota((digits, LANES), 0).astype(F32) == high, 1.0, 0.0
                )
        counts = lax.dot_general(
            high_hot[...].astype(BF16),
            low_hot[...],
            (((1,), (1,)), ((), ())),
            preferred_element_type=F32,
        )
        if had_counts is not None:
            counts = counts + had_counts[0]
        if sent:
            tens = jnp.floor(counts / 64.0)
            out[blocks * size :, :] = jnp.concatenate(
                [tens, counts - 64.0 * tens], axis=1
            ).astype(BF16)
        else:
            out_counts[0] = counts

    group = size // LANES
    for h in range(group):
        row = high_hot[pl.ds(pl.multiple_of(part * group, group), group), :][h : h + 1, :]
        row = jnp.broadcast_to(row, (16, depth)).astype(BF16)
        for at in range(0, LANES, 16):
            onehot[h * LANES + at : h * LANES + at + 16, :] = low_hot[at : at + 16, :] * row
    total = jnp.dot(onehot[...], data[...], preferred_element_type=F32)
    if had_acc is not None:
        total = total + had_acc[0]
    if sent:
        out[pl.ds(pl.multiple_of(part * size, size), size), :] = total.astype(BF16)
    else:
        out[0] = total


def line_sums(arrived, capacity, fine_dev, crosses, had=None, send=False):
    width = arrived[0][0].shape[2]
    tall = capacity + TAIL
    sources = len(arrived)
    digits = fine_dev // LANES
    size = fine_dev // 2
    blocks = fine_dev // size
    many = len(crosses)

    def source(lowest):
        at = crosses[0] - lowest
        return pl.BlockSpec((1, tall, width), lambda q, m: (at + q, 0, 0))

    operands = [a for a, _ in arrived]
    in_specs = [source(lowest) for _, lowest in arrived]
    if had is not None:
        acc, counts, lowest = had
        at = crosses[0] - lowest
        operands += [acc, counts]
        in_specs += [
            pl.BlockSpec((1, size, width), lambda q, m: (at + q, m, 0)),
            pl.BlockSpec((1, digits, LANES), lambda q, m: (at + q, 0, 0)),
        ]
    if send:
        out_shape = jax.ShapeDtypeStruct((fine_dev + 16, width), BF16)
        out_specs = pl.BlockSpec((fine_dev + 16, width), lambda q, m: (0, 0))
    else:
        out_shape = (
            jax.ShapeDtypeStruct((many, fine_dev, width), F32),
            jax.ShapeDtypeStruct((many, digits, LANES), F32),
        )
        out_specs = (
            pl.BlockSpec((1, size, width), lambda q, m: (q, m, 0)),
            pl.BlockSpec((1, digits, LANES), lambda q, m: (q, 0, 0)),
        )
    return pl.pallas_call(
        functools.partial(sums_body, sources, capacity, blocks, had is not None, send),
        grid=(many, blocks),
        out_shape=out_shape,
        in_specs=in_specs,
        out_specs=out_specs,
        scratch_shapes=[
            pltpu.VMEM((LANES, sources * capacity), BF16),
            pltpu.VMEM((digits, sources * capacity), F32),
            pltpu.VMEM((size, sources * capacity), BF16),
            pltpu.VMEM((sources * capacity, width), BF16),
        ],
        cost_estimate=pl.CostEstimate(
            flops=2 * many * sources * capacity * fine_dev * width,
            bytes_accessed=many * (sources * tall * width * 2 + fine_dev * width * 8),
            transcendentals=0,
        ),
        compiler_params=pltpu.CompilerParams(vmem_limit_bytes=32 * MIB),
        name="line_sums",
    )(*operands)


def update_body(acc, counts, old, *refs):
    steps = SIDE - 1
    got, tails, new, column = refs[:steps], refs[steps : 2 * steps], refs[-2], refs[-1]
    digits = counts.shape[1]
    part = pl.program_id(0)
    group = old.shape[0] // LANES

    @pl.when(part == 0)
    def _():
        count = counts[0]
        for tail in tails:
            value = tail[...].astype(F32)
            count = count + value[:, :LANES] * 64.0 + value[:, LANES : 2 * LANES]
        tens = jnp.floor(count / 64.0)
        eye = jnp.where(iota((LANES, LANES), 0) == iota((LANES, LANES), 1), 1.0, 0.0)
        turn = lambda a: lax.dot_general(
            eye.astype(BF16), a.astype(BF16), (((1,), (1,)), ((), ())), preferred_element_type=F32
        )
        column[...] = turn(tens) * 64.0 + turn(count - 64.0 * tens)

    for p in range(digits // group):

        @pl.when(part == p)
        def _():
            for h in range(group):
                at = slice(h * LANES, (h + 1) * LANES)
                total = acc[0, at, :] + old[at, :].astype(F32)
                for g in got:
                    total = total + g[at, :].astype(F32)
                count = column[:, p * group + h : p * group + h + 1]
                new[at, :] = (total / (count + 1.0)).astype(BF16)


def update(acc, counts, old_fine, got):
    fine_dev, width = old_fine.shape
    digits = fine_dev // LANES
    size = fine_dev // 4
    return pl.pallas_call(
        update_body,
        grid=(fine_dev // size,),
        out_shape=jax.ShapeDtypeStruct((fine_dev, width), BF16),
        in_specs=[
            pl.BlockSpec((1, size, width), lambda m: (0, m, 0)),
            pl.BlockSpec((1, digits, LANES), lambda m: (0, 0, 0)),
            pl.BlockSpec((size, width), lambda m: (m, 0)),
        ]
        + [pl.BlockSpec((size, width), lambda m: (m, 0))] * len(got)
        + [pl.BlockSpec((16, width), lambda m: (fine_dev // 16, 0))] * len(got),
        out_specs=pl.BlockSpec((size, width), lambda m: (m, 0)),
        scratch_shapes=[pltpu.VMEM((LANES, digits), F32)],
        compiler_params=pltpu.CompilerParams(vmem_limit_bytes=24 * MIB),
        name="new_fine",
    )(acc, counts, old_fine, *got, *got)


def plan_body(coarse_dev, ids, owner_hot, rank_hot, labels):
    peers, fine_dev = owner_hot.shape
    value = ids[...]
    owner = value // coarse_dev
    local = (value - owner * coarse_dev).astype(F32)
    member = jnp.where(iota((peers, fine_dev), 0) == owner, 1.0, 0.0)
    owner_hot[...] = member
    step = 256
    before = jnp.where(iota((step, step), 0) < iota((step, step), 1), 1.0, 0.0).astype(BF16)
    carry = jnp.zeros((peers, 1), F32)
    for at in range(0, fine_dev, step):
        piece = member[:, at : at + step]
        prefix = jnp.dot(piece.astype(BF16), before, preferred_element_type=F32) + carry
        rank = jnp.sum(prefix * piece, axis=0, keepdims=True)
        carry = carry + jnp.sum(piece, axis=1, keepdims=True)
        hot = jnp.where(iota((rank_hot.shape[0], step), 0).astype(F32) == rank, 1.0, 0.0)
        rank_hot[:, at : at + step] = hot.astype(BF16)
    tagged = (member * (local + 1.0)).astype(BF16)
    labels[...] = lax.dot_general(
        tagged, rank_hot[...], (((1,), (1,)), ((), ())), preferred_element_type=F32
    )


def plan(coarse_ids, peers, capacity, coarse_dev):
    fine_dev = coarse_ids.shape[1]
    return pl.pallas_call(
        functools.partial(plan_body, coarse_dev),
        out_shape=(
            jax.ShapeDtypeStruct((peers, fine_dev), F32),
            jax.ShapeDtypeStruct((capacity, fine_dev), BF16),
            jax.ShapeDtypeStruct((peers, capacity), F32),
        ),
        compiler_params=pltpu.CompilerParams(vmem_limit_bytes=24 * MIB),
        name="plan_clusters",
    )(coarse_ids)


def place_body(group, owner_hot, rank_hot, tags, new, out, placement):
    capacity, fine_dev = rank_hot.shape
    for g in range(group):
        row = jnp.broadcast_to(owner_hot[g : g + 1, :], (16, fine_dev)).astype(BF16)
        for at in range(0, capacity, 16):
            top = g * capacity + at
            placement[top : top + 16, :] = rank_hot[at : at + 16, :] * row
    sent = jnp.dot(placement[...], new[...], preferred_element_type=F32).astype(BF16)
    for g in range(group):
        out[g, :capacity, :] = sent[g * capacity : (g + 1) * capacity, :]
        tag = jnp.broadcast_to(tags[g : g + 1, :], (TAIL, capacity))
        out[g, capacity:, :] = jnp.concatenate([tag, tag], axis=1).astype(BF16)


def place(owner_hot, rank_hot, tags, new_fine, group):
    peers, fine_dev = owner_hot.shape
    capacity = rank_hot.shape[0]
    width = new_fine.shape[1]
    whole = lambda a: pl.BlockSpec(a.shape, lambda i: (0, 0))
    return pl.pallas_call(
        functools.partial(place_body, group),
        grid=(peers // group,),
        out_shape=jax.ShapeDtypeStruct((peers, capacity + TAIL, width), BF16),
        in_specs=[
            pl.BlockSpec((group, fine_dev), lambda i: (i, 0)),
            whole(rank_hot),
            pl.BlockSpec((group, capacity), lambda i: (i, 0)),
            whole(new_fine),
        ],
        out_specs=pl.BlockSpec((group, capacity + TAIL, width), lambda i: (i, 0, 0)),
        scratch_shapes=[pltpu.VMEM((group * capacity, fine_dev), BF16)],
        compiler_params=pltpu.CompilerParams(vmem_limit_bytes=24 * MIB),
        name="place_clusters",
    )(owner_hot, rank_hot, tags, new_fine)


def coarse_body(received, old, means, onehot, data):
    peers, tall, _ = received.shape
    capacity = tall - TAIL
    coarse_dev = old.shape[0]
    total = jnp.zeros((coarse_dev, capacity), F32)
    row = iota((coarse_dev, capacity), 0).astype(F32) + 1.0
    for p in range(peers):
        tag = received[p, capacity:, :].astype(F32)[:1, :capacity]
        hot = jnp.where(row == tag, 1.0, 0.0)
        total = total + hot
        onehot[:, p * capacity : (p + 1) * capacity] = hot.astype(BF16)
        data[p * capacity : (p + 1) * capacity, :] = received[p, :capacity, :]
    sums = jnp.dot(onehot[...], data[...], preferred_element_type=F32)
    count = jnp.sum(total, axis=1, keepdims=True)
    means[...] = ((sums + old[...].astype(F32)) / (count + 1.0)).astype(BF16)


def coarse(received, old_coarse):
    peers, tall, width = received.shape
    deep = peers * (tall - TAIL)
    return pl.pallas_call(
        coarse_body,
        out_shape=jax.ShapeDtypeStruct(old_coarse.shape, BF16),
        scratch_shapes=[
            pltpu.VMEM((old_coarse.shape[0], deep), BF16),
            pltpu.VMEM((deep, width), BF16),
        ],
        compiler_params=pltpu.CompilerParams(vmem_limit_bytes=24 * MIB),
        name="coarse_means",
    )(received, old_coarse)


def finish_body(groups, at, *refs):
    pieces, out, full = refs[:groups], refs[groups], refs[groups + 1]
    width = pieces[0].shape[1]
    for step in range(groups):
        place = lax.rem(at[0] + step, groups) * width
        full[:, pl.ds(pl.multiple_of(place, width), width)] = pieces[step][...].astype(F32)
    whole = full[...]
    scale = lax.rsqrt(jnp.mean(whole * whole, axis=1, keepdims=True) + 1e-06)
    out[...] = (whole * scale).astype(BF16)


def finish(at, pieces):
    groups = len(pieces)
    rows, width = pieces[0].shape
    return pl.pallas_call(
        functools.partial(finish_body, groups),
        out_shape=jax.ShapeDtypeStruct((rows, groups * width), BF16),
        in_specs=[pl.BlockSpec(memory_space=pltpu.SMEM)]
        + [pl.BlockSpec(memory_space=pltpu.VMEM)] * groups,
        scratch_shapes=[pltpu.VMEM((rows, groups * width), F32)],
        compiler_params=pltpu.CompilerParams(vmem_limit_bytes=24 * MIB),
        name="coarse_dirs",
    )(at, *pieces)


def exchange(slots):
    return lax.all_to_all(slots, "rows", split_axis=0, concat_axis=0, tiled=True)


def level_step(embeddings, fine_local, send_counts, old_fine, coarse_ids, old_coarse):
    peers = lax.axis_size("rows")
    groups = lax.axis_size("grp")
    per_dev = embeddings.shape[0]
    fine_dev = old_fine.shape[0]
    coarse_dev = old_coarse.shape[0]
    capacity = 2 * per_dev // peers
    capacity_two = 2 * fine_dev // peers
    local = fine_local.reshape(-1, LANES)
    steps = range(1, SIDE)

    def along(slots, step, same_class):
        return lax.ppermute(slots, "rows", line_pairs(step, same_class))

    rows = (send_counts, embeddings, local, capacity)
    sent, own = tuple(steps), (0,)
    order = (2, 1, 3)

    keep = pack([(True, s, sent) for s in order], *rows)
    kept = []
    for s, a in zip(order, keep):
        kept.append(along(a, s, True))
    more = pack(
        [(False, s, sent) for s in order]
        + [(False, 0, own + sent), (True, 0, own + sent)]
        + [(k, s, own) for k in (True, False) for s in order],
        *rows,
    )
    swapped = along(more[3], 0, False)
    given = [along(a, s, False) for s, a in zip(order, more[:3])]
    owner_hot, rank_hot, tags = plan(
        coarse_ids.reshape(1, -1), peers, capacity_two, coarse_dev
    )
    near = [(more[4], 0), (swapped, 0)]
    had = line_sums(near + [(kept[0], 1)], capacity, fine_dev, sent)
    had = line_sums([(a, 1) for a in kept[1:]], capacity, fine_dev, sent, (*had, 1))
    kept_own = [along(a, s, True) for s, a in zip(order, more[5:8])]
    given_own = [along(a, s, False) for s, a in zip(order, more[8:])]
    got = {}
    for cross in order:
        part = line_sums(
            [(a, 1) for a in given], capacity, fine_dev, (cross,), (*had, 1), send=True
        )
        got[cross] = lax.ppermute(part, "rows", cross_pairs(cross))
    acc, counts = line_sums(near + [(a, 0) for a in kept_own + given_own], capacity, fine_dev, own)
    new_fine = update(acc, counts, old_fine, [got[c] for c in steps])

    received = exchange(place(owner_hot, rank_hot, tags, new_fine, 8))
    means = coarse(received, old_coarse)
    pieces = [means]
    for step in range(1, groups):
        back = [((g + step) % groups, g) for g in range(groups)]
        pieces.append(lax.ppermute(means, "grp", back))
    at = lax.axis_index("grp").astype(jnp.int32).reshape(1)
    return (new_fine, finish(at, pieces))


def solution(mesh):
    in_specs = (
        P("rows", "grp"),
        P("rows"),
        P("rows", None),
        P("rows", "grp"),
        P("rows"),
        P("rows", "grp"),
    )
    out_specs = (P("rows", "grp"), P("rows", None))
    return jax.shard_map(
        level_step, mesh=mesh, in_specs=in_specs, out_specs=out_specs, check_vma=False
    )
```

```python
import functools

import jax
import jax.numpy as jnp
from jax import lax
from jax.experimental import pallas as pl
from jax.experimental.pallas import tpu as pltpu
from jax.sharding import PartitionSpec as P


F32 = jnp.float32
BF16 = jnp.bfloat16
LANES = 128
MIB = 1024 * 1024
TAIL = 8
SIDE = 4


def iota(shape, axis):
    return lax.broadcasted_iota(jnp.int32, shape, axis)


def device(x, y, core):
    return (x % SIDE) * 2 * SIDE + (y % SIDE) * 2 + core


CHIPS = [(x, y) for x in range(SIDE) for y in range(SIDE)]


def line_pairs(step, same_class):
    pairs = []
    for x, y in CHIPS:
        for core in range(2):
            kind = core if same_class else 1 - core
            to = device(x + step, y, 0) if kind == 0 else device(x, y + step, 1)
            pairs.append((device(x, y, core), to))
    return pairs


def cross_pairs(step):
    pairs = []
    for x, y in CHIPS:
        pairs.append((device(x, y, 0), device(x, y + step, 0)))
        pairs.append((device(x, y, 1), device(x + step, y, 1)))
    return pairs


def owner_of(kind, step, cross):
    here = lax.axis_index("rows")
    along = lax.rem(here // (2 * SIDE) + jnp.where(kind == 0, step, cross), SIDE)
    over = lax.rem(lax.rem(here // 2, SIDE) + jnp.where(kind == 0, cross, step), SIDE)
    return along * 2 * SIDE + over * 2 + kind


def pack_body(slots, capacity, tagged, counts, emb, local, *rest):
    tags = rest[0] if tagged else None
    rest = rest[1:] if tagged else rest
    outs, (rows, labels, starts, done) = rest[: len(slots)], rest[len(slots) :]
    per_dev, width = emb.shape
    label_rows = local.shape[0]
    owners = counts.shape[1]
    at_step = pl.program_id(0)

    @pl.when(at_step == 0)
    def _():
        fetch = pltpu.make_async_copy(emb, rows.at[:per_dev, :], done)
        fetch.start()

        def add(o, total):
            starts[o] = total
            return total + counts[0, o]

        lax.fori_loop(0, owners, add, 0)
        labels[:label_rows, :] = local[...]
        labels[label_rows:, :] = jnp.zeros((16, LANES), jnp.int32)
        rows[per_dev:, :] = jnp.zeros((capacity + 16, width), BF16)
        fetch.wait()

    core = lax.rem(lax.axis_index("rows"), 2)
    line = iota((TAIL, LANES), 0) * LANES + iota((TAIL, LANES), 1)
    lane = iota((TAIL, LANES), 1)
    for (same_class, step, crosses), out in zip(slots, outs):

        @pl.when(at_step < len(crosses))
        def _():
            cross = at_step + crosses[0]
            kind = core if same_class else 1 - core
            owner = owner_of(kind, step, cross)
            first = starts[owner]
            count = counts[0, owner]
            aligned = first // 16
            turn = first - aligned * 16
            far = turn >= 8
            small = jnp.where(far, turn - 8, turn)
            turn_back = lax.rem(8 - small, 8)
            kept = iota((9, 8, width), 1) < 8 - small
            for at in range(0, capacity, 64):
                window = rows[pl.ds(pl.multiple_of(aligned * 16 + at, 16), 80), :]
                window = window.astype(F32).reshape(10, 8, width)
                window = pltpu.roll(window, turn_back, 1)
                moved = jnp.where(kept, window[:9], window[1:])
                moved = jnp.where(far, moved[1:], moved[:8])
                out[0, at : at + 64, :] = moved.reshape(64, width).astype(BF16)
            base = first // LANES
            shift = first - base * LANES
            got = [labels[pl.ds(base + i, 1), :] for i in range(TAIL + 1)]
            low_part = jnp.concatenate(got[:TAIL], axis=0)
            high_part = jnp.concatenate(got[1:], axis=0)
            back = lax.rem(LANES - shift, LANES)
            low_part = pltpu.roll(low_part, back, 1)
            high_part = pltpu.roll(high_part, back, 1)
            value = jnp.where(lane < LANES - shift, low_part, high_part)
            live = line < count
            high = jnp.where(live, lax.shift_right_logical(value, 7), 64).astype(F32)
            low = jnp.where(live, value & 127, 0).astype(F32)
            if crosses[0] == 0:
                own_tags = [tags[pl.ds(owner_of(kind, step, c), 1), :] for c in range(SIDE)]
                high = jnp.concatenate([high[: TAIL - SIDE]] + own_tags, axis=0)
            out[0, capacity:, :] = jnp.concatenate([high, low], axis=1).astype(BF16)


def pack(slots, send_counts, embeddings, local, capacity, tags=None):
    per_dev, width = embeddings.shape
    tall = capacity + TAIL
    longest = max(len(c) for _, _, c in slots)

    def spec(length):
        return pl.BlockSpec((1, tall, width), lambda q: (jnp.minimum(q, length - 1), 0, 0))

    many = sum(len(c) for _, _, c in slots)
    return pl.pallas_call(
        functools.partial(pack_body, slots, capacity, tags is not None),
        grid=(longest,),
        out_shape=[jax.ShapeDtypeStruct((len(c), tall, width), BF16) for _, _, c in slots],
        in_specs=[
            pl.BlockSpec(memory_space=pltpu.SMEM),
            pl.BlockSpec(memory_space=pl.ANY),
            pl.BlockSpec(local.shape, lambda q: (0, 0)),
        ]
        + ([] if tags is None else [pl.BlockSpec(tags.shape, lambda q: (0, 0))]),
        out_specs=[spec(len(c)) for _, _, c in slots],
        scratch_shapes=[
            pltpu.VMEM((per_dev + capacity + 16, width), BF16),
            pltpu.VMEM((local.shape[0] + 16, LANES), jnp.int32),
            pltpu.SMEM((send_counts.shape[1],), jnp.int32),
            pltpu.SemaphoreType.DMA,
        ],
        cost_estimate=pl.CostEstimate(
            flops=0,
            bytes_accessed=per_dev * width * 2 + many * tall * width * 2,
            transcendentals=0,
        ),
        compiler_params=pltpu.CompilerParams(vmem_limit_bytes=60 * MIB),
        name="pack_rows",
    )(send_counts, embeddings, local, *([] if tags is None else [tags]))


def sums_body(sources, capacity, blocks, had, sent, *refs):
    arrived, refs = refs[:sources], refs[sources:]
    had_acc, had_counts = None, None
    if had:
        had_acc, had_counts, refs = refs[0], refs[1], refs[2:]
    if sent:
        out, low_hot, high_hot, onehot, data = refs
        out_counts = None
    else:
        out, out_counts, low_hot, high_hot, onehot, data = refs
    digits = high_hot.shape[0]
    depth = sources * capacity
    part = pl.program_id(1)
    size = onehot.shape[0]

    @pl.when(part == 0)
    def _():
        for s in range(sources):
            tail = arrived[s][0, capacity:, :].astype(F32)
            data[s * capacity : (s + 1) * capacity, :] = arrived[s][0, :capacity, :]
            for i in range(capacity // LANES):
                at = s * capacity + i * LANES
                high = tail[i : i + 1, :LANES]
                low = tail[i : i + 1, LANES : 2 * LANES]
                low_hot[:, at : at + LANES] = jnp.where(
                    iota((LANES, LANES), 0).astype(F32) == low, 1.0, 0.0
                ).astype(BF16)
                high_hot[:, at : at + LANES] = jnp.where(
                    iota((digits, LANES), 0).astype(F32) == high, 1.0, 0.0
                )
        counts = lax.dot_general(
            high_hot[...].astype(BF16),
            low_hot[...],
            (((1,), (1,)), ((), ())),
            preferred_element_type=F32,
        )
        if had_counts is not None:
            counts = counts + had_counts[0]
        if sent:
            tens = jnp.floor(counts / 64.0)
            out[blocks * size :, :] = jnp.concatenate(
                [tens, counts - 64.0 * tens], axis=1
            ).astype(BF16)
        else:
            out_counts[0] = counts

    group = size // LANES
    for h in range(group):
        row = high_hot[pl.ds(pl.multiple_of(part * group, group), group), :][h : h + 1, :]
        row = jnp.broadcast_to(row, (16, depth)).astype(BF16)
        for at in range(0, LANES, 16):
            onehot[h * LANES + at : h * LANES + at + 16, :] = low_hot[at : at + 16, :] * row
    total = jnp.dot(onehot[...], data[...], preferred_element_type=F32)
    if had_acc is not None:
        total = total + had_acc[0]
    if sent:
        out[pl.ds(pl.multiple_of(part * size, size), size), :] = total.astype(BF16)
    else:
        out[0] = total


def line_sums(arrived, capacity, fine_dev, crosses, had=None, send=False):
    width = arrived[0][0].shape[2]
    tall = capacity + TAIL
    sources = len(arrived)
    digits = fine_dev // LANES
    size = fine_dev // 2
    blocks = fine_dev // size
    many = len(crosses)

    def source(lowest):
        at = crosses[0] - lowest
        return pl.BlockSpec((1, tall, width), lambda q, m: (at + q, 0, 0))

    operands = [a for a, _ in arrived]
    in_specs = [source(lowest) for _, lowest in arrived]
    if had is not None:
        acc, counts, lowest = had
        at = crosses[0] - lowest
        operands += [acc, counts]
        in_specs += [
            pl.BlockSpec((1, size, width), lambda q, m: (at + q, m, 0)),
            pl.BlockSpec((1, digits, LANES), lambda q, m: (at + q, 0, 0)),
        ]
    if send:
        out_shape = jax.ShapeDtypeStruct((fine_dev + 16, width), BF16)
        out_specs = pl.BlockSpec((fine_dev + 16, width), lambda q, m: (0, 0))
    else:
        out_shape = (
            jax.ShapeDtypeStruct((many, fine_dev, width), F32),
            jax.ShapeDtypeStruct((many, digits, LANES), F32),
        )
        out_specs = (
            pl.BlockSpec((1, size, width), lambda q, m: (q, m, 0)),
            pl.BlockSpec((1, digits, LANES), lambda q, m: (q, 0, 0)),
        )
    return pl.pallas_call(
        functools.partial(sums_body, sources, capacity, blocks, had is not None, send),
        grid=(many, blocks),
        out_shape=out_shape,
        in_specs=in_specs,
        out_specs=out_specs,
        scratch_shapes=[
            pltpu.VMEM((LANES, sources * capacity), BF16),
            pltpu.VMEM((digits, sources * capacity), F32),
            pltpu.VMEM((size, sources * capacity), BF16),
            pltpu.VMEM((sources * capacity, width), BF16),
        ],
        cost_estimate=pl.CostEstimate(
            flops=2 * many * sources * capacity * fine_dev * width,
            bytes_accessed=many * (sources * tall * width * 2 + fine_dev * width * 8),
            transcendentals=0,
        ),
        compiler_params=pltpu.CompilerParams(vmem_limit_bytes=(10 + 2 * sources) * MIB),
        name="line_sums",
    )(*operands)


def update_body(acc, counts, old, *refs):
    steps = SIDE - 1
    got, tails, new, column = refs[:steps], refs[steps : 2 * steps], refs[-2], refs[-1]
    digits = counts.shape[1]
    part = pl.program_id(0)
    group = old.shape[0] // LANES

    @pl.when(part == 0)
    def _():
        count = counts[0]
        for tail in tails:
            value = tail[...].astype(F32)
            count = count + value[:, :LANES] * 64.0 + value[:, LANES : 2 * LANES]
        tens = jnp.floor(count / 64.0)
        eye = jnp.where(iota((LANES, LANES), 0) == iota((LANES, LANES), 1), 1.0, 0.0)
        turn = lambda a: lax.dot_general(
            eye.astype(BF16), a.astype(BF16), (((1,), (1,)), ((), ())), preferred_element_type=F32
        )
        column[...] = turn(tens) * 64.0 + turn(count - 64.0 * tens)

    for p in range(digits // group):

        @pl.when(part == p)
        def _():
            for h in range(group):
                at = slice(h * LANES, (h + 1) * LANES)
                total = acc[0, at, :] + old[at, :].astype(F32)
                for g in got:
                    total = total + g[at, :].astype(F32)
                count = column[:, p * group + h : p * group + h + 1]
                new[at, :] = (total / (count + 1.0)).astype(BF16)


def update(acc, counts, old_fine, got):
    fine_dev, width = old_fine.shape
    digits = fine_dev // LANES
    size = fine_dev // 4
    return pl.pallas_call(
        update_body,
        grid=(fine_dev // size,),
        out_shape=jax.ShapeDtypeStruct((fine_dev, width), BF16),
        in_specs=[
            pl.BlockSpec((1, size, width), lambda m: (0, m, 0)),
            pl.BlockSpec((1, digits, LANES), lambda m: (0, 0, 0)),
            pl.BlockSpec((size, width), lambda m: (m, 0)),
        ]
        + [pl.BlockSpec((size, width), lambda m: (m, 0))] * len(got)
        + [pl.BlockSpec((16, width), lambda m: (fine_dev // 16, 0))] * len(got),
        out_specs=pl.BlockSpec((size, width), lambda m: (m, 0)),
        scratch_shapes=[pltpu.VMEM((LANES, digits), F32)],
        compiler_params=pltpu.CompilerParams(vmem_limit_bytes=24 * MIB),
        name="new_fine",
    )(acc, counts, old_fine, *got, *got)


def plan_body(coarse_dev, ids, owner_hot, rank_hot, labels):
    peers, fine_dev = owner_hot.shape
    value = ids[...]
    owner = value // coarse_dev
    local = (value - owner * coarse_dev).astype(F32)
    member = jnp.where(iota((peers, fine_dev), 0) == owner, 1.0, 0.0)
    owner_hot[...] = member
    step = 256
    before = jnp.where(iota((step, step), 0) < iota((step, step), 1), 1.0, 0.0).astype(BF16)
    carry = jnp.zeros((peers, 1), F32)
    for at in range(0, fine_dev, step):
        piece = member[:, at : at + step]
        prefix = jnp.dot(piece.astype(BF16), before, preferred_element_type=F32) + carry
        rank = jnp.sum(prefix * piece, axis=0, keepdims=True)
        carry = carry + jnp.sum(piece, axis=1, keepdims=True)
        hot = jnp.where(iota((rank_hot.shape[0], step), 0).astype(F32) == rank, 1.0, 0.0)
        rank_hot[:, at : at + step] = hot.astype(BF16)
    tagged = (member * (local + 1.0)).astype(BF16)
    labels[...] = lax.dot_general(
        tagged, rank_hot[...], (((1,), (1,)), ((), ())), preferred_element_type=F32
    )


def plan(coarse_ids, peers, capacity, coarse_dev):
    fine_dev = coarse_ids.shape[1]
    return pl.pallas_call(
        functools.partial(plan_body, coarse_dev),
        out_shape=(
            jax.ShapeDtypeStruct((peers, fine_dev), F32),
            jax.ShapeDtypeStruct((capacity, fine_dev), BF16),
            jax.ShapeDtypeStruct((peers, capacity), F32),
        ),
        compiler_params=pltpu.CompilerParams(vmem_limit_bytes=24 * MIB),
        name="plan_clusters",
    )(coarse_ids)


def place_body(slots, owner_hot, rank_hot, new, *refs):
    outs, placement = refs[:-1], refs[-1]
    capacity, fine_dev = rank_hot.shape
    core = lax.rem(lax.axis_index("rows"), 2)
    for (same_class, step), out in zip(slots, outs):
        kind = core if same_class else 1 - core
        for cross in range(SIDE):
            row = owner_hot[pl.ds(owner_of(kind, step, cross), 1), :]
            row = jnp.broadcast_to(row, (16, fine_dev)).astype(BF16)
            for at in range(0, capacity, 16):
                top = cross * capacity + at
                placement[top : top + 16, :] = rank_hot[at : at + 16, :] * row
        sent = jnp.dot(placement[...], new[...], preferred_element_type=F32).astype(BF16)
        for cross in range(SIDE):
            out[cross, :, :] = sent[cross * capacity : (cross + 1) * capacity, :]


def place(slots, owner_hot, rank_hot, new_fine):
    capacity, fine_dev = rank_hot.shape
    width = new_fine.shape[1]
    return pl.pallas_call(
        functools.partial(place_body, slots),
        out_shape=[jax.ShapeDtypeStruct((SIDE, capacity, width), BF16)] * len(slots),
        scratch_shapes=[pltpu.VMEM((SIDE * capacity, fine_dev), BF16)],
        compiler_params=pltpu.CompilerParams(vmem_limit_bytes=24 * MIB),
        cost_estimate=pl.CostEstimate(
            flops=2 * len(slots) * SIDE * capacity * fine_dev * width,
            bytes_accessed=fine_dev * width * 2,
            transcendentals=0,
        ),
        name="place_clusters",
    )(owner_hot, rank_hot, new_fine)


def tag_hot_body(sources, *refs):
    tails, hot, digits = refs[:sources], refs[-2], refs[-1]
    many, coarse_dev, depth = hot.shape
    capacity = depth // sources
    row = iota((coarse_dev, capacity), 0).astype(F32) + 1.0
    for cross in range(many):
        for s in range(sources):
            at = TAIL - SIDE + cross
            tag = tails[s][0].astype(F32)[at : at + 1, :capacity]
            one = jnp.where(row == tag, 1.0, 0.0).astype(BF16)
            hot[cross, :, s * capacity : (s + 1) * capacity] = one
        count = lax.dot_general(
            jnp.ones((8, depth), BF16),
            hot[cross],
            (((1,), (1,)), ((), ())),
            preferred_element_type=F32,
        )
        tens = jnp.floor(count / 64.0)
        digits[cross] = jnp.concatenate([tens, count - 64.0 * tens], axis=0).astype(BF16)


def tag_hot(tagged, capacity, capacity_two, coarse_dev):
    width = tagged[0].shape[2]
    sources = len(tagged)
    return pl.pallas_call(
        functools.partial(tag_hot_body, sources),
        grid=(1,),
        out_shape=(
            jax.ShapeDtypeStruct((SIDE, coarse_dev, sources * capacity_two), BF16),
            jax.ShapeDtypeStruct((SIDE, 16, coarse_dev), BF16),
        ),
        in_specs=[pl.BlockSpec((1, TAIL, width), lambda i: (0, capacity // TAIL, 0))] * sources,
        out_specs=(
            pl.BlockSpec((SIDE, coarse_dev, sources * capacity_two), lambda i: (0, 0, 0)),
            pl.BlockSpec((SIDE, 16, coarse_dev), lambda i: (0, 0, 0)),
        ),
        compiler_params=pltpu.CompilerParams(vmem_limit_bytes=12 * MIB),
        name="tag_hot",
    )(*tagged)


def coarse_sums_body(sources, order, *refs):
    arrived, (hot, digits), outs, data = (
        refs[:sources],
        refs[sources : sources + 2],
        refs[sources + 2 : -1],
        refs[-1],
    )
    capacity = arrived[0].shape[1]
    coarse_dev = hot.shape[1]
    for cross, out in zip(order, outs):
        for s in range(sources):
            data[s * capacity : (s + 1) * capacity, :] = arrived[s][cross]
        total = jnp.dot(hot[cross], data[...], preferred_element_type=F32)
        if cross == 0:
            out[...] = total
        else:
            out[:coarse_dev, :] = total.astype(BF16)
            out[coarse_dev:, :] = digits[cross]


def coarse_sums(arrived, hot, digits, order):
    capacity, width = arrived[0].shape[1:]
    sources = len(arrived)
    coarse_dev = hot.shape[1]
    sent = jax.ShapeDtypeStruct((coarse_dev + 16, width), BF16)
    kept = jax.ShapeDtypeStruct((coarse_dev, width), F32)
    return pl.pallas_call(
        functools.partial(coarse_sums_body, sources, order),
        out_shape=[kept if c == 0 else sent for c in order],
        scratch_shapes=[pltpu.VMEM((sources * capacity, width), BF16)],
        compiler_params=pltpu.CompilerParams(vmem_limit_bytes=16 * MIB),
        name="coarse_sums",
    )(*arrived, hot, digits)


def coarse_body(acc, digits, old, *refs):
    got, means = refs[:-1], refs[-1]
    coarse_dev, _ = acc.shape
    total = acc[...] + old[...].astype(F32)
    tens = digits[0, :8, :].astype(F32)
    ones = digits[0, 8:, :].astype(F32)
    for g in got:
        total = total + g[:coarse_dev, :].astype(F32)
        tens = tens + g[coarse_dev : coarse_dev + 8, :].astype(F32)
        ones = ones + g[coarse_dev + 8 :, :].astype(F32)
    eye = jnp.where(
        iota((coarse_dev, coarse_dev), 0) == iota((coarse_dev, coarse_dev), 1), 1.0, 0.0
    ).astype(BF16)
    turn = lambda a: lax.dot_general(
        eye, a.astype(BF16), (((1,), (1,)), ((), ())), preferred_element_type=F32
    )
    count = turn(tens) * 64.0 + turn(ones)
    means[...] = (total / (count[:, :1] + 1.0)).astype(BF16)


def coarse(acc, digits, old_coarse, got):
    return pl.pallas_call(
        coarse_body,
        out_shape=jax.ShapeDtypeStruct(old_coarse.shape, BF16),
        compiler_params=pltpu.CompilerParams(vmem_limit_bytes=8 * MIB),
        name="coarse_means",
    )(acc, digits, old_coarse, *got)


def finish_body(groups, at, *refs):
    pieces, out, full = refs[:groups], refs[groups], refs[groups + 1]
    width = pieces[0].shape[1]
    for step in range(groups):
        place = lax.rem(at[0] + step, groups) * width
        full[:, pl.ds(pl.multiple_of(place, width), width)] = pieces[step][...].astype(F32)
    whole = full[...]
    scale = lax.rsqrt(jnp.mean(whole * whole, axis=1, keepdims=True) + 1e-06)
    out[...] = (whole * scale).astype(BF16)


def finish(at, pieces):
    groups = len(pieces)
    rows, width = pieces[0].shape
    return pl.pallas_call(
        functools.partial(finish_body, groups),
        out_shape=jax.ShapeDtypeStruct((rows, groups * width), BF16),
        in_specs=[pl.BlockSpec(memory_space=pltpu.SMEM)]
        + [pl.BlockSpec(memory_space=pltpu.VMEM)] * groups,
        scratch_shapes=[pltpu.VMEM((rows, groups * width), F32)],
        compiler_params=pltpu.CompilerParams(vmem_limit_bytes=24 * MIB),
        name="coarse_dirs",
    )(at, *pieces)


def level_step(embeddings, fine_local, send_counts, old_fine, coarse_ids, old_coarse):
    peers = lax.axis_size("rows")
    groups = lax.axis_size("grp")
    per_dev = embeddings.shape[0]
    fine_dev = old_fine.shape[0]
    coarse_dev = old_coarse.shape[0]
    capacity = 2 * per_dev // peers
    capacity_two = 2 * fine_dev // peers
    local = fine_local.reshape(-1, LANES)
    steps = range(1, SIDE)

    def along(slots, step, same_class):
        return lax.ppermute(slots, "rows", line_pairs(step, same_class))

    rows = (send_counts, embeddings, local, capacity)
    sent, own = tuple(steps), (0,)
    order = (2, 1, 3)

    keep = pack([(True, s, sent) for s in order], *rows)
    kept = []
    for s, a in zip(order, keep):
        kept.append(along(a, s, True))
    owner_hot, rank_hot, tags = plan(
        coarse_ids.reshape(1, -1), peers, capacity_two, coarse_dev
    )
    more = pack(
        [(False, s, sent) for s in order]
        + [(False, 0, own + sent), (True, 0, own + sent)]
        + [(k, s, own) for k in (True, False) for s in order],
        *rows,
        tags,
    )
    swapped = along(more[3], 0, False)
    given = [along(a, s, False) for s, a in zip(order, more[:3])]
    near = [(more[4], 0), (swapped, 0)]
    had = line_sums(near + [(kept[0], 1)], capacity, fine_dev, sent)
    had = line_sums([(a, 1) for a in kept[1:]], capacity, fine_dev, sent, (*had, 1))
    kept_own = [along(a, s, True) for s, a in zip(order, more[5:8])]
    given_own = [along(a, s, False) for s, a in zip(order, more[8:])]
    got = {}
    for cross in order:
        part = line_sums(
            [(a, 1) for a in given], capacity, fine_dev, (cross,), (*had, 1), send=True
        )
        got[cross] = lax.ppermute(part, "rows", cross_pairs(cross))
    acc, counts = line_sums(near + [(a, 0) for a in kept_own + given_own], capacity, fine_dev, own)
    hot, digits = tag_hot(
        [more[4], swapped] + kept_own + given_own, capacity, capacity_two, coarse_dev
    )
    new_fine = update(acc, counts, old_fine, [got[c] for c in steps])

    keep = place([(True, s) for s in order], owner_hot, rank_hot, new_fine)
    arrived = []
    for s, a in zip(order, keep):
        arrived.append(along(a, s, True))
    give = place(
        [(False, s) for s in order] + [(False, 0), (True, 0)], owner_hot, rank_hot, new_fine
    )
    for s, a in zip(order, give):
        arrived.append(along(a, s, False))
    arrived = [give[4], along(give[3], 0, False)] + arrived
    *sent_sums, acc = coarse_sums(arrived, hot, digits, order + own)
    got = []
    for cross, part in zip(order, sent_sums):
        got.append(lax.ppermute(part, "rows", cross_pairs(cross)))
    means = coarse(acc, digits, old_coarse, got)
    pieces = [means]
    for step in range(1, groups):
        back = [((g + step) % groups, g) for g in range(groups)]
        pieces.append(lax.ppermute(means, "grp", back))
    at = lax.axis_index("grp").astype(jnp.int32).reshape(1)
    return (new_fine, finish(at, pieces))


def solution(mesh):
    in_specs = (
        P("rows", "grp"),
        P("rows"),
        P("rows", None),
        P("rows", "grp"),
        P("rows"),
        P("rows", "grp"),
    )
    out_specs = (P("rows", "grp"), P("rows", None))
    return jax.shard_map(
        level_step, mesh=mesh, in_specs=in_specs, out_specs=out_specs, check_vma=False
    )
```

```python
import functools

import jax
import jax.numpy as jnp
from jax import lax
from jax.experimental import pallas as pl
from jax.experimental.pallas import tpu as pltpu
from jax.sharding import PartitionSpec as P


F32 = jnp.float32
BF16 = jnp.bfloat16
LANES = 128
MIB = 1024 * 1024
TAIL = 8
SIDE = 4


def iota(shape, axis):
    return lax.broadcasted_iota(jnp.int32, shape, axis)


def device(x, y, core):
    return (x % SIDE) * 2 * SIDE + (y % SIDE) * 2 + core


CHIPS = [(x, y) for x in range(SIDE) for y in range(SIDE)]


def line_pairs(step, same_class):
    pairs = []
    for x, y in CHIPS:
        for core in range(2):
            kind = core if same_class else 1 - core
            to = device(x + step, y, 0) if kind == 0 else device(x, y + step, 1)
            pairs.append((device(x, y, core), to))
    return pairs


def cross_pairs(step):
    pairs = []
    for x, y in CHIPS:
        pairs.append((device(x, y, 0), device(x, y + step, 0)))
        pairs.append((device(x, y, 1), device(x + step, y, 1)))
    return pairs


def owner_of(kind, step, cross):
    here = lax.axis_index("rows")
    along = lax.rem(here // (2 * SIDE) + jnp.where(kind == 0, step, cross), SIDE)
    over = lax.rem(lax.rem(here // 2, SIDE) + jnp.where(kind == 0, cross, step), SIDE)
    return along * 2 * SIDE + over * 2 + kind


def pack_body(slots, capacity, tagged, counts, emb, local, *rest):
    tags = rest[0] if tagged else None
    rest = rest[1:] if tagged else rest
    outs, (windows, labels, starts, done) = rest[: len(slots)], rest[len(slots) :]
    per_dev, width = emb.shape
    span = capacity + 16
    label_rows = local.shape[0]
    owners = counts.shape[1]
    at_step = pl.program_id(0)
    core = lax.rem(lax.axis_index("rows"), 2)

    def fetch(at, cross, base):
        low = jnp.minimum(base, per_dev - span)
        return pltpu.make_async_copy(
            emb.at[pl.ds(pl.multiple_of(low, 16), span), :],
            windows.at[at, cross, :span, :],
            done.at[at, cross],
        )

    @pl.when(at_step == 0)
    def _():
        def add(o, total):
            starts[o] = total
            return total + counts[0, o]

        lax.fori_loop(0, owners, add, 0)
        for cross in range(max(len(c) for _, _, c in slots)):
            for at, (same_class, step, crosses) in enumerate(slots):
                if cross < len(crosses):
                    kind = core if same_class else 1 - core
                    first = starts[owner_of(kind, step, crosses[cross])]
                    fetch(at, cross, first // 16 * 16).start()
        labels[:label_rows, :] = local[...]
        labels[label_rows:, :] = jnp.zeros((16, LANES), jnp.int32)
        for at, (_, _, crosses) in enumerate(slots):
            for cross in range(len(crosses)):
                windows[at, cross, span:, :] = jnp.zeros((80, width), BF16)

    line = iota((TAIL, LANES), 0) * LANES + iota((TAIL, LANES), 1)
    lane = iota((TAIL, LANES), 1)
    for at_slot, ((same_class, step, crosses), out) in enumerate(zip(slots, outs)):

        @pl.when(at_step < len(crosses))
        def _():
            cross = at_step + crosses[0]
            kind = core if same_class else 1 - core
            owner = owner_of(kind, step, cross)
            first = starts[owner]
            count = counts[0, owner]
            base16 = first // 16 * 16
            turn = first - base16
            far = turn >= 8
            small = jnp.where(far, turn - 8, turn)
            turn_back = lax.rem(8 - small, 8)
            kept = iota((9, 8, width), 1) < 8 - small
            behind = base16 - jnp.minimum(base16, per_dev - span)
            fetch(at_slot, at_step, base16).wait()
            for at in range(0, capacity, 64):
                top = pl.multiple_of(jnp.minimum(behind + at, span), 16)
                window = windows[at_slot, at_step, pl.ds(top, 80), :]
                window = window.astype(F32).reshape(10, 8, width)
                window = pltpu.roll(window, turn_back, 1)
                moved = jnp.where(kept, window[:9], window[1:])
                moved = jnp.where(far, moved[1:], moved[:8])
                out[0, at : at + 64, :] = moved.reshape(64, width).astype(BF16)
            base = first // LANES
            shift = first - base * LANES
            got = [labels[pl.ds(base + i, 1), :] for i in range(TAIL + 1)]
            low_part = jnp.concatenate(got[:TAIL], axis=0)
            high_part = jnp.concatenate(got[1:], axis=0)
            back = lax.rem(LANES - shift, LANES)
            low_part = pltpu.roll(low_part, back, 1)
            high_part = pltpu.roll(high_part, back, 1)
            value = jnp.where(lane < LANES - shift, low_part, high_part)
            live = line < count
            high = jnp.where(live, lax.shift_right_logical(value, 7), 64).astype(F32)
            low = jnp.where(live, value & 127, 0).astype(F32)
            if crosses[0] == 0:
                own_tags = [tags[pl.ds(owner_of(kind, step, c), 1), :] for c in range(SIDE)]
                high = jnp.concatenate([high[: TAIL - SIDE]] + own_tags, axis=0)
            out[0, capacity:, :] = jnp.concatenate([high, low], axis=1).astype(BF16)


def pack(slots, send_counts, embeddings, local, capacity, tags=None, limit=None):
    _, width = embeddings.shape
    tall = capacity + TAIL
    longest = max(len(c) for _, _, c in slots)

    def spec(length):
        return pl.BlockSpec((1, tall, width), lambda q: (jnp.minimum(q, length - 1), 0, 0))

    many = sum(len(c) for _, _, c in slots)
    held = len(slots) * longest * (capacity + 96) * width * 2 + len(slots) * 2 * tall * width * 2
    return pl.pallas_call(
        functools.partial(pack_body, slots, capacity, tags is not None),
        grid=(longest,),
        out_shape=[jax.ShapeDtypeStruct((len(c), tall, width), BF16) for _, _, c in slots],
        in_specs=[
            pl.BlockSpec(memory_space=pltpu.SMEM),
            pl.BlockSpec(memory_space=pltpu.HBM),
            pl.BlockSpec(local.shape, lambda q: (0, 0)),
        ]
        + ([] if tags is None else [pl.BlockSpec(tags.shape, lambda q: (0, 0))]),
        out_specs=[spec(len(c)) for _, _, c in slots],
        scratch_shapes=[
            pltpu.VMEM((len(slots), longest, capacity + 96, width), BF16),
            pltpu.VMEM((local.shape[0] + 16, LANES), jnp.int32),
            pltpu.SMEM((send_counts.shape[1],), jnp.int32),
            pltpu.SemaphoreType.DMA((len(slots), longest)),
        ],
        compiler_params=pltpu.CompilerParams(vmem_limit_bytes=limit or held + 6 * MIB),
        cost_estimate=pl.CostEstimate(
            flops=0,
            bytes_accessed=2 * many * tall * width * 2,
            transcendentals=0,
        ),
        name="pack_rows",
    )(send_counts, embeddings, local, *([] if tags is None else [tags]))


def sums_body(sources, capacity, blocks, had, sent, *refs):
    arrived, refs = refs[:sources], refs[sources:]
    had_acc, had_counts = None, None
    if had:
        had_acc, had_counts, refs = refs[0], refs[1], refs[2:]
    if sent:
        out, low_hot, high_hot, onehot, data = refs
        out_counts = None
    else:
        out, out_counts, low_hot, high_hot, onehot, data = refs
    digits = high_hot.shape[0]
    depth = sources * capacity
    part = pl.program_id(1)
    size = onehot.shape[0]

    @pl.when(part == 0)
    def _():
        for s in range(sources):
            tail = arrived[s][0, capacity:, :].astype(F32)
            data[s * capacity : (s + 1) * capacity, :] = arrived[s][0, :capacity, :]
            for i in range(capacity // LANES):
                at = s * capacity + i * LANES
                high = tail[i : i + 1, :LANES]
                low = tail[i : i + 1, LANES : 2 * LANES]
                low_hot[:, at : at + LANES] = jnp.where(
                    iota((LANES, LANES), 0).astype(F32) == low, 1.0, 0.0
                ).astype(BF16)
                high_hot[:, at : at + LANES] = jnp.where(
                    iota((digits, LANES), 0).astype(F32) == high, 1.0, 0.0
                )
        counts = lax.dot_general(
            high_hot[...].astype(BF16),
            low_hot[...],
            (((1,), (1,)), ((), ())),
            preferred_element_type=F32,
        )
        if had_counts is not None:
            counts = counts + had_counts[0]
        if sent:
            tens = jnp.floor(counts / 64.0)
            out[blocks * size :, :] = jnp.concatenate(
                [tens, counts - 64.0 * tens], axis=1
            ).astype(BF16)
        else:
            out_counts[0] = counts

    group = size // LANES
    for h in range(group):
        row = high_hot[pl.ds(pl.multiple_of(part * group, group), group), :][h : h + 1, :]
        row = jnp.broadcast_to(row, (16, depth)).astype(BF16)
        for at in range(0, LANES, 16):
            onehot[h * LANES + at : h * LANES + at + 16, :] = low_hot[at : at + 16, :] * row
    total = jnp.dot(onehot[...], data[...], preferred_element_type=F32)
    if had_acc is not None:
        total = total + had_acc[0]
    if sent:
        out[pl.ds(pl.multiple_of(part * size, size), size), :] = total.astype(BF16)
    else:
        out[0] = total


def line_sums(arrived, capacity, fine_dev, crosses, had=None, send=False):
    width = arrived[0][0].shape[2]
    tall = capacity + TAIL
    sources = len(arrived)
    digits = fine_dev // LANES
    size = fine_dev // 2
    blocks = fine_dev // size
    many = len(crosses)

    def source(lowest):
        at = crosses[0] - lowest
        return pl.BlockSpec((1, tall, width), lambda q, m: (at + q, 0, 0))

    operands = [a for a, _ in arrived]
    in_specs = [source(lowest) for _, lowest in arrived]
    if had is not None:
        acc, counts, lowest = had
        at = crosses[0] - lowest
        operands += [acc, counts]
        in_specs += [
            pl.BlockSpec((1, size, width), lambda q, m: (at + q, m, 0)),
            pl.BlockSpec((1, digits, LANES), lambda q, m: (at + q, 0, 0)),
        ]
    if send:
        out_shape = jax.ShapeDtypeStruct((fine_dev + 16, width), BF16)
        out_specs = pl.BlockSpec((fine_dev + 16, width), lambda q, m: (0, 0))
    else:
        out_shape = (
            jax.ShapeDtypeStruct((many, fine_dev, width), F32),
            jax.ShapeDtypeStruct((many, digits, LANES), F32),
        )
        out_specs = (
            pl.BlockSpec((1, size, width), lambda q, m: (q, m, 0)),
            pl.BlockSpec((1, digits, LANES), lambda q, m: (q, 0, 0)),
        )
    return pl.pallas_call(
        functools.partial(sums_body, sources, capacity, blocks, had is not None, send),
        grid=(many, blocks),
        out_shape=out_shape,
        in_specs=in_specs,
        out_specs=out_specs,
        scratch_shapes=[
            pltpu.VMEM((LANES, sources * capacity), BF16),
            pltpu.VMEM((digits, sources * capacity), F32),
            pltpu.VMEM((size, sources * capacity), BF16),
            pltpu.VMEM((sources * capacity, width), BF16),
        ],
        cost_estimate=pl.CostEstimate(
            flops=2 * many * sources * capacity * fine_dev * width,
            bytes_accessed=many * (sources * tall * width * 2 + fine_dev * width * 8),
            transcendentals=0,
        ),
        compiler_params=pltpu.CompilerParams(vmem_limit_bytes=(10 + 2 * sources) * MIB),
        name="line_sums",
    )(*operands)


def update_body(slots, acc, counts, old, owner_hot, rank_hot, *refs):
    steps = SIDE - 1
    got, tails, refs = refs[:steps], refs[steps : 2 * steps], refs[2 * steps :]
    new, whole, outs, (column, placement) = refs[0], refs[1], refs[2:-2], refs[-2:]
    digits = counts.shape[1]
    part = pl.program_id(0)
    size = old.shape[0]
    group = size // LANES

    @pl.when(part == 0)
    def _():
        count = counts[0]
        for tail in tails:
            value = tail[...].astype(F32)
            count = count + value[:, :LANES] * 64.0 + value[:, LANES : 2 * LANES]
        tens = jnp.floor(count / 64.0)
        eye = jnp.where(iota((LANES, LANES), 0) == iota((LANES, LANES), 1), 1.0, 0.0)
        turn = lambda a: lax.dot_general(
            eye.astype(BF16), a.astype(BF16), (((1,), (1,)), ((), ())), preferred_element_type=F32
        )
        column[...] = turn(tens) * 64.0 + turn(count - 64.0 * tens)

    for p in range(digits // group):

        @pl.when(part == p)
        def _():
            for h in range(group):
                at = slice(h * LANES, (h + 1) * LANES)
                total = acc[0, at, :] + old[at, :].astype(F32)
                for g in got:
                    total = total + g[at, :].astype(F32)
                count = column[:, p * group + h : p * group + h + 1]
                fresh = (total / (count + 1.0)).astype(BF16)
                new[at, :] = fresh
                whole[p * size + h * LANES : p * size + (h + 1) * LANES, :] = fresh

    @pl.when(part == pl.num_programs(0) - 1)
    def _():
        place_body(slots, owner_hot, rank_hot, whole, *outs, placement)


def update(acc, counts, old_fine, got, slots, owner_hot, rank_hot):
    fine_dev, width = old_fine.shape
    capacity = rank_hot.shape[0]
    digits = fine_dev // LANES
    size = fine_dev // 4
    fixed = lambda a: pl.BlockSpec(a.shape, lambda m: (0, 0))
    return pl.pallas_call(
        functools.partial(update_body, slots),
        grid=(fine_dev // size,),
        out_shape=[jax.ShapeDtypeStruct((fine_dev, width), BF16)] * 2
        + [jax.ShapeDtypeStruct((SIDE, capacity, width), BF16)] * len(slots),
        in_specs=[
            pl.BlockSpec((1, size, width), lambda m: (0, m, 0)),
            pl.BlockSpec((1, digits, LANES), lambda m: (0, 0, 0)),
            pl.BlockSpec((size, width), lambda m: (m, 0)),
            fixed(owner_hot),
            fixed(rank_hot),
        ]
        + [pl.BlockSpec((size, width), lambda m: (m, 0))] * len(got)
        + [pl.BlockSpec((16, width), lambda m: (fine_dev // 16, 0))] * len(got),
        out_specs=[pl.BlockSpec((size, width), lambda m: (m, 0)), fixed(old_fine)]
        + [pl.BlockSpec((SIDE, capacity, width), lambda m: (0, 0, 0))] * len(slots),
        scratch_shapes=[
            pltpu.VMEM((LANES, digits), F32),
            pltpu.VMEM((SIDE * capacity, fine_dev), BF16),
        ],
        compiler_params=pltpu.CompilerParams(vmem_limit_bytes=24 * MIB),
        name="new_fine",
    )(acc, counts, old_fine, owner_hot, rank_hot, *got, *got)


def plan_body(coarse_dev, ids, owner_hot, rank_hot, labels):
    peers, fine_dev = owner_hot.shape
    value = ids[...]
    owner = value // coarse_dev
    local = (value - owner * coarse_dev).astype(F32)
    member = jnp.where(iota((peers, fine_dev), 0) == owner, 1.0, 0.0)
    owner_hot[...] = member
    step = 256
    before = jnp.where(iota((step, step), 0) < iota((step, step), 1), 1.0, 0.0).astype(BF16)
    carry = jnp.zeros((peers, 1), F32)
    for at in range(0, fine_dev, step):
        piece = member[:, at : at + step]
        prefix = jnp.dot(piece.astype(BF16), before, preferred_element_type=F32) + carry
        rank = jnp.sum(prefix * piece, axis=0, keepdims=True)
        carry = carry + jnp.sum(piece, axis=1, keepdims=True)
        hot = jnp.where(iota((rank_hot.shape[0], step), 0).astype(F32) == rank, 1.0, 0.0)
        rank_hot[:, at : at + step] = hot.astype(BF16)
    tagged = (member * (local + 1.0)).astype(BF16)
    labels[...] = lax.dot_general(
        tagged, rank_hot[...], (((1,), (1,)), ((), ())), preferred_element_type=F32
    )


def plan(coarse_ids, peers, capacity, coarse_dev):
    fine_dev = coarse_ids.shape[1]
    return pl.pallas_call(
        functools.partial(plan_body, coarse_dev),
        out_shape=(
            jax.ShapeDtypeStruct((peers, fine_dev), F32),
            jax.ShapeDtypeStruct((capacity, fine_dev), BF16),
            jax.ShapeDtypeStruct((peers, capacity), F32),
        ),
        compiler_params=pltpu.CompilerParams(vmem_limit_bytes=24 * MIB),
        name="plan_clusters",
    )(coarse_ids)


def place_body(slots, owner_hot, rank_hot, new, *refs):
    outs, placement = refs[:-1], refs[-1]
    capacity, fine_dev = rank_hot.shape
    core = lax.rem(lax.axis_index("rows"), 2)
    for (same_class, step), out in zip(slots, outs):
        kind = core if same_class else 1 - core
        for cross in range(SIDE):
            row = owner_hot[pl.ds(owner_of(kind, step, cross), 1), :]
            row = jnp.broadcast_to(row, (16, fine_dev)).astype(BF16)
            for at in range(0, capacity, 16):
                top = cross * capacity + at
                placement[top : top + 16, :] = rank_hot[at : at + 16, :] * row
        sent = jnp.dot(placement[...], new[...], preferred_element_type=F32).astype(BF16)
        for cross in range(SIDE):
            out[cross, :, :] = sent[cross * capacity : (cross + 1) * capacity, :]


def place(slots, owner_hot, rank_hot, new_fine):
    capacity, fine_dev = rank_hot.shape
    width = new_fine.shape[1]
    return pl.pallas_call(
        functools.partial(place_body, slots),
        out_shape=[jax.ShapeDtypeStruct((SIDE, capacity, width), BF16)] * len(slots),
        scratch_shapes=[pltpu.VMEM((SIDE * capacity, fine_dev), BF16)],
        compiler_params=pltpu.CompilerParams(vmem_limit_bytes=24 * MIB),
        cost_estimate=pl.CostEstimate(
            flops=2 * len(slots) * SIDE * capacity * fine_dev * width,
            bytes_accessed=fine_dev * width * 2,
            transcendentals=0,
        ),
        name="place_clusters",
    )(owner_hot, rank_hot, new_fine)


def tag_hot_body(sources, *refs):
    tails, hot, digits = refs[:sources], refs[-2], refs[-1]
    many, coarse_dev, depth = hot.shape
    capacity = depth // sources
    row = iota((coarse_dev, capacity), 0).astype(F32) + 1.0
    for cross in range(many):
        for s in range(sources):
            at = TAIL - SIDE + cross
            tag = tails[s][0].astype(F32)[at : at + 1, :capacity]
            one = jnp.where(row == tag, 1.0, 0.0).astype(BF16)
            hot[cross, :, s * capacity : (s + 1) * capacity] = one
        count = lax.dot_general(
            jnp.ones((8, depth), BF16),
            hot[cross],
            (((1,), (1,)), ((), ())),
            preferred_element_type=F32,
        )
        tens = jnp.floor(count / 64.0)
        digits[cross] = jnp.concatenate([tens, count - 64.0 * tens], axis=0).astype(BF16)


def tag_hot(tagged, capacity, capacity_two, coarse_dev):
    width = tagged[0].shape[2]
    sources = len(tagged)
    return pl.pallas_call(
        functools.partial(tag_hot_body, sources),
        grid=(1,),
        out_shape=(
            jax.ShapeDtypeStruct((SIDE, coarse_dev, sources * capacity_two), BF16),
            jax.ShapeDtypeStruct((SIDE, 16, coarse_dev), BF16),
        ),
        in_specs=[pl.BlockSpec((1, TAIL, width), lambda i: (0, capacity // TAIL, 0))] * sources,
        out_specs=(
            pl.BlockSpec((SIDE, coarse_dev, sources * capacity_two), lambda i: (0, 0, 0)),
            pl.BlockSpec((SIDE, 16, coarse_dev), lambda i: (0, 0, 0)),
        ),
        compiler_params=pltpu.CompilerParams(vmem_limit_bytes=12 * MIB),
        name="tag_hot",
    )(*tagged)


def coarse_sums_body(sources, order, *refs):
    arrived, (hot, digits), outs, data = (
        refs[:sources],
        refs[sources : sources + 2],
        refs[sources + 2 : -1],
        refs[-1],
    )
    capacity = arrived[0].shape[1]
    coarse_dev = hot.shape[1]
    for cross, out in zip(order, outs):
        for s in range(sources):
            data[s * capacity : (s + 1) * capacity, :] = arrived[s][cross]
        total = jnp.dot(hot[cross], data[...], preferred_element_type=F32)
        if cross == 0:
            out[...] = total
        else:
            out[:coarse_dev, :] = total.astype(BF16)
            out[coarse_dev:, :] = digits[cross]


def coarse_sums(arrived, hot, digits, order):
    capacity, width = arrived[0].shape[1:]
    sources = len(arrived)
    coarse_dev = hot.shape[1]
    sent = jax.ShapeDtypeStruct((coarse_dev + 16, width), BF16)
    kept = jax.ShapeDtypeStruct((coarse_dev, width), F32)
    return pl.pallas_call(
        functools.partial(coarse_sums_body, sources, order),
        out_shape=[kept if c == 0 else sent for c in order],
        scratch_shapes=[pltpu.VMEM((sources * capacity, width), BF16)],
        compiler_params=pltpu.CompilerParams(vmem_limit_bytes=16 * MIB),
        name="coarse_sums",
    )(*arrived, hot, digits)


def coarse_body(acc, digits, old, *refs):
    got, means = refs[:-1], refs[-1]
    coarse_dev, _ = acc.shape
    total = acc[...] + old[...].astype(F32)
    tens = digits[0, :8, :].astype(F32)
    ones = digits[0, 8:, :].astype(F32)
    for g in got:
        total = total + g[:coarse_dev, :].astype(F32)
        tens = tens + g[coarse_dev : coarse_dev + 8, :].astype(F32)
        ones = ones + g[coarse_dev + 8 :, :].astype(F32)
    eye = jnp.where(
        iota((coarse_dev, coarse_dev), 0) == iota((coarse_dev, coarse_dev), 1), 1.0, 0.0
    ).astype(BF16)
    turn = lambda a: lax.dot_general(
        eye, a.astype(BF16), (((1,), (1,)), ((), ())), preferred_element_type=F32
    )
    count = turn(tens) * 64.0 + turn(ones)
    means[...] = (total / (count[:, :1] + 1.0)).astype(BF16)


def coarse(acc, digits, old_coarse, got):
    return pl.pallas_call(
        coarse_body,
        out_shape=jax.ShapeDtypeStruct(old_coarse.shape, BF16),
        compiler_params=pltpu.CompilerParams(vmem_limit_bytes=8 * MIB),
        name="coarse_means",
    )(acc, digits, old_coarse, *got)


def finish_body(groups, at, *refs):
    pieces, out, full = refs[:groups], refs[groups], refs[groups + 1]
    width = pieces[0].shape[1]
    for step in range(groups):
        place = lax.rem(at[0] + step, groups) * width
        full[:, pl.ds(pl.multiple_of(place, width), width)] = pieces[step][...].astype(F32)
    whole = full[...]
    scale = lax.rsqrt(jnp.mean(whole * whole, axis=1, keepdims=True) + 1e-06)
    out[...] = (whole * scale).astype(BF16)


def finish(at, pieces):
    groups = len(pieces)
    rows, width = pieces[0].shape
    return pl.pallas_call(
        functools.partial(finish_body, groups),
        out_shape=jax.ShapeDtypeStruct((rows, groups * width), BF16),
        in_specs=[pl.BlockSpec(memory_space=pltpu.SMEM)]
        + [pl.BlockSpec(memory_space=pltpu.VMEM)] * groups,
        scratch_shapes=[pltpu.VMEM((rows, groups * width), F32)],
        compiler_params=pltpu.CompilerParams(vmem_limit_bytes=24 * MIB),
        name="coarse_dirs",
    )(at, *pieces)


def level_step(embeddings, fine_local, send_counts, old_fine, coarse_ids, old_coarse):
    peers = lax.axis_size("rows")
    groups = lax.axis_size("grp")
    per_dev = embeddings.shape[0]
    fine_dev = old_fine.shape[0]
    coarse_dev = old_coarse.shape[0]
    capacity = 2 * per_dev // peers
    capacity_two = 2 * fine_dev // peers
    local = fine_local.reshape(-1, LANES)
    steps = range(1, SIDE)

    def along(slots, step, same_class):
        return lax.ppermute(slots, "rows", line_pairs(step, same_class))

    rows = (send_counts, embeddings, local, capacity)
    sent, own = tuple(steps), (0,)
    order = (2, 1, 3)

    kept = []
    for part, group in (("far", order[:1]), ("near", order[1:])):
        limit = 60 * MIB if part == "far" else None
        keep = pack([(True, s, sent) for s in group], *rows, limit=limit)
        for s, a in zip(group, keep):
            kept.append(along(a, s, True))
    owner_hot, rank_hot, tags = plan(
        coarse_ids.reshape(1, -1), peers, capacity_two, coarse_dev
    )
    more = pack(
        [(False, s, sent) for s in order]
        + [(False, 0, own + sent), (True, 0, own + sent)]
        + [(k, s, own) for k in (True, False) for s in order],
        *rows,
        tags,
    )
    swapped = along(more[3], 0, False)
    given = [along(a, s, False) for s, a in zip(order, more[:3])]
    near = [(more[4], 0), (swapped, 0)]
    had = line_sums(near + [(kept[0], 1)], capacity, fine_dev, sent)
    had = line_sums([(a, 1) for a in kept[1:]], capacity, fine_dev, sent, (*had, 1))
    kept_own = [along(a, s, True) for s, a in zip(order, more[5:8])]
    given_own = [along(a, s, False) for s, a in zip(order, more[8:])]
    got = {}
    for cross in order:
        part = line_sums(
            [(a, 1) for a in given], capacity, fine_dev, (cross,), (*had, 1), send=True
        )
        got[cross] = lax.ppermute(part, "rows", cross_pairs(cross))
    acc, counts = line_sums(near + [(a, 0) for a in kept_own + given_own], capacity, fine_dev, own)
    hot, digits = tag_hot(
        [more[4], swapped] + kept_own + given_own, capacity, capacity_two, coarse_dev
    )
    new_fine, near_fine, *keep = update(
        acc,
        counts,
        old_fine,
        [got[c] for c in steps],
        [(True, s) for s in order],
        owner_hot,
        rank_hot,
    )
    arrived = []
    for s, a in zip(order, keep):
        arrived.append(along(a, s, True))
    give = place(
        [(False, s) for s in order] + [(False, 0), (True, 0)], owner_hot, rank_hot, near_fine
    )
    for s, a in zip(order, give):
        arrived.append(along(a, s, False))
    arrived = [give[4], along(give[3], 0, False)] + arrived
    *sent_sums, acc = coarse_sums(arrived, hot, digits, order + own)
    got = []
    for cross, part in zip(order, sent_sums):
        got.append(lax.ppermute(part, "rows", cross_pairs(cross)))
    means = coarse(acc, digits, old_coarse, got)
    pieces = [means]
    for step in range(1, groups):
        back = [((g + step) % groups, g) for g in range(groups)]
        pieces.append(lax.ppermute(means, "grp", back))
    at = lax.axis_index("grp").astype(jnp.int32).reshape(1)
    return (new_fine, finish(at, pieces))


def solution(mesh):
    in_specs = (
        P("rows", "grp"),
        P("rows"),
        P("rows", None),
        P("rows", "grp"),
        P("rows"),
        P("rows", "grp"),
    )
    out_specs = (P("rows", "grp"), P("rows", None))
    return jax.shard_map(
        level_step, mesh=mesh, in_specs=in_specs, out_specs=out_specs, check_vma=False
    )
```

```python
import functools

import jax
import jax.numpy as jnp
from jax import lax
from jax.experimental import pallas as pl
from jax.experimental.pallas import tpu as pltpu
from jax.sharding import PartitionSpec as P


F32 = jnp.float32
BF16 = jnp.bfloat16
LANES = 128
MIB = 1024 * 1024
TAIL = 8
SIDE = 4


def iota(shape, axis):
    return lax.broadcasted_iota(jnp.int32, shape, axis)


def device(x, y, core):
    return (x % SIDE) * 2 * SIDE + (y % SIDE) * 2 + core


CHIPS = [(x, y) for x in range(SIDE) for y in range(SIDE)]


def line_pairs(step, same_class):
    pairs = []
    for x, y in CHIPS:
        for core in range(2):
            kind = core if same_class else 1 - core
            to = device(x + step, y, 0) if kind == 0 else device(x, y + step, 1)
            pairs.append((device(x, y, core), to))
    return pairs


def cross_pairs(step):
    pairs = []
    for x, y in CHIPS:
        pairs.append((device(x, y, 0), device(x, y + step, 0)))
        pairs.append((device(x, y, 1), device(x + step, y, 1)))
    return pairs


def owner_of(kind, step, cross):
    here = lax.axis_index("rows")
    along = lax.rem(here // (2 * SIDE) + jnp.where(kind == 0, step, cross), SIDE)
    over = lax.rem(lax.rem(here // 2, SIDE) + jnp.where(kind == 0, cross, step), SIDE)
    return along * 2 * SIDE + over * 2 + kind


def pack_body(slots, capacity, tagged, counts, emb, local, *rest):
    tags = rest[0] if tagged else None
    rest = rest[1:] if tagged else rest
    outs, (windows, labels, starts, done, arrived) = rest[: len(slots)], rest[len(slots) :]
    per_dev, width = emb.shape
    span = capacity + 16
    label_rows = local.shape[0]
    owners = counts.shape[1]
    at_step = pl.program_id(0)
    core = lax.rem(lax.axis_index("rows"), 2)

    def fetch(at, cross, base):
        low = jnp.minimum(base, per_dev - span)
        return pltpu.make_async_copy(
            emb.at[pl.ds(pl.multiple_of(low, 16), span), :],
            windows.at[at, cross, :span, :],
            done.at[at, cross],
        )

    @pl.when(at_step == 0)
    def _():
        fetch_labels = pltpu.make_async_copy(local, labels.at[:label_rows, :], arrived)
        fetch_labels.start()

        def add(o, total):
            starts[o] = total
            return total + counts[0, o]

        lax.fori_loop(0, owners, add, 0)
        for cross in range(max(len(c) for _, _, c in slots)):
            for at, (same_class, step, crosses) in enumerate(slots):
                if cross < len(crosses):
                    kind = core if same_class else 1 - core
                    first = starts[owner_of(kind, step, crosses[cross])]
                    fetch(at, cross, first // 16 * 16).start()
        labels[label_rows:, :] = jnp.zeros((16, LANES), jnp.int32)
        for at, (_, _, crosses) in enumerate(slots):
            for cross in range(len(crosses)):
                windows[at, cross, span:, :] = jnp.zeros((80, width), BF16)
        fetch_labels.wait()

    line = iota((TAIL, LANES), 0) * LANES + iota((TAIL, LANES), 1)
    lane = iota((TAIL, LANES), 1)
    for at_slot, ((same_class, step, crosses), out) in enumerate(zip(slots, outs)):

        @pl.when(at_step < len(crosses))
        def _():
            cross = at_step + crosses[0]
            kind = core if same_class else 1 - core
            owner = owner_of(kind, step, cross)
            first = starts[owner]
            count = counts[0, owner]
            base16 = first // 16 * 16
            turn = first - base16
            far = turn >= 8
            small = jnp.where(far, turn - 8, turn)
            turn_back = lax.rem(8 - small, 8)
            kept = iota((9, 8, width), 1) < 8 - small
            behind = base16 - jnp.minimum(base16, per_dev - span)
            fetch(at_slot, at_step, base16).wait()
            for at in range(0, capacity, 64):
                top = pl.multiple_of(jnp.minimum(behind + at, span), 16)
                window = windows[at_slot, at_step, pl.ds(top, 80), :]
                window = window.astype(F32).reshape(10, 8, width)
                window = pltpu.roll(window, turn_back, 1)
                moved = jnp.where(kept, window[:9], window[1:])
                moved = jnp.where(far, moved[1:], moved[:8])
                out[0, at : at + 64, :] = moved.reshape(64, width).astype(BF16)
            base = first // LANES
            shift = first - base * LANES
            got = [labels[pl.ds(base + i, 1), :] for i in range(TAIL + 1)]
            low_part = jnp.concatenate(got[:TAIL], axis=0)
            high_part = jnp.concatenate(got[1:], axis=0)
            back = lax.rem(LANES - shift, LANES)
            low_part = pltpu.roll(low_part, back, 1)
            high_part = pltpu.roll(high_part, back, 1)
            value = jnp.where(lane < LANES - shift, low_part, high_part)
            live = line < count
            high = jnp.where(live, lax.shift_right_logical(value, 7), 64).astype(F32)
            low = jnp.where(live, value & 127, 0).astype(F32)
            if crosses[0] == 0:
                own_tags = [tags[pl.ds(owner_of(kind, step, c), 1), :] for c in range(SIDE)]
                high = jnp.concatenate([high[: TAIL - SIDE]] + own_tags, axis=0)
            out[0, capacity:, :] = jnp.concatenate([high, low], axis=1).astype(BF16)


def pack(slots, send_counts, embeddings, local, capacity, tags=None, limit=None):
    _, width = embeddings.shape
    tall = capacity + TAIL
    longest = max(len(c) for _, _, c in slots)

    def spec(length):
        return pl.BlockSpec((1, tall, width), lambda q: (jnp.minimum(q, length - 1), 0, 0))

    many = sum(len(c) for _, _, c in slots)
    held = len(slots) * longest * (capacity + 96) * width * 2 + len(slots) * 2 * tall * width * 2
    return pl.pallas_call(
        functools.partial(pack_body, slots, capacity, tags is not None),
        grid=(longest,),
        out_shape=[jax.ShapeDtypeStruct((len(c), tall, width), BF16) for _, _, c in slots],
        in_specs=[
            pl.BlockSpec(memory_space=pltpu.SMEM),
            pl.BlockSpec(memory_space=pltpu.HBM),
            pl.BlockSpec(memory_space=pltpu.HBM),
        ]
        + ([] if tags is None else [pl.BlockSpec(tags.shape, lambda q: (0, 0))]),
        out_specs=[spec(len(c)) for _, _, c in slots],
        scratch_shapes=[
            pltpu.VMEM((len(slots), longest, capacity + 96, width), BF16),
            pltpu.VMEM((local.shape[0] + 16, LANES), jnp.int32),
            pltpu.SMEM((send_counts.shape[1],), jnp.int32),
            pltpu.SemaphoreType.DMA((len(slots), longest)),
            pltpu.SemaphoreType.DMA,
        ],
        compiler_params=pltpu.CompilerParams(vmem_limit_bytes=limit or held + 6 * MIB),
        cost_estimate=pl.CostEstimate(
            flops=0,
            bytes_accessed=2 * many * tall * width * 2,
            transcendentals=0,
        ),
        name="pack_rows",
    )(send_counts, embeddings, local, *([] if tags is None else [tags]))


def sums_body(lowest, capacity, crosses, had_lowest, sent, *refs):
    sources = len(lowest)
    arrived, refs = refs[:sources], refs[sources:]
    had_acc, had_counts = None, None
    if had_lowest is not None:
        had_acc, had_counts, refs = refs[0], refs[1], refs[2:]
    if sent:
        out, low_hot, high_hot, onehot, data = refs
        out_counts = None
    else:
        out, out_counts, low_hot, high_hot, onehot, data = refs
    digits = high_hot.shape[0]
    depth = sources * capacity
    size = onehot.shape[0]
    group = size // LANES
    fine_dev = digits * LANES

    def one(i):
        for s in range(sources):
            slot = arrived[s].at[crosses[0] - lowest[s] + i]
            tail = slot[capacity:, :].astype(F32)
            data[s * capacity : (s + 1) * capacity, :] = slot[:capacity, :]
            for part in range(capacity // LANES):
                at = s * capacity + part * LANES
                high = tail[part : part + 1, :LANES]
                low = tail[part : part + 1, LANES : 2 * LANES]
                low_hot[:, at : at + LANES] = jnp.where(
                    iota((LANES, LANES), 0).astype(F32) == low, 1.0, 0.0
                ).astype(BF16)
                high_hot[:, at : at + LANES] = jnp.where(
                    iota((digits, LANES), 0).astype(F32) == high, 1.0, 0.0
                )
        counts = lax.dot_general(
            high_hot[...].astype(BF16),
            low_hot[...],
            (((1,), (1,)), ((), ())),
            preferred_element_type=F32,
        )
        if had_counts is not None:
            counts = counts + had_counts[crosses[0] - had_lowest + i]
        if sent:
            tens = jnp.floor(counts / 64.0)
            out[fine_dev:, :] = jnp.concatenate([tens, counts - 64.0 * tens], axis=1).astype(BF16)
        else:
            out_counts[i] = counts
        for part in range(digits // group):
            for h in range(group):
                at_high = part * group + h
                row = jnp.broadcast_to(high_hot[at_high : at_high + 1, :], (16, depth)).astype(BF16)
                for at in range(0, LANES, 16):
                    top = h * LANES + at
                    onehot[top : top + 16, :] = low_hot[at : at + 16, :] * row
            total = jnp.dot(onehot[...], data[...], preferred_element_type=F32)
            rows = slice(part * size, (part + 1) * size)
            if had_acc is not None:
                total = total + had_acc[crosses[0] - had_lowest + i, rows, :]
            if sent:
                out[rows, :] = total.astype(BF16)
            else:
                out[i, rows, :] = total

    if len(crosses) == 1:
        one(0)
    else:
        pl.loop(0, len(crosses))(one)


def line_sums(arrived, capacity, fine_dev, crosses, had=None, send=False):
    width = arrived[0][0].shape[2]
    tall = capacity + TAIL
    sources = len(arrived)
    digits = fine_dev // LANES
    size = fine_dev // 2
    many = len(crosses)
    operands = [a for a, _ in arrived]
    had_lowest = None
    if had is not None:
        acc, counts, had_lowest = had
        operands += [acc, counts]
    if send:
        out_shape = jax.ShapeDtypeStruct((fine_dev + 16, width), BF16)
    else:
        out_shape = (
            jax.ShapeDtypeStruct((many, fine_dev, width), F32),
            jax.ShapeDtypeStruct((many, digits, LANES), F32),
        )
    body = functools.partial(
        sums_body, tuple(low for _, low in arrived), capacity, crosses, had_lowest, send
    )
    return pl.pallas_call(
        body,
        out_shape=out_shape,
        scratch_shapes=[
            pltpu.VMEM((LANES, sources * capacity), BF16),
            pltpu.VMEM((digits, sources * capacity), F32),
            pltpu.VMEM((size, sources * capacity), BF16),
            pltpu.VMEM((sources * capacity, width), BF16),
        ],
        compiler_params=pltpu.CompilerParams(vmem_limit_bytes=(8 + 2 * sources) * MIB),
        cost_estimate=pl.CostEstimate(
            flops=2 * many * sources * capacity * fine_dev * width,
            bytes_accessed=many * (sources * tall * width * 2 + fine_dev * width * 8),
            transcendentals=0,
        ),
        name="line_sums",
    )(*operands)


def update_body(slots, acc, counts, old, owner_hot, rank_hot, *refs):
    steps = SIDE - 1
    got, refs = refs[:steps], refs[steps:]
    new, whole, outs, placement = refs[0], refs[1], refs[2:-1], refs[-1]
    fine_dev = old.shape[0]
    count = counts[0]
    for g in got:
        value = g[fine_dev:, :].astype(F32)
        count = count + value[:, :LANES] * 64.0 + value[:, LANES : 2 * LANES]
    tens = jnp.floor(count / 64.0)
    eye = jnp.where(iota((LANES, LANES), 0) == iota((LANES, LANES), 1), 1.0, 0.0)
    turn = lambda a: lax.dot_general(
        eye.astype(BF16), a.astype(BF16), (((1,), (1,)), ((), ())), preferred_element_type=F32
    )
    column = turn(tens) * 64.0 + turn(count - 64.0 * tens)
    for h in range(fine_dev // LANES):
        at = slice(h * LANES, (h + 1) * LANES)
        total = acc[0, at, :] + old[at, :].astype(F32)
        for g in got:
            total = total + g[at, :].astype(F32)
        fresh = (total / (column[:, h : h + 1] + 1.0)).astype(BF16)
        new[at, :] = fresh
        whole[at, :] = fresh
    place_body(slots, owner_hot, rank_hot, whole, *outs, placement)


def update(acc, counts, old_fine, got, slots, owner_hot, rank_hot):
    fine_dev, width = old_fine.shape
    capacity = rank_hot.shape[0]
    return pl.pallas_call(
        functools.partial(update_body, slots),
        out_shape=[jax.ShapeDtypeStruct((fine_dev, width), BF16)] * 2
        + [jax.ShapeDtypeStruct((SIDE, capacity, width), BF16)] * len(slots),
        scratch_shapes=[pltpu.VMEM((SIDE * capacity, fine_dev), BF16)],
        compiler_params=pltpu.CompilerParams(vmem_limit_bytes=24 * MIB),
        name="new_fine",
    )(acc, counts, old_fine, owner_hot, rank_hot, *got)


def plan_body(coarse_dev, ids, owner_hot, rank_hot, labels):
    peers, fine_dev = owner_hot.shape
    value = ids[...]
    owner = value // coarse_dev
    local = (value - owner * coarse_dev).astype(F32)
    member = jnp.where(iota((peers, fine_dev), 0) == owner, 1.0, 0.0)
    owner_hot[...] = member
    step = 256
    before = jnp.where(iota((step, step), 0) < iota((step, step), 1), 1.0, 0.0).astype(BF16)
    carry = jnp.zeros((peers, 1), F32)
    for at in range(0, fine_dev, step):
        piece = member[:, at : at + step]
        prefix = jnp.dot(piece.astype(BF16), before, preferred_element_type=F32) + carry
        rank = jnp.sum(prefix * piece, axis=0, keepdims=True)
        carry = carry + jnp.sum(piece, axis=1, keepdims=True)
        hot = jnp.where(iota((rank_hot.shape[0], step), 0).astype(F32) == rank, 1.0, 0.0)
        rank_hot[:, at : at + step] = hot.astype(BF16)
    tagged = (member * (local + 1.0)).astype(BF16)
    labels[...] = lax.dot_general(
        tagged, rank_hot[...], (((1,), (1,)), ((), ())), preferred_element_type=F32
    )


def plan(coarse_ids, peers, capacity, coarse_dev):
    fine_dev = coarse_ids.shape[1]
    return pl.pallas_call(
        functools.partial(plan_body, coarse_dev),
        out_shape=(
            jax.ShapeDtypeStruct((peers, fine_dev), F32),
            jax.ShapeDtypeStruct((capacity, fine_dev), BF16),
            jax.ShapeDtypeStruct((peers, capacity), F32),
        ),
        compiler_params=pltpu.CompilerParams(vmem_limit_bytes=24 * MIB),
        name="plan_clusters",
    )(coarse_ids)


def place_body(slots, owner_hot, rank_hot, new, *refs):
    outs, placement = refs[:-1], refs[-1]
    capacity, fine_dev = rank_hot.shape
    core = lax.rem(lax.axis_index("rows"), 2)
    for (same_class, step), out in zip(slots, outs):
        kind = core if same_class else 1 - core
        for cross in range(SIDE):
            row = owner_hot[pl.ds(owner_of(kind, step, cross), 1), :]
            row = jnp.broadcast_to(row, (16, fine_dev)).astype(BF16)
            for at in range(0, capacity, 16):
                top = cross * capacity + at
                placement[top : top + 16, :] = rank_hot[at : at + 16, :] * row
        sent = jnp.dot(placement[...], new[...], preferred_element_type=F32).astype(BF16)
        for cross in range(SIDE):
            out[cross, :, :] = sent[cross * capacity : (cross + 1) * capacity, :]


def place(slots, owner_hot, rank_hot, new_fine):
    capacity, fine_dev = rank_hot.shape
    width = new_fine.shape[1]
    return pl.pallas_call(
        functools.partial(place_body, slots),
        out_shape=[jax.ShapeDtypeStruct((SIDE, capacity, width), BF16)] * len(slots),
        scratch_shapes=[pltpu.VMEM((SIDE * capacity, fine_dev), BF16)],
        compiler_params=pltpu.CompilerParams(vmem_limit_bytes=24 * MIB),
        cost_estimate=pl.CostEstimate(
            flops=2 * len(slots) * SIDE * capacity * fine_dev * width,
            bytes_accessed=fine_dev * width * 2,
            transcendentals=0,
        ),
        name="place_clusters",
    )(owner_hot, rank_hot, new_fine)


def tag_hot_body(sources, *refs):
    tails, hot, digits = refs[:sources], refs[-2], refs[-1]
    many, coarse_dev, depth = hot.shape
    capacity = depth // sources
    row = iota((coarse_dev, capacity), 0).astype(F32) + 1.0
    for cross in range(many):
        for s in range(sources):
            at = TAIL - SIDE + cross
            tag = tails[s][0].astype(F32)[at : at + 1, :capacity]
            one = jnp.where(row == tag, 1.0, 0.0).astype(BF16)
            hot[cross, :, s * capacity : (s + 1) * capacity] = one
        count = lax.dot_general(
            jnp.ones((8, depth), BF16),
            hot[cross],
            (((1,), (1,)), ((), ())),
            preferred_element_type=F32,
        )
        tens = jnp.floor(count / 64.0)
        digits[cross] = jnp.concatenate([tens, count - 64.0 * tens], axis=0).astype(BF16)


def tag_hot(tagged, capacity, capacity_two, coarse_dev):
    width = tagged[0].shape[2]
    sources = len(tagged)
    return pl.pallas_call(
        functools.partial(tag_hot_body, sources),
        grid=(1,),
        out_shape=(
            jax.ShapeDtypeStruct((SIDE, coarse_dev, sources * capacity_two), BF16),
            jax.ShapeDtypeStruct((SIDE, 16, coarse_dev), BF16),
        ),
        in_specs=[pl.BlockSpec((1, TAIL, width), lambda i: (0, capacity // TAIL, 0))] * sources,
        out_specs=(
            pl.BlockSpec((SIDE, coarse_dev, sources * capacity_two), lambda i: (0, 0, 0)),
            pl.BlockSpec((SIDE, 16, coarse_dev), lambda i: (0, 0, 0)),
        ),
        compiler_params=pltpu.CompilerParams(vmem_limit_bytes=12 * MIB),
        name="tag_hot",
    )(*tagged)


def coarse_sums_body(sources, order, *refs):
    arrived, (hot, digits), outs, data = (
        refs[:sources],
        refs[sources : sources + 2],
        refs[sources + 2 : -1],
        refs[-1],
    )
    capacity = arrived[0].shape[1]
    coarse_dev = hot.shape[1]
    for cross, out in zip(order, outs):
        for s in range(sources):
            data[s * capacity : (s + 1) * capacity, :] = arrived[s][cross]
        total = jnp.dot(hot[cross], data[...], preferred_element_type=F32)
        if cross == 0:
            out[...] = total
        else:
            out[:coarse_dev, :] = total.astype(BF16)
            out[coarse_dev:, :] = digits[cross]


def coarse_sums(arrived, hot, digits, order):
    capacity, width = arrived[0].shape[1:]
    sources = len(arrived)
    coarse_dev = hot.shape[1]
    sent = jax.ShapeDtypeStruct((coarse_dev + 16, width), BF16)
    kept = jax.ShapeDtypeStruct((coarse_dev, width), F32)
    return pl.pallas_call(
        functools.partial(coarse_sums_body, sources, order),
        out_shape=[kept if c == 0 else sent for c in order],
        scratch_shapes=[pltpu.VMEM((sources * capacity, width), BF16)],
        compiler_params=pltpu.CompilerParams(vmem_limit_bytes=16 * MIB),
        name="coarse_sums",
    )(*arrived, hot, digits)


def coarse_body(acc, digits, old, *refs):
    got, means = refs[:-1], refs[-1]
    coarse_dev, _ = acc.shape
    total = acc[...] + old[...].astype(F32)
    tens = digits[0, :8, :].astype(F32)
    ones = digits[0, 8:, :].astype(F32)
    for g in got:
        total = total + g[:coarse_dev, :].astype(F32)
        tens = tens + g[coarse_dev : coarse_dev + 8, :].astype(F32)
        ones = ones + g[coarse_dev + 8 :, :].astype(F32)
    eye = jnp.where(
        iota((coarse_dev, coarse_dev), 0) == iota((coarse_dev, coarse_dev), 1), 1.0, 0.0
    ).astype(BF16)
    turn = lambda a: lax.dot_general(
        eye, a.astype(BF16), (((1,), (1,)), ((), ())), preferred_element_type=F32
    )
    count = turn(tens) * 64.0 + turn(ones)
    means[...] = (total / (count[:, :1] + 1.0)).astype(BF16)


def coarse(acc, digits, old_coarse, got):
    return pl.pallas_call(
        coarse_body,
        out_shape=jax.ShapeDtypeStruct(old_coarse.shape, BF16),
        compiler_params=pltpu.CompilerParams(vmem_limit_bytes=8 * MIB),
        name="coarse_means",
    )(acc, digits, old_coarse, *got)


def finish_body(groups, at, *refs):
    pieces, out, full = refs[:groups], refs[groups], refs[groups + 1]
    width = pieces[0].shape[1]
    for step in range(groups):
        place = lax.rem(at[0] + step, groups) * width
        full[:, pl.ds(pl.multiple_of(place, width), width)] = pieces[step][...].astype(F32)
    whole = full[...]
    scale = lax.rsqrt(jnp.mean(whole * whole, axis=1, keepdims=True) + 1e-06)
    out[...] = (whole * scale).astype(BF16)


def finish(at, pieces):
    groups = len(pieces)
    rows, width = pieces[0].shape
    return pl.pallas_call(
        functools.partial(finish_body, groups),
        out_shape=jax.ShapeDtypeStruct((rows, groups * width), BF16),
        in_specs=[pl.BlockSpec(memory_space=pltpu.SMEM)]
        + [pl.BlockSpec(memory_space=pltpu.VMEM)] * groups,
        scratch_shapes=[pltpu.VMEM((rows, groups * width), F32)],
        compiler_params=pltpu.CompilerParams(vmem_limit_bytes=24 * MIB),
        name="coarse_dirs",
    )(at, *pieces)


def level_step(embeddings, fine_local, send_counts, old_fine, coarse_ids, old_coarse):
    peers = lax.axis_size("rows")
    groups = lax.axis_size("grp")
    per_dev = embeddings.shape[0]
    fine_dev = old_fine.shape[0]
    coarse_dev = old_coarse.shape[0]
    capacity = 2 * per_dev // peers
    capacity_two = 2 * fine_dev // peers
    local = fine_local.reshape(-1, LANES)
    steps = range(1, SIDE)

    def along(slots, step, same_class):
        return lax.ppermute(slots, "rows", line_pairs(step, same_class))

    rows = (send_counts, embeddings, local, capacity)
    sent, own = tuple(steps), (0,)
    order = (2, 1, 3)

    kept = []
    for part, group in (("far", order[:1]), ("near", order[1:])):
        limit = 61 * MIB
        keep = pack([(True, s, sent) for s in group], *rows, limit=limit)
        for s, a in zip(group, keep):
            kept.append(along(a, s, True))
    owner_hot, rank_hot, tags = plan(
        coarse_ids.reshape(1, -1), peers, capacity_two, coarse_dev
    )
    more = pack(
        [(False, s, sent) for s in order]
        + [(False, 0, own + sent), (True, 0, own + sent)]
        + [(k, s, own) for k in (True, False) for s in order],
        *rows,
        tags,
    )
    swapped = along(more[3], 0, False)
    given = [along(a, s, False) for s, a in zip(order, more[:3])]
    near = [(more[4], 0), (swapped, 0)]
    had = line_sums(near + [(kept[0], 1)], capacity, fine_dev, sent)
    had = line_sums([(a, 1) for a in kept[1:]], capacity, fine_dev, sent, (*had, 1))
    kept_own = [along(a, s, True) for s, a in zip(order, more[5:8])]
    given_own = [along(a, s, False) for s, a in zip(order, more[8:])]
    got = {}
    for cross in order:
        part = line_sums(
            [(a, 1) for a in given], capacity, fine_dev, (cross,), (*had, 1), send=True
        )
        got[cross] = lax.ppermute(part, "rows", cross_pairs(cross))
    acc, counts = line_sums(near + [(a, 0) for a in kept_own + given_own], capacity, fine_dev, own)
    hot, digits = tag_hot(
        [more[4], swapped] + kept_own + given_own, capacity, capacity_two, coarse_dev
    )
    new_fine, near_fine, *keep = update(
        acc,
        counts,
        old_fine,
        [got[c] for c in steps],
        [(True, s) for s in order],
        owner_hot,
        rank_hot,
    )
    arrived = []
    for s, a in zip(order, keep):
        arrived.append(along(a, s, True))
    give = place([(False, s) for s in order], owner_hot, rank_hot, near_fine)
    for s, a in zip(order, give):
        arrived.append(along(a, s, False))
    here = place([(False, 0), (True, 0)], owner_hot, rank_hot, near_fine)
    arrived = [here[1], along(here[0], 0, False)] + arrived
    *sent_sums, acc = coarse_sums(arrived, hot, digits, order + own)
    got = []
    for cross, part in zip(order, sent_sums):
        got.append(lax.ppermute(part, "rows", cross_pairs(cross)))
    means = coarse(acc, digits, old_coarse, got)
    pieces = [means]
    for step in range(1, groups):
        back = [((g + step) % groups, g) for g in range(groups)]
        pieces.append(lax.ppermute(means, "grp", back))
    at = lax.axis_index("grp").astype(jnp.int32).reshape(1)
    return (new_fine, finish(at, pieces))


def solution(mesh):
    in_specs = (
        P("rows", "grp"),
        P("rows"),
        P("rows", None),
        P("rows", "grp"),
        P("rows"),
        P("rows", "grp"),
    )
    out_specs = (P("rows", "grp"), P("rows", None))
    return jax.shard_map(
        level_step, mesh=mesh, in_specs=in_specs, out_specs=out_specs, check_vma=False
    )
```

```python
import functools

import jax
import jax.numpy as jnp
from jax import lax
from jax.experimental import pallas as pl
from jax.experimental.pallas import tpu as pltpu
from jax.sharding import PartitionSpec as P


F32 = jnp.float32
BF16 = jnp.bfloat16
LANES = 128
MIB = 1024 * 1024
TAIL = 8
SIDE = 4


def iota(shape, axis):
    return lax.broadcasted_iota(jnp.int32, shape, axis)


def device(x, y, core):
    return (x % SIDE) * 2 * SIDE + (y % SIDE) * 2 + core


CHIPS = [(x, y) for x in range(SIDE) for y in range(SIDE)]


def line_pairs(step, same_class):
    pairs = []
    for x, y in CHIPS:
        for core in range(2):
            kind = core if same_class else 1 - core
            to = device(x + step, y, 0) if kind == 0 else device(x, y + step, 1)
            pairs.append((device(x, y, core), to))
    return pairs


def cross_pairs(step):
    pairs = []
    for x, y in CHIPS:
        pairs.append((device(x, y, 0), device(x, y + step, 0)))
        pairs.append((device(x, y, 1), device(x + step, y, 1)))
    return pairs


def owner_of(kind, step, cross):
    here = lax.axis_index("rows")
    along = lax.rem(here // (2 * SIDE) + jnp.where(kind == 0, step, cross), SIDE)
    over = lax.rem(lax.rem(here // 2, SIDE) + jnp.where(kind == 0, cross, step), SIDE)
    return along * 2 * SIDE + over * 2 + kind


def pack_body(slots, capacity, tagged, counts, emb, local, *rest):
    tags = rest[0] if tagged else None
    rest = rest[1:] if tagged else rest
    outs, (windows, labels, starts, done, arrived) = rest[: len(slots)], rest[len(slots) :]
    per_dev, width = emb.shape
    span = capacity + 16
    label_rows = local.shape[0]
    owners = counts.shape[1]
    at_step = pl.program_id(0)
    core = lax.rem(lax.axis_index("rows"), 2)

    def fetch(at, cross, base):
        low = jnp.minimum(base, per_dev - span)
        return pltpu.make_async_copy(
            emb.at[pl.ds(pl.multiple_of(low, 16), span), :],
            windows.at[at, cross, :span, :],
            done.at[at, cross],
        )

    @pl.when(at_step == 0)
    def _():
        fetch_labels = pltpu.make_async_copy(local, labels.at[:label_rows, :], arrived)
        fetch_labels.start()

        def add(o, total):
            starts[o] = total
            return total + counts[0, o]

        lax.fori_loop(0, owners, add, 0)
        for cross in range(max(len(c) for _, _, c in slots)):
            for at, (same_class, step, crosses) in enumerate(slots):
                if cross < len(crosses):
                    kind = core if same_class else 1 - core
                    first = starts[owner_of(kind, step, crosses[cross])]
                    fetch(at, cross, first // 16 * 16).start()
        labels[label_rows:, :] = jnp.zeros((16, LANES), jnp.int32)
        for at, (_, _, crosses) in enumerate(slots):
            for cross in range(len(crosses)):
                windows[at, cross, span:, :] = jnp.zeros((80, width), BF16)
        fetch_labels.wait()

    line = iota((TAIL, LANES), 0) * LANES + iota((TAIL, LANES), 1)
    lane = iota((TAIL, LANES), 1)
    for at_slot, ((same_class, step, crosses), out) in enumerate(zip(slots, outs)):

        @pl.when(at_step < len(crosses))
        def _():
            stride = crosses[1] - crosses[0] if len(crosses) > 1 else 1
            cross = at_step * stride + crosses[0]
            kind = core if same_class else 1 - core
            owner = owner_of(kind, step, cross)
            first = starts[owner]
            count = counts[0, owner]
            base16 = first // 16 * 16
            turn = first - base16
            far = turn >= 8
            small = jnp.where(far, turn - 8, turn)
            turn_back = lax.rem(8 - small, 8)
            kept = iota((9, 8, width), 1) < 8 - small
            behind = base16 - jnp.minimum(base16, per_dev - span)
            fetch(at_slot, at_step, base16).wait()
            for at in range(0, capacity, 64):
                top = pl.multiple_of(jnp.minimum(behind + at, span), 16)
                window = windows[at_slot, at_step, pl.ds(top, 80), :]
                window = window.astype(F32).reshape(10, 8, width)
                window = pltpu.roll(window, turn_back, 1)
                moved = jnp.where(kept, window[:9], window[1:])
                moved = jnp.where(far, moved[1:], moved[:8])
                out[0, at : at + 64, :] = moved.reshape(64, width).astype(BF16)
            base = first // LANES
            shift = first - base * LANES
            got = [labels[pl.ds(base + i, 1), :] for i in range(TAIL + 1)]
            low_part = jnp.concatenate(got[:TAIL], axis=0)
            high_part = jnp.concatenate(got[1:], axis=0)
            back = lax.rem(LANES - shift, LANES)
            low_part = pltpu.roll(low_part, back, 1)
            high_part = pltpu.roll(high_part, back, 1)
            value = jnp.where(lane < LANES - shift, low_part, high_part)
            live = line < count
            high = jnp.where(live, lax.shift_right_logical(value, 7), 64).astype(F32)
            low = jnp.where(live, value & 127, 0).astype(F32)
            if crosses[0] == 0:
                own_tags = [tags[pl.ds(owner_of(kind, step, c), 1), :] for c in range(SIDE)]
                high = jnp.concatenate([high[: TAIL - SIDE]] + own_tags, axis=0)
            out[0, capacity:, :] = jnp.concatenate([high, low], axis=1).astype(BF16)


def pack(slots, send_counts, embeddings, local, capacity, tags=None, limit=None):
    _, width = embeddings.shape
    tall = capacity + TAIL
    longest = max(len(c) for _, _, c in slots)

    def spec(length):
        return pl.BlockSpec((1, tall, width), lambda q: (jnp.minimum(q, length - 1), 0, 0))

    many = sum(len(c) for _, _, c in slots)
    held = len(slots) * longest * (capacity + 96) * width * 2 + len(slots) * 2 * tall * width * 2
    return pl.pallas_call(
        functools.partial(pack_body, slots, capacity, tags is not None),
        grid=(longest,),
        out_shape=[jax.ShapeDtypeStruct((len(c), tall, width), BF16) for _, _, c in slots],
        in_specs=[
            pl.BlockSpec(memory_space=pltpu.SMEM),
            pl.BlockSpec(memory_space=pltpu.HBM),
            pl.BlockSpec(memory_space=pltpu.HBM),
        ]
        + ([] if tags is None else [pl.BlockSpec(tags.shape, lambda q: (0, 0))]),
        out_specs=[spec(len(c)) for _, _, c in slots],
        scratch_shapes=[
            pltpu.VMEM((len(slots), longest, capacity + 96, width), BF16),
            pltpu.VMEM((local.shape[0] + 16, LANES), jnp.int32),
            pltpu.SMEM((send_counts.shape[1],), jnp.int32),
            pltpu.SemaphoreType.DMA((len(slots), longest)),
            pltpu.SemaphoreType.DMA,
        ],
        compiler_params=pltpu.CompilerParams(vmem_limit_bytes=limit or held + 6 * MIB),
        cost_estimate=pl.CostEstimate(
            flops=0,
            bytes_accessed=2 * many * tall * width * 2,
            transcendentals=0,
        ),
        name="pack_rows",
    )(send_counts, embeddings, local, *([] if tags is None else [tags]))


def sums_body(lowest, capacity, crosses, had_lowest, sent, *refs):
    sources = len(lowest)
    arrived, refs = refs[:sources], refs[sources:]
    had_acc, had_counts = None, None
    if had_lowest is not None:
        had_acc, had_counts, refs = refs[0], refs[1], refs[2:]
    if sent:
        out, low_hot, high_hot, onehot, data = refs
        out_counts = None
    else:
        out, out_counts, low_hot, high_hot, onehot, data = refs
    digits = high_hot.shape[0]
    depth = sources * capacity
    size = onehot.shape[0]
    group = size // LANES
    fine_dev = digits * LANES

    def one(i):
        for s in range(sources):
            slot = arrived[s].at[crosses[0] - lowest[s] + i]
            tail = slot[capacity:, :].astype(F32)
            data[s * capacity : (s + 1) * capacity, :] = slot[:capacity, :]
            for part in range(capacity // LANES):
                at = s * capacity + part * LANES
                high = tail[part : part + 1, :LANES]
                low = tail[part : part + 1, LANES : 2 * LANES]
                low_hot[:, at : at + LANES] = jnp.where(
                    iota((LANES, LANES), 0).astype(F32) == low, 1.0, 0.0
                ).astype(BF16)
                high_hot[:, at : at + LANES] = jnp.where(
                    iota((digits, LANES), 0).astype(F32) == high, 1.0, 0.0
                )
        counts = lax.dot_general(
            high_hot[...].astype(BF16),
            low_hot[...],
            (((1,), (1,)), ((), ())),
            preferred_element_type=F32,
        )
        if had_counts is not None:
            counts = counts + had_counts[crosses[0] - had_lowest + i]
        if sent:
            tens = jnp.floor(counts / 64.0)
            out[fine_dev:, :] = jnp.concatenate([tens, counts - 64.0 * tens], axis=1).astype(BF16)
        else:
            out_counts[i] = counts
        for part in range(digits // group):
            for h in range(group):
                at_high = part * group + h
                row = jnp.broadcast_to(high_hot[at_high : at_high + 1, :], (16, depth)).astype(BF16)
                for at in range(0, LANES, 16):
                    top = h * LANES + at
                    onehot[top : top + 16, :] = low_hot[at : at + 16, :] * row
            total = jnp.dot(onehot[...], data[...], preferred_element_type=F32)
            rows = slice(part * size, (part + 1) * size)
            if had_acc is not None:
                total = total + had_acc[crosses[0] - had_lowest + i, rows, :]
            if sent:
                out[rows, :] = total.astype(BF16)
            else:
                out[i, rows, :] = total

    if len(crosses) == 1:
        one(0)
    else:
        pl.loop(0, len(crosses))(one)


def line_sums(arrived, capacity, fine_dev, crosses, had=None, send=False):
    width = arrived[0][0].shape[2]
    tall = capacity + TAIL
    sources = len(arrived)
    digits = fine_dev // LANES
    size = fine_dev // 2
    many = len(crosses)
    operands = [a for a, _ in arrived]
    had_lowest = None
    if had is not None:
        acc, counts, had_lowest = had
        operands += [acc, counts]
    if send:
        out_shape = jax.ShapeDtypeStruct((fine_dev + 16, width), BF16)
    else:
        out_shape = (
            jax.ShapeDtypeStruct((many, fine_dev, width), F32),
            jax.ShapeDtypeStruct((many, digits, LANES), F32),
        )
    body = functools.partial(
        sums_body, tuple(low for _, low in arrived), capacity, crosses, had_lowest, send
    )
    return pl.pallas_call(
        body,
        out_shape=out_shape,
        scratch_shapes=[
            pltpu.VMEM((LANES, sources * capacity), BF16),
            pltpu.VMEM((digits, sources * capacity), F32),
            pltpu.VMEM((size, sources * capacity), BF16),
            pltpu.VMEM((sources * capacity, width), BF16),
        ],
        compiler_params=pltpu.CompilerParams(vmem_limit_bytes=(8 + 2 * sources) * MIB),
        cost_estimate=pl.CostEstimate(
            flops=2 * many * sources * capacity * fine_dev * width,
            bytes_accessed=many * (sources * tall * width * 2 + fine_dev * width * 8),
            transcendentals=0,
        ),
        name="line_sums",
    )(*operands)


def update_body(slots, acc, counts, old, owner_hot, rank_hot, *refs):
    steps = SIDE - 1
    got, refs = refs[:steps], refs[steps:]
    new, whole, outs, placement = refs[0], refs[1], refs[2:-1], refs[-1]
    fine_dev = old.shape[0]
    count = counts[0]
    for g in got:
        value = g[fine_dev:, :].astype(F32)
        count = count + value[:, :LANES] * 64.0 + value[:, LANES : 2 * LANES]
    tens = jnp.floor(count / 64.0)
    eye = jnp.where(iota((LANES, LANES), 0) == iota((LANES, LANES), 1), 1.0, 0.0)
    turn = lambda a: lax.dot_general(
        eye.astype(BF16), a.astype(BF16), (((1,), (1,)), ((), ())), preferred_element_type=F32
    )
    column = turn(tens) * 64.0 + turn(count - 64.0 * tens)
    for h in range(fine_dev // LANES):
        at = slice(h * LANES, (h + 1) * LANES)
        total = acc[0, at, :] + old[at, :].astype(F32)
        for g in got:
            total = total + g[at, :].astype(F32)
        fresh = (total / (column[:, h : h + 1] + 1.0)).astype(BF16)
        new[at, :] = fresh
        whole[at, :] = fresh
    place_body(slots, owner_hot, rank_hot, whole, *outs, placement)


def update(acc, counts, old_fine, got, slots, owner_hot, rank_hot):
    fine_dev, width = old_fine.shape
    capacity = rank_hot.shape[0]
    return pl.pallas_call(
        functools.partial(update_body, slots),
        out_shape=[jax.ShapeDtypeStruct((fine_dev, width), BF16)] * 2
        + [jax.ShapeDtypeStruct((SIDE, capacity, width), BF16)] * len(slots),
        scratch_shapes=[pltpu.VMEM((SIDE * capacity, fine_dev), BF16)],
        compiler_params=pltpu.CompilerParams(vmem_limit_bytes=24 * MIB),
        name="new_fine",
    )(acc, counts, old_fine, owner_hot, rank_hot, *got)


def plan_body(coarse_dev, ids, owner_hot, rank_hot, labels):
    peers, fine_dev = owner_hot.shape
    value = ids[...]
    owner = value // coarse_dev
    local = (value - owner * coarse_dev).astype(F32)
    member = jnp.where(iota((peers, fine_dev), 0) == owner, 1.0, 0.0)
    owner_hot[...] = member
    step = 256
    before = jnp.where(iota((step, step), 0) < iota((step, step), 1), 1.0, 0.0).astype(BF16)
    carry = jnp.zeros((peers, 1), F32)
    for at in range(0, fine_dev, step):
        piece = member[:, at : at + step]
        prefix = jnp.dot(piece.astype(BF16), before, preferred_element_type=F32) + carry
        rank = jnp.sum(prefix * piece, axis=0, keepdims=True)
        carry = carry + jnp.sum(piece, axis=1, keepdims=True)
        hot = jnp.where(iota((rank_hot.shape[0], step), 0).astype(F32) == rank, 1.0, 0.0)
        rank_hot[:, at : at + step] = hot.astype(BF16)
    tagged = (member * (local + 1.0)).astype(BF16)
    labels[...] = lax.dot_general(
        tagged, rank_hot[...], (((1,), (1,)), ((), ())), preferred_element_type=F32
    )


def plan(coarse_ids, peers, capacity, coarse_dev):
    fine_dev = coarse_ids.shape[1]
    return pl.pallas_call(
        functools.partial(plan_body, coarse_dev),
        out_shape=(
            jax.ShapeDtypeStruct((peers, fine_dev), F32),
            jax.ShapeDtypeStruct((capacity, fine_dev), BF16),
            jax.ShapeDtypeStruct((peers, capacity), F32),
        ),
        compiler_params=pltpu.CompilerParams(vmem_limit_bytes=24 * MIB),
        name="plan_clusters",
    )(coarse_ids)


def place_body(slots, owner_hot, rank_hot, new, *refs):
    outs, placement = refs[:-1], refs[-1]
    capacity, fine_dev = rank_hot.shape
    core = lax.rem(lax.axis_index("rows"), 2)
    for (same_class, step), out in zip(slots, outs):
        kind = core if same_class else 1 - core
        for cross in range(SIDE):
            row = owner_hot[pl.ds(owner_of(kind, step, cross), 1), :]
            row = jnp.broadcast_to(row, (16, fine_dev)).astype(BF16)
            for at in range(0, capacity, 16):
                top = cross * capacity + at
                placement[top : top + 16, :] = rank_hot[at : at + 16, :] * row
        sent = jnp.dot(placement[...], new[...], preferred_element_type=F32).astype(BF16)
        for cross in range(SIDE):
            out[cross, :, :] = sent[cross * capacity : (cross + 1) * capacity, :]


def place(slots, owner_hot, rank_hot, new_fine):
    capacity, fine_dev = rank_hot.shape
    width = new_fine.shape[1]
    return pl.pallas_call(
        functools.partial(place_body, slots),
        out_shape=[jax.ShapeDtypeStruct((SIDE, capacity, width), BF16)] * len(slots),
        scratch_shapes=[pltpu.VMEM((SIDE * capacity, fine_dev), BF16)],
        compiler_params=pltpu.CompilerParams(vmem_limit_bytes=24 * MIB),
        cost_estimate=pl.CostEstimate(
            flops=2 * len(slots) * SIDE * capacity * fine_dev * width,
            bytes_accessed=fine_dev * width * 2,
            transcendentals=0,
        ),
        name="place_clusters",
    )(owner_hot, rank_hot, new_fine)


def tag_hot_body(sources, *refs):
    tails, hot, digits = refs[:sources], refs[-2], refs[-1]
    many, coarse_dev, depth = hot.shape
    capacity = depth // sources
    row = iota((coarse_dev, capacity), 0).astype(F32) + 1.0
    for cross in range(many):
        for s in range(sources):
            at = TAIL - SIDE + cross
            tag = tails[s][0].astype(F32)[at : at + 1, :capacity]
            one = jnp.where(row == tag, 1.0, 0.0).astype(BF16)
            hot[cross, :, s * capacity : (s + 1) * capacity] = one
        count = lax.dot_general(
            jnp.ones((8, depth), BF16),
            hot[cross],
            (((1,), (1,)), ((), ())),
            preferred_element_type=F32,
        )
        tens = jnp.floor(count / 64.0)
        digits[cross] = jnp.concatenate([tens, count - 64.0 * tens], axis=0).astype(BF16)


def tag_hot(tagged, capacity, capacity_two, coarse_dev):
    width = tagged[0].shape[2]
    sources = len(tagged)
    return pl.pallas_call(
        functools.partial(tag_hot_body, sources),
        grid=(1,),
        out_shape=(
            jax.ShapeDtypeStruct((SIDE, coarse_dev, sources * capacity_two), BF16),
            jax.ShapeDtypeStruct((SIDE, 16, coarse_dev), BF16),
        ),
        in_specs=[pl.BlockSpec((1, TAIL, width), lambda i: (0, capacity // TAIL, 0))] * sources,
        out_specs=(
            pl.BlockSpec((SIDE, coarse_dev, sources * capacity_two), lambda i: (0, 0, 0)),
            pl.BlockSpec((SIDE, 16, coarse_dev), lambda i: (0, 0, 0)),
        ),
        compiler_params=pltpu.CompilerParams(vmem_limit_bytes=12 * MIB),
        name="tag_hot",
    )(*tagged)


def coarse_sums_body(sources, order, *refs):
    arrived, (hot, digits), outs, data = (
        refs[:sources],
        refs[sources : sources + 2],
        refs[sources + 2 : -1],
        refs[-1],
    )
    capacity = arrived[0].shape[1]
    coarse_dev = hot.shape[1]
    for cross, out in zip(order, outs):
        for s in range(sources):
            data[s * capacity : (s + 1) * capacity, :] = arrived[s][cross]
        total = jnp.dot(hot[cross], data[...], preferred_element_type=F32)
        if cross == 0:
            out[...] = total
        else:
            out[:coarse_dev, :] = total.astype(BF16)
            out[coarse_dev:, :] = digits[cross]


def coarse_sums(arrived, hot, digits, order):
    capacity, width = arrived[0].shape[1:]
    sources = len(arrived)
    coarse_dev = hot.shape[1]
    sent = jax.ShapeDtypeStruct((coarse_dev + 16, width), BF16)
    kept = jax.ShapeDtypeStruct((coarse_dev, width), F32)
    return pl.pallas_call(
        functools.partial(coarse_sums_body, sources, order),
        out_shape=[kept if c == 0 else sent for c in order],
        scratch_shapes=[pltpu.VMEM((sources * capacity, width), BF16)],
        compiler_params=pltpu.CompilerParams(vmem_limit_bytes=16 * MIB),
        name="coarse_sums",
    )(*arrived, hot, digits)


def coarse_body(acc, digits, old, *refs):
    got, means = refs[:-1], refs[-1]
    coarse_dev, _ = acc.shape
    total = acc[...] + old[...].astype(F32)
    tens = digits[0, :8, :].astype(F32)
    ones = digits[0, 8:, :].astype(F32)
    for g in got:
        total = total + g[:coarse_dev, :].astype(F32)
        tens = tens + g[coarse_dev : coarse_dev + 8, :].astype(F32)
        ones = ones + g[coarse_dev + 8 :, :].astype(F32)
    eye = jnp.where(
        iota((coarse_dev, coarse_dev), 0) == iota((coarse_dev, coarse_dev), 1), 1.0, 0.0
    ).astype(BF16)
    turn = lambda a: lax.dot_general(
        eye, a.astype(BF16), (((1,), (1,)), ((), ())), preferred_element_type=F32
    )
    count = turn(tens) * 64.0 + turn(ones)
    means[...] = (total / (count[:, :1] + 1.0)).astype(BF16)


def coarse(acc, digits, old_coarse, got):
    return pl.pallas_call(
        coarse_body,
        out_shape=jax.ShapeDtypeStruct(old_coarse.shape, BF16),
        compiler_params=pltpu.CompilerParams(vmem_limit_bytes=8 * MIB),
        name="coarse_means",
    )(acc, digits, old_coarse, *got)


def finish_body(groups, at, *refs):
    pieces, out, full = refs[:groups], refs[groups], refs[groups + 1]
    width = pieces[0].shape[1]
    for step in range(groups):
        place = lax.rem(at[0] + step, groups) * width
        full[:, pl.ds(pl.multiple_of(place, width), width)] = pieces[step][...].astype(F32)
    whole = full[...]
    scale = lax.rsqrt(jnp.mean(whole * whole, axis=1, keepdims=True) + 1e-06)
    out[...] = (whole * scale).astype(BF16)


def finish(at, pieces):
    groups = len(pieces)
    rows, width = pieces[0].shape
    return pl.pallas_call(
        functools.partial(finish_body, groups),
        out_shape=jax.ShapeDtypeStruct((rows, groups * width), BF16),
        in_specs=[pl.BlockSpec(memory_space=pltpu.SMEM)]
        + [pl.BlockSpec(memory_space=pltpu.VMEM)] * groups,
        scratch_shapes=[pltpu.VMEM((rows, groups * width), F32)],
        compiler_params=pltpu.CompilerParams(vmem_limit_bytes=24 * MIB),
        name="coarse_dirs",
    )(at, *pieces)


def level_step(embeddings, fine_local, send_counts, old_fine, coarse_ids, old_coarse):
    peers = lax.axis_size("rows")
    groups = lax.axis_size("grp")
    per_dev = embeddings.shape[0]
    fine_dev = old_fine.shape[0]
    coarse_dev = old_coarse.shape[0]
    capacity = 2 * per_dev // peers
    capacity_two = 2 * fine_dev // peers
    local = fine_local.reshape(-1, LANES)
    steps = range(1, SIDE)

    def along(slots, step, same_class):
        return lax.ppermute(slots, "rows", line_pairs(step, same_class))

    rows = (send_counts, embeddings, local, capacity)
    sent, own = tuple(steps), (0,)
    order = (2, 1, 3)

    kept = []
    for part, group in (("far", order[:1]), ("near", order[1:])):
        limit = 61 * MIB
        keep = pack([(True, s, sent) for s in group], *rows, limit=limit)
        for s, a in zip(group, keep):
            kept.append(along(a, s, True))
    owner_hot, rank_hot, tags = plan(
        coarse_ids.reshape(1, -1), peers, capacity_two, coarse_dev
    )
    more = pack(
        [(False, s, (2,)) for s in order]
        + [(False, 0, own + sent), (True, 0, own + sent)]
        + [(k, s, own) for k in (True, False) for s in order]
        + [(False, s, (1, 3)) for s in order],
        *rows,
        tags,
    )
    swapped = along(more[3], 0, False)
    far_given = [along(a, s, False) for s, a in zip(order, more[:3])]
    given = [along(a, s, False) for s, a in zip(order, more[11:])]
    near = [(more[4], 0), (swapped, 0)]
    had = line_sums(near + [(kept[0], 1)], capacity, fine_dev, sent)
    had = line_sums([(a, 1) for a in kept[1:]], capacity, fine_dev, sent, (*had, 1))
    kept_own = [along(a, s, True) for s, a in zip(order, more[5:8])]
    given_own = [along(a, s, False) for s, a in zip(order, more[8:11])]
    got = {}
    for cross in order:
        source = [(a, 2) for a in far_given] if cross == 2 else [(a, (cross + 1) // 2) for a in given]
        part = line_sums(source, capacity, fine_dev, (cross,), (*had, 1), send=True)
        got[cross] = lax.ppermute(part, "rows", cross_pairs(cross))
    acc, counts = line_sums(near + [(a, 0) for a in kept_own + given_own], capacity, fine_dev, own)
    hot, digits = tag_hot(
        [more[4], swapped] + kept_own + given_own, capacity, capacity_two, coarse_dev
    )
    new_fine, near_fine, *keep = update(
        acc,
        counts,
        old_fine,
        [got[c] for c in steps],
        [(True, s) for s in order],
        owner_hot,
        rank_hot,
    )
    arrived = []
    for s, a in zip(order, keep):
        arrived.append(along(a, s, True))
    give = place([(False, s) for s in order], owner_hot, rank_hot, near_fine)
    for s, a in zip(order, give):
        arrived.append(along(a, s, False))
    here = place([(False, 0), (True, 0)], owner_hot, rank_hot, near_fine)
    arrived = [here[1], along(here[0], 0, False)] + arrived
    *sent_sums, acc = coarse_sums(arrived, hot, digits, order + own)
    got = []
    for cross, part in zip(order, sent_sums):
        got.append(lax.ppermute(part, "rows", cross_pairs(cross)))
    means = coarse(acc, digits, old_coarse, got)
    pieces = [means]
    for step in range(1, groups):
        back = [((g + step) % groups, g) for g in range(groups)]
        pieces.append(lax.ppermute(means, "grp", back))
    at = lax.axis_index("grp").astype(jnp.int32).reshape(1)
    return (new_fine, finish(at, pieces))


def solution(mesh):
    in_specs = (
        P("rows", "grp"),
        P("rows"),
        P("rows", None),
        P("rows", "grp"),
        P("rows"),
        P("rows", "grp"),
    )
    out_specs = (P("rows", "grp"), P("rows", None))
    return jax.shard_map(
        level_step, mesh=mesh, in_specs=in_specs, out_specs=out_specs, check_vma=False
    )
```

```python
import functools

import jax
import jax.numpy as jnp
from jax import lax
from jax.experimental import pallas as pl
from jax.experimental.pallas import tpu as pltpu
from jax.sharding import PartitionSpec as P


F32 = jnp.float32
BF16 = jnp.bfloat16
LANES = 128
MIB = 1024 * 1024
TAIL = 8
SIDE = 4


def iota(shape, axis):
    return lax.broadcasted_iota(jnp.int32, shape, axis)


def device(x, y, core):
    return (x % SIDE) * 2 * SIDE + (y % SIDE) * 2 + core


CHIPS = [(x, y) for x in range(SIDE) for y in range(SIDE)]


def line_pairs(step, same_class):
    pairs = []
    for x, y in CHIPS:
        for core in range(2):
            kind = core if same_class else 1 - core
            to = device(x + step, y, 0) if kind == 0 else device(x, y + step, 1)
            pairs.append((device(x, y, core), to))
    return pairs


def cross_pairs(step):
    pairs = []
    for x, y in CHIPS:
        pairs.append((device(x, y, 0), device(x, y + step, 0)))
        pairs.append((device(x, y, 1), device(x + step, y, 1)))
    return pairs


def owner_of(kind, step, cross):
    here = lax.axis_index("rows")
    along = lax.rem(here // (2 * SIDE) + jnp.where(kind == 0, step, cross), SIDE)
    over = lax.rem(lax.rem(here // 2, SIDE) + jnp.where(kind == 0, cross, step), SIDE)
    return along * 2 * SIDE + over * 2 + kind


def pack_body(slots, capacity, tagged, counts, emb, local, *rest):
    tags = rest[0] if tagged else None
    rest = rest[1:] if tagged else rest
    outs, (windows, labels, starts, done, arrived) = rest[: len(slots)], rest[len(slots) :]
    per_dev, width = emb.shape
    span = capacity + 16
    label_rows = local.shape[0]
    owners = counts.shape[1]
    at_step = pl.program_id(0)
    core = lax.rem(lax.axis_index("rows"), 2)

    def fetch(at, cross, base):
        low = jnp.minimum(base, per_dev - span)
        return pltpu.make_async_copy(
            emb.at[pl.ds(pl.multiple_of(low, 16), span), :],
            windows.at[at, cross, :span, :],
            done.at[at, cross],
        )

    @pl.when(at_step == 0)
    def _():
        fetch_labels = pltpu.make_async_copy(local, labels.at[:label_rows, :], arrived)
        fetch_labels.start()

        def add(o, total):
            starts[o] = total
            return total + counts[0, o]

        lax.fori_loop(0, owners, add, 0)
        for cross in range(max(len(c) for _, _, c in slots)):
            for at, (same_class, step, crosses) in enumerate(slots):
                if cross < len(crosses):
                    kind = core if same_class else 1 - core
                    first = starts[owner_of(kind, step, crosses[cross])]
                    fetch(at, cross, first // 16 * 16).start()
        labels[label_rows:, :] = jnp.zeros((16, LANES), jnp.int32)
        for at, (_, _, crosses) in enumerate(slots):
            for cross in range(len(crosses)):
                windows[at, cross, span:, :] = jnp.zeros((80, width), BF16)
        fetch_labels.wait()

    line = iota((TAIL, LANES), 0) * LANES + iota((TAIL, LANES), 1)
    lane = iota((TAIL, LANES), 1)
    for at_slot, ((same_class, step, crosses), out) in enumerate(zip(slots, outs)):

        @pl.when(at_step < len(crosses))
        def _():
            stride = crosses[1] - crosses[0] if len(crosses) > 1 else 1
            cross = at_step * stride + crosses[0]
            kind = core if same_class else 1 - core
            owner = owner_of(kind, step, cross)
            first = starts[owner]
            count = counts[0, owner]
            base16 = first // 16 * 16
            turn = first - base16
            far = turn >= 8
            small = jnp.where(far, turn - 8, turn)
            turn_back = lax.rem(8 - small, 8)
            kept = iota((9, 8, width), 1) < 8 - small
            behind = base16 - jnp.minimum(base16, per_dev - span)
            fetch(at_slot, at_step, base16).wait()
            for at in range(0, capacity, 64):
                top = pl.multiple_of(jnp.minimum(behind + at, span), 16)
                window = windows[at_slot, at_step, pl.ds(top, 80), :]
                window = window.astype(F32).reshape(10, 8, width)
                window = pltpu.roll(window, turn_back, 1)
                moved = jnp.where(kept, window[:9], window[1:])
                moved = jnp.where(far, moved[1:], moved[:8])
                out[0, at : at + 64, :] = moved.reshape(64, width).astype(BF16)
            base = first // LANES
            shift = first - base * LANES
            got = [labels[pl.ds(base + i, 1), :] for i in range(TAIL + 1)]
            low_part = jnp.concatenate(got[:TAIL], axis=0)
            high_part = jnp.concatenate(got[1:], axis=0)
            back = lax.rem(LANES - shift, LANES)
            low_part = pltpu.roll(low_part, back, 1)
            high_part = pltpu.roll(high_part, back, 1)
            value = jnp.where(lane < LANES - shift, low_part, high_part)
            live = line < count
            high = jnp.where(live, lax.shift_right_logical(value, 7), 64).astype(F32)
            low = jnp.where(live, value & 127, 0).astype(F32)
            if crosses[0] == 0:
                own_tags = [tags[pl.ds(owner_of(kind, step, c), 1), :] for c in range(SIDE)]
                high = jnp.concatenate([high[: TAIL - SIDE]] + own_tags, axis=0)
            out[0, capacity:, :] = jnp.concatenate([high, low], axis=1).astype(BF16)


def pack(slots, send_counts, embeddings, local, capacity, tags=None, limit=None):
    _, width = embeddings.shape
    tall = capacity + TAIL
    longest = max(len(c) for _, _, c in slots)

    def spec(length):
        return pl.BlockSpec((1, tall, width), lambda q: (jnp.minimum(q, length - 1), 0, 0))

    many = sum(len(c) for _, _, c in slots)
    held = len(slots) * longest * (capacity + 96) * width * 2 + len(slots) * 2 * tall * width * 2
    return pl.pallas_call(
        functools.partial(pack_body, slots, capacity, tags is not None),
        grid=(longest,),
        out_shape=[jax.ShapeDtypeStruct((len(c), tall, width), BF16) for _, _, c in slots],
        in_specs=[
            pl.BlockSpec(memory_space=pltpu.SMEM),
            pl.BlockSpec(memory_space=pltpu.HBM),
            pl.BlockSpec(memory_space=pltpu.HBM),
        ]
        + ([] if tags is None else [pl.BlockSpec(tags.shape, lambda q: (0, 0))]),
        out_specs=[spec(len(c)) for _, _, c in slots],
        scratch_shapes=[
            pltpu.VMEM((len(slots), longest, capacity + 96, width), BF16),
            pltpu.VMEM((local.shape[0] + 16, LANES), jnp.int32),
            pltpu.SMEM((send_counts.shape[1],), jnp.int32),
            pltpu.SemaphoreType.DMA((len(slots), longest)),
            pltpu.SemaphoreType.DMA,
        ],
        compiler_params=pltpu.CompilerParams(vmem_limit_bytes=limit or held + 6 * MIB),
        cost_estimate=pl.CostEstimate(
            flops=0,
            bytes_accessed=2 * many * tall * width * 2,
            transcendentals=0,
        ),
        name="pack_rows",
    )(send_counts, embeddings, local, *([] if tags is None else [tags]))


def sums_body(lowest, capacity, crosses, had_lowest, sent, *refs):
    sources = len(lowest)
    arrived, refs = refs[:sources], refs[sources:]
    had_acc, had_counts = None, None
    if had_lowest is not None:
        had_acc, had_counts, refs = refs[0], refs[1], refs[2:]
    if sent:
        out, low_hot, high_hot, onehot, data = refs
        out_counts = None
    else:
        out, out_counts, low_hot, high_hot, onehot, data = refs
    digits = high_hot.shape[0]
    depth = sources * capacity
    size = onehot.shape[0]
    group = size // LANES
    fine_dev = digits * LANES
    stride = crosses[1] - crosses[0] if len(crosses) > 1 else 1

    def one(i):
        cross = crosses[0] + i * stride
        for s in range(sources):
            slot = arrived[s].at[cross - lowest[s]]
            tail = slot[capacity:, :].astype(F32)
            data[s * capacity : (s + 1) * capacity, :] = slot[:capacity, :]
            for part in range(capacity // LANES):
                at = s * capacity + part * LANES
                high = tail[part : part + 1, :LANES]
                low = tail[part : part + 1, LANES : 2 * LANES]
                low_hot[:, at : at + LANES] = jnp.where(
                    iota((LANES, LANES), 0).astype(F32) == low, 1.0, 0.0
                ).astype(BF16)
                high_hot[:, at : at + LANES] = jnp.where(
                    iota((digits, LANES), 0).astype(F32) == high, 1.0, 0.0
                )
        counts = lax.dot_general(
            high_hot[...].astype(BF16),
            low_hot[...],
            (((1,), (1,)), ((), ())),
            preferred_element_type=F32,
        )
        if had_counts is not None:
            counts = counts + had_counts[cross - had_lowest]
        if sent:
            tens = jnp.floor(counts / 64.0)
            out[fine_dev:, :] = jnp.concatenate([tens, counts - 64.0 * tens], axis=1).astype(BF16)
        else:
            out_counts[i] = counts
        for part in range(digits // group):
            for h in range(group):
                at_high = part * group + h
                row = jnp.broadcast_to(high_hot[at_high : at_high + 1, :], (16, depth)).astype(BF16)
                for at in range(0, LANES, 16):
                    top = h * LANES + at
                    onehot[top : top + 16, :] = low_hot[at : at + 16, :] * row
            total = jnp.dot(onehot[...], data[...], preferred_element_type=F32)
            rows = slice(part * size, (part + 1) * size)
            if had_acc is not None:
                total = total + had_acc[cross - had_lowest, rows, :]
            if sent:
                out[rows, :] = total.astype(BF16)
            else:
                out[i, rows, :] = total

    if len(crosses) == 1:
        one(0)
    else:
        pl.loop(0, len(crosses))(one)


def line_sums(arrived, capacity, fine_dev, crosses, had=None, send=False):
    width = arrived[0][0].shape[2]
    tall = capacity + TAIL
    sources = len(arrived)
    digits = fine_dev // LANES
    size = fine_dev // 4
    many = len(crosses)
    operands = [a for a, _ in arrived]
    had_lowest = None
    if had is not None:
        acc, counts, had_lowest = had
        operands += [acc, counts]
    if send:
        out_shape = jax.ShapeDtypeStruct((fine_dev + 16, width), BF16)
    else:
        out_shape = (
            jax.ShapeDtypeStruct((many, fine_dev, width), F32),
            jax.ShapeDtypeStruct((many, digits, LANES), F32),
        )
    body = functools.partial(
        sums_body, tuple(low for _, low in arrived), capacity, crosses, had_lowest, send
    )
    return pl.pallas_call(
        body,
        out_shape=out_shape,
        scratch_shapes=[
            pltpu.VMEM((LANES, sources * capacity), BF16),
            pltpu.VMEM((digits, sources * capacity), F32),
            pltpu.VMEM((size, sources * capacity), BF16),
            pltpu.VMEM((sources * capacity, width), BF16),
        ],
        compiler_params=pltpu.CompilerParams(vmem_limit_bytes=(8 + 2 * sources) * MIB),
        cost_estimate=pl.CostEstimate(
            flops=2 * many * sources * capacity * fine_dev * width,
            bytes_accessed=many * (sources * tall * width * 2 + fine_dev * width * 8),
            transcendentals=0,
        ),
        name="line_sums",
    )(*operands)


def update_body(slots, acc, counts, old, owner_hot, rank_hot, *refs):
    steps = SIDE - 1
    got, refs = refs[:steps], refs[steps:]
    new, whole, outs, placement = refs[0], refs[1], refs[2:-1], refs[-1]
    fine_dev = old.shape[0]
    count = counts[0]
    for g in got:
        value = g[fine_dev:, :].astype(F32)
        count = count + value[:, :LANES] * 64.0 + value[:, LANES : 2 * LANES]
    tens = jnp.floor(count / 64.0)
    eye = jnp.where(iota((LANES, LANES), 0) == iota((LANES, LANES), 1), 1.0, 0.0)
    turn = lambda a: lax.dot_general(
        eye.astype(BF16), a.astype(BF16), (((1,), (1,)), ((), ())), preferred_element_type=F32
    )
    column = turn(tens) * 64.0 + turn(count - 64.0 * tens)
    for h in range(fine_dev // LANES):
        at = slice(h * LANES, (h + 1) * LANES)
        total = acc[0, at, :] + old[at, :].astype(F32)
        for g in got:
            total = total + g[at, :].astype(F32)
        fresh = (total / (column[:, h : h + 1] + 1.0)).astype(BF16)
        new[at, :] = fresh
        whole[at, :] = fresh
    place_body(slots, owner_hot, rank_hot, whole, *outs, placement)


def update(acc, counts, old_fine, got, slots, owner_hot, rank_hot):
    fine_dev, width = old_fine.shape
    capacity = rank_hot.shape[0]
    return pl.pallas_call(
        functools.partial(update_body, slots),
        out_shape=[jax.ShapeDtypeStruct((fine_dev, width), BF16)] * 2
        + [jax.ShapeDtypeStruct((SIDE, capacity, width), BF16)] * len(slots),
        scratch_shapes=[pltpu.VMEM((SIDE * capacity, fine_dev), BF16)],
        compiler_params=pltpu.CompilerParams(vmem_limit_bytes=24 * MIB),
        name="new_fine",
    )(acc, counts, old_fine, owner_hot, rank_hot, *got)


def plan_body(coarse_dev, ids, owner_hot, rank_hot, labels):
    peers, fine_dev = owner_hot.shape
    value = ids[...]
    owner = value // coarse_dev
    local = (value - owner * coarse_dev).astype(F32)
    member = jnp.where(iota((peers, fine_dev), 0) == owner, 1.0, 0.0)
    owner_hot[...] = member
    step = 256
    before = jnp.where(iota((step, step), 0) < iota((step, step), 1), 1.0, 0.0).astype(BF16)
    carry = jnp.zeros((peers, 1), F32)
    for at in range(0, fine_dev, step):
        piece = member[:, at : at + step]
        prefix = jnp.dot(piece.astype(BF16), before, preferred_element_type=F32) + carry
        rank = jnp.sum(prefix * piece, axis=0, keepdims=True)
        carry = carry + jnp.sum(piece, axis=1, keepdims=True)
        hot = jnp.where(iota((rank_hot.shape[0], step), 0).astype(F32) == rank, 1.0, 0.0)
        rank_hot[:, at : at + step] = hot.astype(BF16)
    tagged = (member * (local + 1.0)).astype(BF16)
    labels[...] = lax.dot_general(
        tagged, rank_hot[...], (((1,), (1,)), ((), ())), preferred_element_type=F32
    )


def plan(coarse_ids, peers, capacity, coarse_dev):
    fine_dev = coarse_ids.shape[1]
    return pl.pallas_call(
        functools.partial(plan_body, coarse_dev),
        out_shape=(
            jax.ShapeDtypeStruct((peers, fine_dev), F32),
            jax.ShapeDtypeStruct((capacity, fine_dev), BF16),
            jax.ShapeDtypeStruct((peers, capacity), F32),
        ),
        compiler_params=pltpu.CompilerParams(vmem_limit_bytes=24 * MIB),
        name="plan_clusters",
    )(coarse_ids)


def place_body(slots, owner_hot, rank_hot, new, *refs):
    outs, placement = refs[:-1], refs[-1]
    capacity, fine_dev = rank_hot.shape
    core = lax.rem(lax.axis_index("rows"), 2)
    for (same_class, step), out in zip(slots, outs):
        kind = core if same_class else 1 - core
        for cross in range(SIDE):
            row = owner_hot[pl.ds(owner_of(kind, step, cross), 1), :]
            row = jnp.broadcast_to(row, (16, fine_dev)).astype(BF16)
            for at in range(0, capacity, 16):
                top = cross * capacity + at
                placement[top : top + 16, :] = rank_hot[at : at + 16, :] * row
        sent = jnp.dot(placement[...], new[...], preferred_element_type=F32).astype(BF16)
        for cross in range(SIDE):
            out[cross, :, :] = sent[cross * capacity : (cross + 1) * capacity, :]


def place(slots, owner_hot, rank_hot, new_fine):
    capacity, fine_dev = rank_hot.shape
    width = new_fine.shape[1]
    return pl.pallas_call(
        functools.partial(place_body, slots),
        out_shape=[jax.ShapeDtypeStruct((SIDE, capacity, width), BF16)] * len(slots),
        scratch_shapes=[pltpu.VMEM((SIDE * capacity, fine_dev), BF16)],
        compiler_params=pltpu.CompilerParams(vmem_limit_bytes=24 * MIB),
        cost_estimate=pl.CostEstimate(
            flops=2 * len(slots) * SIDE * capacity * fine_dev * width,
            bytes_accessed=fine_dev * width * 2,
            transcendentals=0,
        ),
        name="place_clusters",
    )(owner_hot, rank_hot, new_fine)


def tag_hot_body(sources, *refs):
    tails, hot, digits = refs[:sources], refs[-2], refs[-1]
    many, coarse_dev, depth = hot.shape
    capacity = depth // sources
    row = iota((coarse_dev, capacity), 0).astype(F32) + 1.0
    for cross in range(many):
        for s in range(sources):
            at = TAIL - SIDE + cross
            tag = tails[s][0].astype(F32)[at : at + 1, :capacity]
            one = jnp.where(row == tag, 1.0, 0.0).astype(BF16)
            hot[cross, :, s * capacity : (s + 1) * capacity] = one
        count = lax.dot_general(
            jnp.ones((8, depth), BF16),
            hot[cross],
            (((1,), (1,)), ((), ())),
            preferred_element_type=F32,
        )
        tens = jnp.floor(count / 64.0)
        digits[cross] = jnp.concatenate([tens, count - 64.0 * tens], axis=0).astype(BF16)


def tag_hot(tagged, capacity, capacity_two, coarse_dev):
    width = tagged[0].shape[2]
    sources = len(tagged)
    return pl.pallas_call(
        functools.partial(tag_hot_body, sources),
        grid=(1,),
        out_shape=(
            jax.ShapeDtypeStruct((SIDE, coarse_dev, sources * capacity_two), BF16),
            jax.ShapeDtypeStruct((SIDE, 16, coarse_dev), BF16),
        ),
        in_specs=[pl.BlockSpec((1, TAIL, width), lambda i: (0, capacity // TAIL, 0))] * sources,
        out_specs=(
            pl.BlockSpec((SIDE, coarse_dev, sources * capacity_two), lambda i: (0, 0, 0)),
            pl.BlockSpec((SIDE, 16, coarse_dev), lambda i: (0, 0, 0)),
        ),
        compiler_params=pltpu.CompilerParams(vmem_limit_bytes=12 * MIB),
        name="tag_hot",
    )(*tagged)


def coarse_sums_body(sources, order, *refs):
    arrived, (hot, digits), outs, data = (
        refs[:sources],
        refs[sources : sources + 2],
        refs[sources + 2 : -1],
        refs[-1],
    )
    capacity = arrived[0].shape[1]
    coarse_dev = hot.shape[1]
    for cross, out in zip(order, outs):
        for s in range(sources):
            data[s * capacity : (s + 1) * capacity, :] = arrived[s][cross]
        total = jnp.dot(hot[cross], data[...], preferred_element_type=F32)
        if cross == 0:
            out[...] = total
        else:
            out[:coarse_dev, :] = total.astype(BF16)
            out[coarse_dev:, :] = digits[cross]


def coarse_sums(arrived, hot, digits, order):
    capacity, width = arrived[0].shape[1:]
    sources = len(arrived)
    coarse_dev = hot.shape[1]
    sent = jax.ShapeDtypeStruct((coarse_dev + 16, width), BF16)
    kept = jax.ShapeDtypeStruct((coarse_dev, width), F32)
    return pl.pallas_call(
        functools.partial(coarse_sums_body, sources, order),
        out_shape=[kept if c == 0 else sent for c in order],
        scratch_shapes=[pltpu.VMEM((sources * capacity, width), BF16)],
        compiler_params=pltpu.CompilerParams(vmem_limit_bytes=16 * MIB),
        name="coarse_sums",
    )(*arrived, hot, digits)


def coarse_body(acc, digits, old, *refs):
    got, means = refs[:-1], refs[-1]
    coarse_dev, _ = acc.shape
    total = acc[...] + old[...].astype(F32)
    tens = digits[0, :8, :].astype(F32)
    ones = digits[0, 8:, :].astype(F32)
    for g in got:
        total = total + g[:coarse_dev, :].astype(F32)
        tens = tens + g[coarse_dev : coarse_dev + 8, :].astype(F32)
        ones = ones + g[coarse_dev + 8 :, :].astype(F32)
    eye = jnp.where(
        iota((coarse_dev, coarse_dev), 0) == iota((coarse_dev, coarse_dev), 1), 1.0, 0.0
    ).astype(BF16)
    turn = lambda a: lax.dot_general(
        eye, a.astype(BF16), (((1,), (1,)), ((), ())), preferred_element_type=F32
    )
    count = turn(tens) * 64.0 + turn(ones)
    means[...] = (total / (count[:, :1] + 1.0)).astype(BF16)


def coarse(acc, digits, old_coarse, got):
    return pl.pallas_call(
        coarse_body,
        out_shape=jax.ShapeDtypeStruct(old_coarse.shape, BF16),
        compiler_params=pltpu.CompilerParams(vmem_limit_bytes=8 * MIB),
        name="coarse_means",
    )(acc, digits, old_coarse, *got)


def finish_body(groups, at, *refs):
    pieces, out, full = refs[:groups], refs[groups], refs[groups + 1]
    width = pieces[0].shape[1]
    for step in range(groups):
        place = lax.rem(at[0] + step, groups) * width
        full[:, pl.ds(pl.multiple_of(place, width), width)] = pieces[step][...].astype(F32)
    whole = full[...]
    scale = lax.rsqrt(jnp.mean(whole * whole, axis=1, keepdims=True) + 1e-06)
    out[...] = (whole * scale).astype(BF16)


def finish(at, pieces):
    groups = len(pieces)
    rows, width = pieces[0].shape
    return pl.pallas_call(
        functools.partial(finish_body, groups),
        out_shape=jax.ShapeDtypeStruct((rows, groups * width), BF16),
        in_specs=[pl.BlockSpec(memory_space=pltpu.SMEM)]
        + [pl.BlockSpec(memory_space=pltpu.VMEM)] * groups,
        scratch_shapes=[pltpu.VMEM((rows, groups * width), F32)],
        compiler_params=pltpu.CompilerParams(vmem_limit_bytes=24 * MIB),
        name="coarse_dirs",
    )(at, *pieces)


def level_step(embeddings, fine_local, send_counts, old_fine, coarse_ids, old_coarse):
    peers = lax.axis_size("rows")
    groups = lax.axis_size("grp")
    per_dev = embeddings.shape[0]
    fine_dev = old_fine.shape[0]
    coarse_dev = old_coarse.shape[0]
    capacity = 2 * per_dev // peers
    capacity_two = 2 * fine_dev // peers
    local = fine_local.reshape(-1, LANES)
    steps = range(1, SIDE)

    def along(slots, step, same_class):
        return lax.ppermute(slots, "rows", line_pairs(step, same_class))

    rows = (send_counts, embeddings, local, capacity)
    sent, own = tuple(steps), (0,)
    order = (2, 1, 3)

    kept = []
    for part, group in (("far", order[:1]), ("near", order[1:])):
        limit = 61 * MIB if part == "far" else None
        keep = pack([(True, s, sent) for s in group], *rows, limit=limit)
        for s, a in zip(group, keep):
            kept.append(along(a, s, True))
    owner_hot, rank_hot, tags = plan(
        coarse_ids.reshape(1, -1), peers, capacity_two, coarse_dev
    )
    more = pack(
        [(False, s, (2,)) for s in order]
        + [(False, 0, own + sent), (True, 0, own + sent)]
        + [(k, s, own) for k in (True, False) for s in order]
        + [(False, s, (1, 3)) for s in order],
        *rows,
        tags,
    )
    swapped = along(more[3], 0, False)
    far_given = [along(a, s, False) for s, a in zip(order, more[:3])]
    given = [along(a, s, False) for s, a in zip(order, more[11:])]
    near = [(more[4], 0), (swapped, 0)]
    had = line_sums(near + [(kept[0], 1)], capacity, fine_dev, sent)
    kept_own = [along(a, s, True) for s, a in zip(order, more[5:8])]
    given_own = [along(a, s, False) for s, a in zip(order, more[8:11])]
    close = [(a, 1) for a in kept[1:]]
    got = {}
    for cross in order:
        source = [(a, (cross + 1) // 2) for a in given]
        before = (*had, (cross + 1) // 2)
        if cross == 2:
            source, before = close + [(a, 2) for a in far_given], (*had, 1)
        part = line_sums(source, capacity, fine_dev, (cross,), before, send=True)
        got[cross] = lax.ppermute(part, "rows", cross_pairs(cross))
        if cross == 2:
            had = line_sums(close, capacity, fine_dev, (1, 3), (*had, 1))
    acc, counts = line_sums(near + [(a, 0) for a in kept_own + given_own], capacity, fine_dev, own)
    hot, digits = tag_hot(
        [more[4], swapped] + kept_own + given_own, capacity, capacity_two, coarse_dev
    )
    new_fine, near_fine, *keep = update(
        acc,
        counts,
        old_fine,
        [got[c] for c in steps],
        [(True, s) for s in order],
        owner_hot,
        rank_hot,
    )
    arrived = []
    for s, a in zip(order, keep):
        arrived.append(along(a, s, True))
    give = place([(False, s) for s in order], owner_hot, rank_hot, near_fine)
    for s, a in zip(order, give):
        arrived.append(along(a, s, False))
    here = place([(False, 0), (True, 0)], owner_hot, rank_hot, near_fine)
    arrived = [here[1], along(here[0], 0, False)] + arrived
    *sent_sums, acc = coarse_sums(arrived, hot, digits, order + own)
    got = []
    for cross, part in zip(order, sent_sums):
        got.append(lax.ppermute(part, "rows", cross_pairs(cross)))
    means = coarse(acc, digits, old_coarse, got)
    pieces = [means]
    for step in range(1, groups):
        back = [((g + step) % groups, g) for g in range(groups)]
        pieces.append(lax.ppermute(means, "grp", back))
    at = lax.axis_index("grp").astype(jnp.int32).reshape(1)
    return (new_fine, finish(at, pieces))


def solution(mesh):
    in_specs = (
        P("rows", "grp"),
        P("rows"),
        P("rows", None),
        P("rows", "grp"),
        P("rows"),
        P("rows", "grp"),
    )
    out_specs = (P("rows", "grp"), P("rows", None))
    return jax.shard_map(
        level_step, mesh=mesh, in_specs=in_specs, out_specs=out_specs, check_vma=False
    )
```
